32 devices in a mesh: outer: 4 (over x, core), inner: 8 (over z, y).
Axes of the slice: x: 2, y: 2, z: 4, core: 2. Of those that a mesh axis runs over, the one named last changes fastest.
Arguments:
- query_tiles: bfloat16 [4096, 768], P(('outer', 'inner')), may hold values from -7 to 7
- key_tiles: bfloat16 [4096, 768], P(('outer', 'inner')), may hold values from -6 to 6
- value_tiles: bfloat16 [4096, 768], P(('outer', 'inner')), may hold values from -6 to 6
- cotangent: bfloat16 [4096, 768], P(('outer', 'inner')), may hold values from -6 to 6
- row_lengths: int32 [128], P(('outer', 'inner')), may hold values from 1 to 32
Outputs:
- attended: bfloat16 [4096, 768], P(('outer', 'inner'))
- query_grad: bfloat16 [4096, 768], P(('outer', 'inner'))
- key_grad: bfloat16 [4096, 768], P(('outer', 'inner'))
- value_grad: bfloat16 [4096, 768], P(('outer', 'inner'))
The draws below stay inside these ranges and needn't reach their ends.
All inputs are finite; a program needn't handle non-finite values.
Results may differ from the reference program's by a relative error of at most 0.0203.
Values may be sent and summed in bfloat16 or wider, within the bound.
A program may use at most 128 MiB of HBM per device.

```python
import jax
import jax.numpy as jnp
import numpy as np
from jax import lax

HEADS = 16
HEAD = 48
D = 768
TOK_DEV = 128
ROW = 32
STRIDE_GROUP = 4
STRIDE_SLIDE = 16
TOKENS = 4096
ROWS = 128
GROUP = 1024


def base_field(key, salt_value):
    field_key = jax.random.fold_in(key, salt_value)
    return jnp.clip(1.4 * jax.random.normal(field_key, (TOKENS, HEADS, HEAD), jnp.float32), -6.0, 6.0)


def draw_query_tiles(key, part):
    field_values = base_field(key, 11)
    return field_values.reshape(TOKENS, HEADS * HEAD).astype(jnp.bfloat16)


def draw_key_tiles(key, part):
    field_values = base_field(key, 23)
    return field_values.reshape(TOKENS, HEADS * HEAD).astype(jnp.bfloat16)


def place_ends(values, rng, smallest, high):
    place = [jax.random.randint(jax.random.fold_in(rng, axis), (), 0, length) for axis, length in enumerate(values.shape)]
    widest = values.shape.index(max(values.shape))
    neighbour = place[:widest] + [(place[widest] + 1) % values.shape[widest]] + place[widest + 1:]
    return values.at[tuple(place)].set(smallest).at[tuple(neighbour)].set(high)


def steps_of(key, shape, cuts, smallest, high):
    loudness, own = 1.0, jax.random.fold_in(key, 6)
    for dim, parts in cuts:
        draws = jnp.exp(jax.random.uniform(jax.random.fold_in(own, dim), (parts,), jnp.float32, smallest / len(cuts), high / len(cuts)))
        loudness = loudness * jnp.repeat(draws, shape[dim] // parts).reshape([-1 if axis == dim else 1 for axis in range(len(shape))])
    return loudness


def normal_values(own_key, dims, deviation, bound, split=(), kind=jnp.bfloat16):
    entries = deviation * jax.random.normal(own_key, dims, jnp.float32)
    if split:
        entries = entries * steps_of(own_key, dims, split, -0.22, 0.18)
    return jnp.clip(entries, -bound, bound).astype(kind)


def setup_inputs(seed: int = 0) -> dict:
    seeds = jax.random.split(jax.random.key(seed), 6)
    query_tiles = draw_query_tiles(jax.random.fold_in(seeds[5], 71), 0)
    key_tiles = draw_key_tiles(jax.random.fold_in(seeds[5], 71), 0)
    value_tiles = normal_values(seeds[2], (TOKENS, D), 1.0, 6.0, ((0, 32),))
    cotangent = normal_values(seeds[3], (TOKENS, D), 1.0, 6.0, ((0, 32),))
    row_lengths = place_ends(jax.random.randint(seeds[4], (ROWS,), 1, ROW + 1), jax.random.fold_in(seeds[4], 1), 1, ROW).astype(jnp.int32)
    return dict(query_tiles=query_tiles, key_tiles=key_tiles, value_tiles=value_tiles, cotangent=cotangent, row_lengths=row_lengths)


NEGATIVE_FILL = -1.0e30


def settle(values_in):
    return lax.optimization_barrier(values_in.astype(jnp.bfloat16)).astype(jnp.float32)


def scores_of(query_heads, key_heads, score_scale):
    return jnp.einsum("qhd,khd->hqk", query_heads.astype(jnp.float32), key_heads.astype(jnp.float32)) * score_scale


def branch_stats(query_heads, key_heads, value_heads, key_valid, score_scale):
    raw_scores = scores_of(query_heads, key_heads, score_scale)
    key_keep = jnp.transpose(key_valid)[:, None, :]
    masked = jnp.where(key_keep, raw_scores, NEGATIVE_FILL)
    row_peak = jnp.max(masked, axis=2)
    weights = jnp.where(key_keep, jnp.exp(masked - row_peak[:, :, None]), 0.0)
    row_total = jnp.sum(weights, axis=2)
    weighted = jnp.einsum("hqk,khd->qhd", settle(weights), value_heads.astype(jnp.float32))
    return jnp.transpose(row_peak), jnp.transpose(row_total), weighted


def branch_grads(query_heads, key_heads, value_heads, cotan_heads, log_norm, out_dot, key_valid, score_scale):
    raw_scores = scores_of(query_heads, key_heads, score_scale)
    key_keep = jnp.transpose(key_valid)[:, None, :]
    weights = jnp.where(key_keep, jnp.exp(raw_scores - jnp.transpose(log_norm)[:, :, None]), 0.0)
    weight_grads = jnp.einsum("qhd,khd->hqk", cotan_heads.astype(jnp.float32), value_heads.astype(jnp.float32))
    score_grads = weights * (weight_grads - jnp.transpose(out_dot)[:, :, None])
    low_weights = settle(weights)
    low_grads = settle(score_grads)
    query_part = score_scale * jnp.einsum("hqk,khd->qhd", low_grads, key_heads.astype(jnp.float32))
    key_part = score_scale * jnp.einsum("hqk,qhd->khd", low_grads, query_heads.astype(jnp.float32))
    value_part = jnp.einsum("hqk,qhd->khd", low_weights, cotan_heads.astype(jnp.float32))
    return query_part, key_part, value_part


def head_offsets(head_total, stride):
    return (np.arange(head_total) * stride) // head_total


def select_rows(array_in, stride):
    head_total = array_in.shape[1]
    folded = array_in.reshape((array_in.shape[0] // stride, stride) + array_in.shape[1:])
    return folded[:, head_offsets(head_total, stride), np.arange(head_total)]


def spread_rows(array_in, stride, fill_value):
    head_total = array_in.shape[1]
    chosen = np.arange(stride)[:, None] == head_offsets(head_total, stride)[None, :]
    chosen = chosen.reshape((1, stride, head_total) + (1,) * (array_in.ndim - 2))
    full = jnp.where(chosen, array_in[:, None], fill_value)
    return full.reshape((array_in.shape[0] * stride,) + array_in.shape[1:])


def add_picked(full, addend, stride):
    head_total = full.shape[1]
    folded = full.reshape((full.shape[0] // stride, stride) + full.shape[1:])
    folded = folded.at[:, head_offsets(head_total, stride), np.arange(head_total)].add(addend)
    return folded.reshape(full.shape)


def by_heads(array_in):
    return jnp.moveaxis(array_in, 1, 0)[:, :, None]


def from_heads(array_in):
    return jnp.moveaxis(array_in[:, :, 0], 0, 1)


def reference(query_tiles, key_tiles, value_tiles, cotangent, row_lengths):
    tile_count = query_tiles.shape[0]
    score_scale = HEAD ** -0.5
    head_shape = (tile_count, HEADS, HEAD)
    query_heads = query_tiles.reshape(head_shape)
    key_heads = key_tiles.reshape(head_shape)
    value_heads = value_tiles.reshape(head_shape)
    cotan_heads = cotangent.reshape(head_shape)
    tile_slot = jnp.arange(tile_count, dtype=jnp.int32)
    tile_valid = (tile_slot % ROW) < jnp.repeat(row_lengths, ROW, total_repeat_length=tile_count)
    valid_heads = jnp.broadcast_to(tile_valid[:, None], (tile_count, HEADS))
    block_count = tile_count // TOK_DEV
    group_count = tile_count // GROUP

    def by_blocks(array_in):
        return array_in.reshape((block_count, TOK_DEV) + array_in.shape[1:])

    def by_groups(array_in):
        picked = select_rows(array_in, STRIDE_GROUP)
        return picked.reshape((group_count, picked.shape[0] // group_count) + picked.shape[1:])

    def by_slide(array_in):
        return by_heads(select_rows(array_in, STRIDE_SLIDE))

    def stats_of(members):
        return branch_stats(members[0], members[1], members[2], members[3], score_scale)

    def grads_of(members):
        return branch_grads(members[0], members[1], members[2], members[3], members[4], members[5], members[6], score_scale)

    near_peak, near_total, near_sum = lax.map(stats_of, (by_blocks(query_heads), by_blocks(key_heads), by_blocks(value_heads), by_blocks(valid_heads)))
    near_peak = near_peak.reshape(tile_count, HEADS)
    near_total = near_total.reshape(tile_count, HEADS)
    near_sum = near_sum.reshape(head_shape)
    group_peak, group_total, group_sum = lax.map(stats_of, (by_groups(query_heads), by_groups(key_heads), by_groups(value_heads), by_groups(valid_heads)))
    group_peak = group_peak.reshape(-1, HEADS)
    group_total = group_total.reshape(-1, HEADS)
    group_sum = group_sum.reshape(-1, HEADS, HEAD)
    slide_peak, slide_total, slide_sum = lax.map(stats_of, (by_slide(query_heads), by_slide(key_heads), by_slide(value_heads), by_slide(valid_heads)))
    slide_peak = from_heads(slide_peak)
    slide_total = from_heads(slide_total)
    slide_sum = from_heads(slide_sum)
    group_peak_full = spread_rows(group_peak, STRIDE_GROUP, NEGATIVE_FILL)
    slide_peak_full = spread_rows(slide_peak, STRIDE_SLIDE, NEGATIVE_FILL)
    best_peak = jnp.maximum(jnp.maximum(near_peak, group_peak_full), slide_peak_full)
    near_weight = jnp.exp(near_peak - best_peak)
    group_weight = jnp.exp(group_peak_full - best_peak)
    slide_weight = jnp.exp(slide_peak_full - best_peak)
    denominator = near_total * near_weight + spread_rows(group_total, STRIDE_GROUP, 0.0) * group_weight + spread_rows(slide_total, STRIDE_SLIDE, 0.0) * slide_weight
    numerator = near_sum * near_weight[:, :, None]
    numerator = add_picked(numerator, group_sum * select_rows(group_weight, STRIDE_GROUP)[:, :, None], STRIDE_GROUP)
    numerator = add_picked(numerator, slide_sum * select_rows(slide_weight, STRIDE_SLIDE)[:, :, None], STRIDE_SLIDE)
    attended = (numerator / denominator[:, :, None]).astype(jnp.bfloat16)
    log_norm = best_peak + jnp.log(denominator)
    out_dot = jnp.sum(cotan_heads.astype(jnp.float32) * lax.optimization_barrier(attended).astype(jnp.float32), axis=2)

    near_grads = lax.map(grads_of, (by_blocks(query_heads), by_blocks(key_heads), by_blocks(value_heads), by_blocks(cotan_heads), by_blocks(log_norm), by_blocks(out_dot), by_blocks(valid_heads)))
    query_grad = near_grads[0].reshape(head_shape)
    key_grad = near_grads[1].reshape(head_shape)
    value_grad = near_grads[2].reshape(head_shape)
    group_grads = lax.map(grads_of, (by_groups(query_heads), by_groups(key_heads), by_groups(value_heads), by_groups(cotan_heads), by_groups(log_norm), by_groups(out_dot), by_groups(valid_heads)))
    query_grad = add_picked(query_grad, group_grads[0].reshape(-1, HEADS, HEAD), STRIDE_GROUP)
    key_grad = add_picked(key_grad, group_grads[1].reshape(-1, HEADS, HEAD), STRIDE_GROUP)
    value_grad = add_picked(value_grad, group_grads[2].reshape(-1, HEADS, HEAD), STRIDE_GROUP)
    slide_grads = lax.map(grads_of, (by_slide(query_heads), by_slide(key_heads), by_slide(value_heads), by_slide(cotan_heads), by_slide(log_norm), by_slide(out_dot), by_slide(valid_heads)))
    query_grad = add_picked(query_grad, from_heads(slide_grads[0]), STRIDE_SLIDE)
    key_grad = add_picked(key_grad, from_heads(slide_grads[1]), STRIDE_SLIDE)
    value_grad = add_picked(value_grad, from_heads(slide_grads[2]), STRIDE_SLIDE)
    flat_shape = (tile_count, HEADS * HEAD)
    return (attended.reshape(flat_shape), query_grad.astype(jnp.bfloat16).reshape(flat_shape), key_grad.astype(jnp.bfloat16).reshape(flat_shape), value_grad.astype(jnp.bfloat16).reshape(flat_shape))
```

```python
import jax
import jax.numpy as jnp
import numpy as np
from jax import lax
from jax.experimental import pallas as pl
from jax.experimental.pallas import tpu as pltpu
from jax.sharding import PartitionSpec as P

HEADS = 16
HEAD = 48
ROW = 32
STRIDE_GROUP = 4
STRIDE_SLIDE = 16


NEGATIVE_FILL = -1e30
heads_at_once = 4


def as_sent(value):

    def short(part):
        return part.astype(jnp.bfloat16) if part.dtype == jnp.float32 else part

    return jax.tree.map(short, value)


def head_ranges(head_total):
    step_size = min(head_total, heads_at_once)
    return [(first_head, first_head + step_size) for first_head in range(0, head_total, step_size)]


def scores_of(query_block, key_block, score_scale):
    return (
        jnp.einsum("hdq,hdk->hqk", query_block, key_block, preferred_element_type=jnp.float32)
        * score_scale
    )


def branch_stats(query_heads, key_heads, value_heads, key_valid, score_scale):
    peak_list, total_list, sum_list = ([], [], [])
    for first_head, last_head in head_ranges(query_heads.shape[0]):
        raw_scores = scores_of(
            query_heads[first_head:last_head], key_heads[first_head:last_head], score_scale
        )
        key_keep = key_valid[first_head:last_head][:, None, :]
        masked = jnp.where(key_keep, raw_scores, NEGATIVE_FILL)
        row_peak = jnp.max(masked, axis=2)
        weights = jnp.where(key_keep, jnp.exp(masked - row_peak[:, :, None]), 0.0)
        peak_list.append(row_peak)
        total_list.append(jnp.sum(weights, axis=2))
        sum_list.append(
            jnp.einsum(
                "hqk,hdk->hdq",
                weights.astype(jnp.bfloat16),
                value_heads[first_head:last_head],
                preferred_element_type=jnp.float32,
            )
        )
    return (
        jnp.concatenate(peak_list, axis=0),
        jnp.concatenate(total_list, axis=0),
        jnp.concatenate(sum_list, axis=0),
    )


def branch_grads(
    query_heads,
    key_heads,
    value_heads,
    cotan_heads,
    log_norm,
    out_dot,
    key_valid,
    score_scale,
    want_query,
    want_keys,
):
    query_list, key_list, value_list = ([], [], [])
    for first_head, last_head in head_ranges(query_heads.shape[0]):
        query_block = query_heads[first_head:last_head]
        key_block = key_heads[first_head:last_head]
        cotan_block = cotan_heads[first_head:last_head]
        raw_scores = scores_of(query_block, key_block, score_scale)
        key_keep = key_valid[first_head:last_head][:, None, :]
        weights = jnp.where(
            key_keep, jnp.exp(raw_scores - log_norm[first_head:last_head][:, :, None]), 0.0
        )
        weight_grads = jnp.einsum(
            "hdq,hdk->hqk",
            cotan_block,
            value_heads[first_head:last_head],
            preferred_element_type=jnp.float32,
        )
        low_grads = (weights * (weight_grads - out_dot[first_head:last_head][:, :, None])).astype(
            jnp.bfloat16
        )
        if want_query:
            query_list.append(
                score_scale
                * jnp.einsum(
                    "hqk,hdk->hdq", low_grads, key_block, preferred_element_type=jnp.float32
                )
            )
        if want_keys:
            key_list.append(
                score_scale
                * jnp.einsum(
                    "hqk,hdq->hdk", low_grads, query_block, preferred_element_type=jnp.float32
                )
            )
            value_list.append(
                jnp.einsum(
                    "hqk,hdq->hdk",
                    weights.astype(jnp.bfloat16),
                    cotan_block,
                    preferred_element_type=jnp.float32,
                )
            )
    query_part = jnp.concatenate(query_list, axis=0) if want_query else None
    key_part = jnp.concatenate(key_list, axis=0) if want_keys else None
    value_part = jnp.concatenate(value_list, axis=0) if want_keys else None
    return (query_part, key_part, value_part)


def head_offsets(head_total, stride):
    return np.arange(head_total) * stride // head_total


def select_rows(array_in, stride):
    head_total = array_in.shape[0]
    offsets = head_offsets(head_total, stride)
    folded = array_in.reshape(array_in.shape[:-1] + (array_in.shape[-1] // stride, stride))
    return jnp.stack(
        [folded[head_index, ..., int(offsets[head_index])] for head_index in range(head_total)]
    )


def spread_rows(array_in, stride, fill_value):
    head_total = array_in.shape[0]
    chosen = np.arange(stride)[None, :] == head_offsets(head_total, stride)[:, None]
    chosen = chosen.reshape((head_total,) + (1,) * (array_in.ndim - 1) + (stride,))
    full = jnp.where(chosen, array_in[..., None], fill_value)
    return full.reshape(array_in.shape[:-1] + (array_in.shape[-1] * stride,))


def to_heads(flat_in):
    return jnp.transpose(flat_in.reshape(flat_in.shape[0], HEADS, -1), (1, 2, 0))


def to_flat(heads_in):
    return jnp.transpose(heads_in, (2, 0, 1)).reshape(heads_in.shape[2], -1)


def local(query_tiles, key_tiles, value_tiles, cotangent, row_lengths):
    tile_count = query_tiles.shape[0]
    score_scale = HEAD ** (-0.5)
    query_heads = to_heads(query_tiles)
    key_heads = to_heads(key_tiles)
    value_heads = to_heads(value_tiles)
    cotan_heads = to_heads(cotangent)
    tile_slot = jnp.arange(tile_count, dtype=jnp.int32)
    tile_valid = tile_slot % ROW < jnp.repeat(row_lengths, ROW, total_repeat_length=tile_count)
    valid_heads = jnp.broadcast_to(tile_valid[None, :], (HEADS, tile_count))
    group_query = select_rows(query_heads, STRIDE_GROUP)
    group_key = select_rows(key_heads, STRIDE_GROUP)
    group_value = select_rows(value_heads, STRIDE_GROUP)
    group_cotan = select_rows(cotan_heads, STRIDE_GROUP)
    group_valid = select_rows(valid_heads, STRIDE_GROUP)
    group_flag = group_valid.astype(jnp.bfloat16)[:, None, :]
    slide_query = select_rows(query_heads, STRIDE_SLIDE)
    slide_key = select_rows(key_heads, STRIDE_SLIDE)
    slide_value = select_rows(value_heads, STRIDE_SLIDE)
    slide_flag = select_rows(valid_heads, STRIDE_SLIDE).astype(jnp.bfloat16)[:, None, :]
    owned_query, owned_key, owned_value, owned_flag = (
        lax.all_to_all(slide_query, "outer", split_axis=0, concat_axis=2, tiled=True),
        lax.all_to_all(slide_key, "outer", split_axis=0, concat_axis=2, tiled=True),
        lax.all_to_all(slide_value, "outer", split_axis=0, concat_axis=2, tiled=True),
        lax.all_to_all(slide_flag, "outer", split_axis=0, concat_axis=2, tiled=True),
    )
    got_group = (
        lax.all_gather(group_key, "inner", axis=2, tiled=True),
        lax.all_gather(group_value, "inner", axis=2, tiled=True),
        lax.all_gather(group_flag, "inner", axis=2, tiled=True),
    )
    got_slide = (
        lax.all_gather(owned_key, "inner", axis=2, tiled=True),
        lax.all_gather(owned_value, "inner", axis=2, tiled=True),
        lax.all_gather(owned_flag, "inner", axis=2, tiled=True),
    )
    near_peak, near_total, near_sum = branch_stats(
        query_heads, key_heads, value_heads, valid_heads, score_scale
    )
    remote_group_key = got_group[0]
    remote_group_value = got_group[1]
    remote_group_valid = got_group[2][:, 0, :] > 0.5
    group_peak, group_total, group_sum = branch_stats(
        group_query, remote_group_key, remote_group_value, remote_group_valid, score_scale
    )
    slide_all_key = got_slide[0]
    slide_all_value = got_slide[1]
    slide_all_valid = got_slide[2][:, 0, :] > 0.5
    owner_peak, owner_total, owner_sum = branch_stats(
        owned_query, slide_all_key, slide_all_value, slide_all_valid, score_scale
    )
    slide_peak, slide_total, slide_sum = (
        lax.all_to_all(owner_peak[:, None, :], "outer", split_axis=2, concat_axis=0, tiled=True),
        lax.all_to_all(owner_total[:, None, :], "outer", split_axis=2, concat_axis=0, tiled=True),
        lax.all_to_all(owner_sum, "outer", split_axis=2, concat_axis=0, tiled=True),
    )
    slide_peak = slide_peak[:, 0, :]
    slide_total = slide_total[:, 0, :]
    group_peak_full = spread_rows(group_peak, STRIDE_GROUP, NEGATIVE_FILL)
    slide_peak_full = spread_rows(slide_peak, STRIDE_SLIDE, NEGATIVE_FILL)
    best_peak = jnp.maximum(jnp.maximum(near_peak, group_peak_full), slide_peak_full)
    near_weight = jnp.exp(near_peak - best_peak)
    group_weight = jnp.exp(group_peak_full - best_peak)
    slide_weight = jnp.exp(slide_peak_full - best_peak)
    denominator = (
        near_total * near_weight
        + spread_rows(group_total, STRIDE_GROUP, 0.0) * group_weight
        + spread_rows(slide_total, STRIDE_SLIDE, 0.0) * slide_weight
    )
    numerator = (
        near_sum * near_weight[:, None, :]
        + spread_rows(group_sum, STRIDE_GROUP, 0.0) * group_weight[:, None, :]
        + spread_rows(slide_sum, STRIDE_SLIDE, 0.0) * slide_weight[:, None, :]
    )
    attended = (numerator / denominator[:, None, :]).astype(jnp.bfloat16)
    log_norm = best_peak + jnp.log(denominator)
    out_dot = jnp.sum(cotan_heads.astype(jnp.float32) * attended.astype(jnp.float32), axis=1)
    near_query, near_key, near_value = branch_grads(
        query_heads,
        key_heads,
        value_heads,
        cotan_heads,
        log_norm,
        out_dot,
        valid_heads,
        score_scale,
        True,
        True,
    )
    group_lse = select_rows(log_norm, STRIDE_GROUP)
    group_dot = select_rows(out_dot, STRIDE_GROUP)
    group_query_grad = branch_grads(
        group_query,
        remote_group_key,
        remote_group_value,
        group_cotan,
        group_lse,
        group_dot,
        remote_group_valid,
        score_scale,
        True,
        False,
    )[0]
    got_group_rows = (
        lax.all_gather(group_query, "inner", axis=2, tiled=True),
        lax.all_gather(group_cotan, "inner", axis=2, tiled=True),
    )
    got_group_stats = (
        lax.all_gather(group_lse, "inner", axis=1, tiled=True),
        lax.all_gather(group_dot, "inner", axis=1, tiled=True),
    )
    unused_group, group_key_grad, group_value_grad = branch_grads(
        got_group_rows[0],
        group_key,
        group_value,
        got_group_rows[1],
        got_group_stats[0],
        got_group_stats[1],
        group_valid,
        score_scale,
        False,
        True,
    )
    slide_cotan = select_rows(cotan_heads, STRIDE_SLIDE)
    slide_lse = select_rows(log_norm, STRIDE_SLIDE)
    slide_dot = select_rows(out_dot, STRIDE_SLIDE)
    owned_cotan = lax.all_to_all(slide_cotan, "outer", split_axis=0, concat_axis=2, tiled=True)
    owned_lse, owned_dot = (
        lax.all_to_all(slide_lse, "outer", split_axis=0, concat_axis=1, tiled=True),
        lax.all_to_all(slide_dot, "outer", split_axis=0, concat_axis=1, tiled=True),
    )
    owned_query_grad, partial_key, partial_value = branch_grads(
        owned_query,
        slide_all_key,
        slide_all_value,
        owned_cotan,
        owned_lse,
        owned_dot,
        slide_all_valid,
        score_scale,
        True,
        True,
    )
    owned_key_grad, owned_value_grad = (
        lax.psum_scatter(
            partial_key.astype(jnp.bfloat16), "inner", scatter_dimension=2, tiled=True
        ).astype(jnp.float32),
        lax.psum_scatter(
            partial_value.astype(jnp.bfloat16), "inner", scatter_dimension=2, tiled=True
        ).astype(jnp.float32),
    )
    slide_query_grad, slide_key_grad, slide_value_grad = (
        lax.all_to_all(
            as_sent(owned_query_grad), "outer", split_axis=2, concat_axis=0, tiled=True
        ).astype(owned_query_grad.dtype),
        lax.all_to_all(
            owned_key_grad.astype(jnp.bfloat16), "outer", split_axis=2, concat_axis=0, tiled=True
        ).astype(owned_key_grad.dtype),
        lax.all_to_all(
            owned_value_grad.astype(jnp.bfloat16), "outer", split_axis=2, concat_axis=0, tiled=True
        ).astype(owned_value_grad.dtype),
    )
    query_grad = (
        near_query
        + spread_rows(group_query_grad, STRIDE_GROUP, 0.0)
        + spread_rows(slide_query_grad, STRIDE_SLIDE, 0.0)
    )
    key_grad = (
        near_key
        + spread_rows(group_key_grad, STRIDE_GROUP, 0.0)
        + spread_rows(slide_key_grad, STRIDE_SLIDE, 0.0)
    )
    value_grad = (
        near_value
        + spread_rows(group_value_grad, STRIDE_GROUP, 0.0)
        + spread_rows(slide_value_grad, STRIDE_SLIDE, 0.0)
    )
    return (
        to_flat(attended),
        to_flat(query_grad.astype(jnp.bfloat16)),
        to_flat(key_grad.astype(jnp.bfloat16)),
        to_flat(value_grad.astype(jnp.bfloat16)),
    )


BF = jnp.bfloat16
F32 = jnp.float32
LANES = 128
SCALE = HEAD ** (-0.5)
PAIR = 2 * HEAD


def window(first_col, width):
    start = first_col // LANES * LANES
    shift = first_col - start
    return start, (LANES if shift + width <= LANES else 2 * LANES), shift


def iota2(shape, axis):
    return lax.broadcasted_iota(jnp.int32, shape, axis)


def original_tile(j):
    return (j & 7) * 16 + ((j >> 3) & 3) * 4 + (j >> 5)


def permute_matrix(inverse):
    shape = (LANES, LANES)
    j, i = (iota2(shape, 1), iota2(shape, 0)) if inverse else (iota2(shape, 0), iota2(shape, 1))
    return (original_tile(j) == i).astype(F32).astype(BF)


def key_bias(len_ref, axis):
    tile = original_tile(iota2((LANES, LANES), axis))
    row = tile >> 5
    length = jnp.full((LANES, LANES), len_ref[0], jnp.int32)
    for index in range(1, 4):
        length = jnp.where(row == index, len_ref[index], length)
    return jnp.where((tile & 31) < length, 0.0, NEGATIVE_FILL).astype(F32)


def shift_in(width, shift, kept):
    row, col = iota2((width, LANES), 0), iota2((width, LANES), 1)
    return ((row - shift == col) & (col < kept)).astype(F32).astype(BF)


def shift_out(width, shift, kept):
    row, col = iota2((LANES, width), 0), iota2((LANES, width), 1)
    return ((col - shift == row) & (row < kept)).astype(F32).astype(BF)


def lane_mask(width, first, last, extra=-1):
    lane = iota2((1, width), 1)
    keep = (lane >= first) & (lane < last)
    if extra >= 0:
        keep = keep | (lane == extra)
    return keep.astype(F32).astype(BF)


def mm(a, b):
    return jnp.dot(a, b, preferred_element_type=F32)


def mm_t(a, b):
    return lax.dot_general(a, b, (((1,), (1,)), ((), ())), preferred_element_type=F32)


def t_mm(a, b):
    return lax.dot_general(a, b, (((0,), (0,)), ((), ())), preferred_element_type=F32)


def slide_row(r):
    return (r % 4) * 32 + (r // 4) * 8


def split_mm(a, onehot):
    high = a.astype(BF)
    low = (a - high.astype(F32)).astype(BF)
    return mm(high, onehot) + mm(low, onehot)


def prep_kernel(copies, len_ref, q_ref, k_ref, v_ref, c_ref, xp_ref, gs_ref, ss_ref):
    perm = permute_matrix(False)
    xs = []
    for index, ref in enumerate((q_ref, k_ref, v_ref, c_ref)):
        xs.append(mm(perm, ref[...]))
        xp_ref[index] = xs[-1].astype(BF)
    bias = key_bias(len_ref, 0)
    for p in range(HEADS // 2):
        row = p // 2 * 32
        start, width, shift = window(PAIR * p, PAIR)
        stacked = jnp.concatenate(
            [x[row : row + 32, start : start + width].astype(BF) for x in xs], axis=0
        )
        moved = mm(stacked, shift_in(width, shift, PAIR))
        flag = iota2((32, LANES), 1) == PAIR
        gs_ref[p, 0] = jnp.where(flag, 1.0, moved[0:32]).astype(BF)
        gs_ref[p, 1] = jnp.where(flag, bias[row : row + 32], moved[32:64]).astype(BF)
        gs_ref[p, 2] = moved[64:96].astype(BF)
        gs_ref[p, 3] = moved[96:128].astype(BF)
    for r in range(HEADS):
        row = slide_row(r)
        start, width, shift = window(HEAD * r, HEAD)
        stacked = jnp.concatenate(
            [x[row : row + 8, start : start + width] for x in xs], axis=0
        ).astype(BF)
        moved = mm(stacked, shift_in(width, shift, HEAD))
        flag = iota2((8, LANES), 1) == HEAD
        block = jnp.concatenate(
            [
                jnp.where(flag, 1.0, moved[0:8]),
                jnp.where(flag, bias[row : row + 8], moved[8:16]),
                moved[16:32],
            ],
            axis=0,
        ).astype(BF)
        for copy in range(copies):
            ss_ref[copy * HEADS + r] = block


def near_fwd_kernel(len_ref, xp_ref, o_ref, lse_ref):
    bias = key_bias(len_ref, 1)
    lane = iota2((LANES, LANES), 1)
    lse = jnp.full((LANES, LANES), NEGATIVE_FILL, F32)
    total = [None] * (HEADS * HEAD // LANES)
    for h in range(HEADS):
        start, width, shift = window(HEAD * h, HEAD)
        mask = lane_mask(width, shift, shift + HEAD)
        s = mm_t(xp_ref[0, :, start : start + width] * mask, xp_ref[1, :, start : start + width])
        s = s * SCALE + bias
        peak = jnp.max(s, axis=1, keepdims=True)
        e = jnp.exp(s - peak)
        norm = jnp.sum(e, axis=1, keepdims=True)
        o = mm(e.astype(BF), xp_ref[2, :, start : start + width] * mask) / norm
        lse = jnp.where(lane == h, peak + jnp.log(norm), lse)
        for part in range(width // LANES):
            t = start // LANES + part
            piece = o[:, part * LANES : (part + 1) * LANES]
            total[t] = piece if total[t] is None else total[t] + piece
    for t, value in enumerate(total):
        o_ref[:, t * LANES : (t + 1) * LANES] = value
    lse_ref[...] = lse


def owner_fwd(q, k, v, heads):
    rows = q.shape[0]
    lane = iota2((rows, LANES), 1)
    lse = jnp.full((rows, LANES), NEGATIVE_FILL, F32)
    out = jnp.zeros((rows, LANES), F32)
    for e in range(heads):
        mask = lane_mask(LANES, HEAD * e, HEAD * (e + 1), HEAD * heads)
        s = mm_t(q * mask, k) * SCALE
        peak = jnp.max(s, axis=1, keepdims=True)
        weights = jnp.exp(s - peak)
        norm = jnp.sum(weights, axis=1, keepdims=True)
        part = mm(weights.astype(BF), v * lane_mask(LANES, HEAD * e, HEAD * (e + 1)))
        out = out + part / norm
        lse = jnp.where(lane == e, peak + jnp.log(norm), lse)
    return out, lse


def slide_members(ss_ref, sources):
    wide = ss_ref[...].astype(F32)
    return [
        wide[:, 8 * a : 8 * a + 8].reshape(sources * 8, LANES).astype(BF) for a in range(4)
    ]


def owner_fwd_kernel(gr_ref, sr_ref, go_ref, so_ref):
    groups, sources = gr_ref.shape[0], sr_ref.shape[0]
    q, k, v = [gr_ref[:, a].reshape(groups * 32, LANES) for a in range(3)]
    out, lse = owner_fwd(q, k, v, 2)
    go_ref[:, 0] = out.reshape(groups, 32, LANES)
    go_ref[:, 1] = lse.reshape(groups, 32, LANES)
    q, k, v, _ = slide_members(sr_ref, sources)
    out, lse = owner_fwd(q, k, v, 1)
    so_ref[:, 0] = out.reshape(sources, 8, LANES)
    so_ref[:, 1] = lse.reshape(sources, 8, LANES)


def head_spread(transposed):
    shape = (HEADS * HEAD, LANES) if transposed else (LANES, HEADS * HEAD)
    head, col = (iota2(shape, 1), iota2(shape, 0)) if transposed else (iota2(shape, 0), iota2(shape, 1))
    return ((col >= head * HEAD) & (col < head * HEAD + HEAD)).astype(F32).astype(BF)


def combine_kernel(
    copies, xp_ref, on_ref, ln_ref, go_ref, so_ref, att_ref, plane_t_ref, g2_ref, s2_ref, acc_ref
):
    lane32 = iota2((32, LANES), 1)
    lane8 = iota2((8, LANES), 1)
    near = ln_ref[...]
    group_rows, slide_rows = [], [None] * HEADS
    for o in range(4):
        pieces = []
        for p in (2 * o, 2 * o + 1):
            moved = pltpu.roll(go_ref[p, 1], 2 * p, 1) if p else go_ref[p, 1]
            keep = (lane32 >= 2 * p) & (lane32 < 2 * p + 2)
            pieces.append(jnp.where(keep, moved, NEGATIVE_FILL))
        group_rows.append(jnp.maximum(pieces[0], pieces[1]))
    for r in range(HEADS):
        moved = pltpu.roll(so_ref[r, 1], r, 1) if r else so_ref[r, 1]
        slide_rows[slide_row(r) // 8] = jnp.where(lane8 == r, moved, NEGATIVE_FILL)
    group = jnp.concatenate(group_rows, axis=0)
    slide = jnp.concatenate(slide_rows, axis=0)
    best = jnp.maximum(jnp.maximum(near, group), slide)
    near_w, group_w, slide_w = jnp.exp(near - best), jnp.exp(group - best), jnp.exp(slide - best)
    den = near_w + group_w + slide_w
    lse = best + jnp.log(den)
    spread = head_spread(False)
    acc_ref[...] = jnp.zeros_like(acc_ref)
    for p in range(HEADS // 2):
        row = p // 2 * 32
        start, width, shift = window(PAIR * p, PAIR)
        acc_ref[0, row : row + 32, start : start + width] += mm(
            go_ref[p, 0].astype(BF), shift_out(width, shift, PAIR)
        )
    for r in range(HEADS):
        row = slide_row(r)
        start, width, shift = window(HEAD * r, HEAD)
        acc_ref[1, row : row + 8, start : start + width] += mm(
            so_ref[r, 0].astype(BF), shift_out(width, shift, HEAD)
        )
    attended = (
        on_ref[...] * split_mm(near_w / den, spread)
        + acc_ref[0] * split_mm(group_w / den, spread)
        + acc_ref[1] * split_mm(slide_w / den, spread)
    ).astype(BF)
    att_ref[...] = mm(permute_matrix(True), attended).astype(BF)
    product = xp_ref[3].astype(F32) * attended.astype(F32)
    delta = split_mm(product, head_spread(True))
    lane = iota2((LANES, LANES), 1)
    plane = jnp.where(lane < HEADS, lse, pltpu.roll(delta, HEADS, 1))
    plane_t_ref[...] = plane.T
    for p in range(HEADS // 2):
        row = p // 2 * 32
        block = plane[row : row + 32]
        g2_ref[p] = pltpu.roll(block, LANES - 2 * p, 1) if p else block
    for r in range(HEADS):
        row = slide_row(r)
        block = plane[row : row + 8]
        block = pltpu.roll(block, LANES - r, 1) if r else block
        for copy in range(copies):
            s2_ref[copy * HEADS + r] = block


def near_bwd_kernel(len_ref, xp_ref, plane_t_ref, grads_ref):
    bias = key_bias(len_ref, 0)
    tiles = HEADS * HEAD // LANES
    totals = [[None] * tiles for _ in range(3)]
    for h in range(HEADS):
        start, width, shift = window(HEAD * h, HEAD)
        mask = lane_mask(width, shift, shift + HEAD)
        qm, km, vm, cm = [xp_ref[a, :, start : start + width] * mask for a in range(4)]
        s = mm_t(km, qm) * SCALE + bias
        weights = jnp.exp(s - plane_t_ref[h : h + 1, :])
        dp = mm_t(vm, cm)
        ds = (weights * (dp - plane_t_ref[HEADS + h : HEADS + h + 1, :])).astype(BF)
        results = (t_mm(ds, km), mm(ds, qm), mm(weights.astype(BF), cm))
        for index, value in enumerate(results):
            for part in range(width // LANES):
                t = start // LANES + part
                piece = value[:, part * LANES : (part + 1) * LANES]
                old = totals[index][t]
                totals[index][t] = piece if old is None else old + piece
    for index in range(3):
        for t in range(tiles):
            value = totals[index][t]
            grads_ref[index, :, t * LANES : (t + 1) * LANES] = value * SCALE if index < 2 else value


def owner_bwd(q, k, v, c, plane, heads):
    plane_t = plane.T
    sums = [None] * 3
    for e in range(heads):
        mask = lane_mask(LANES, HEAD * e, HEAD * (e + 1))
        q_flag = q * lane_mask(LANES, HEAD * e, HEAD * (e + 1), HEAD * heads)
        cm = c * mask
        s = mm_t(k, q_flag) * SCALE
        weights = jnp.exp(s - plane_t[e : e + 1, :])
        dp = mm_t(v, cm)
        ds = (weights * (dp - plane_t[HEADS + e : HEADS + e + 1, :])).astype(BF)
        parts = (t_mm(ds, k * mask), mm(ds, q * mask), mm(weights.astype(BF), cm))
        sums = [part if old is None else old + part for old, part in zip(sums, parts)]
    return sums[0] * SCALE, sums[1] * SCALE, sums[2]


def owner_bwd_kernel(gr_ref, sr_ref, gp_ref, sp_ref, go_ref, so_ref):
    groups, sources = gr_ref.shape[0], sr_ref.shape[0]
    members = [gr_ref[:, a].reshape(groups * 32, LANES) for a in range(4)]
    grads = owner_bwd(*members, gp_ref[...].reshape(groups * 32, LANES), 2)
    for a in range(3):
        go_ref[:, a] = grads[a].reshape(groups, 32, LANES).astype(BF)
    members = slide_members(sr_ref, sources)
    grads = owner_bwd(*members, sp_ref[...].reshape(sources * 8, LANES), 1)
    stacked = [grad.reshape(sources, 8, LANES) for grad in grads]
    stacked.append(jnp.zeros((sources, 8, LANES), F32))
    so_ref[...] = jnp.concatenate(stacked, axis=1).astype(BF)


def final_kernel(near_ref, go_ref, so_ref, dq_ref, dk_ref, dv_ref, acc_ref):
    acc_ref[...] = near_ref[...]
    for p in range(HEADS // 2):
        row = p // 2 * 32
        start, width, shift = window(PAIR * p, PAIR)
        moved = mm(go_ref[p].reshape(96, LANES), shift_out(width, shift, PAIR))
        for a in range(3):
            acc_ref[a, row : row + 32, start : start + width] += moved[32 * a : 32 * a + 32]
    for r in range(HEADS):
        row = slide_row(r)
        start, width, shift = window(HEAD * r, HEAD)
        moved = mm(so_ref[r], shift_out(width, shift, HEAD))
        for a in range(3):
            acc_ref[a, row : row + 8, start : start + width] += moved[8 * a : 8 * a + 8]
    back = permute_matrix(True)
    for a, ref in enumerate((dq_ref, dk_ref, dv_ref)):
        ref[...] = mm(back, acc_ref[a].astype(BF)).astype(BF)


def shaped(shape, dtype):
    return jax.ShapeDtypeStruct(shape, dtype)


def run(kernel, outs, args, scalars=0, scratch=(), flops=20_000_000):
    in_specs = [pl.BlockSpec(memory_space=pltpu.SMEM)] * scalars
    in_specs += [pl.BlockSpec(memory_space=pltpu.VMEM)] * (len(args) - scalars)
    out_specs = jax.tree.map(lambda _: pl.BlockSpec(memory_space=pltpu.VMEM), outs)
    return pl.pallas_call(
        kernel,
        out_shape=outs,
        in_specs=in_specs,
        out_specs=out_specs,
        scratch_shapes=list(scratch),
        cost_estimate=pl.CostEstimate(flops=flops, bytes_accessed=4_000_000, transcendentals=300_000),
        compiler_params=pltpu.CompilerParams(vmem_limit_bytes=48 * 1024 * 1024),
    )(*args)


def fast_local(inner, devices, query_tiles, key_tiles, value_tiles, cotangent, row_lengths):
    copies = devices // HEADS
    tiles, width = query_tiles.shape
    every = ("outer", "inner")

    def swap(array, axes):
        return lax.all_to_all(array, axes, split_axis=0, concat_axis=0, tiled=True)

    xp, group_send, slide_send = run(
        lambda *refs: prep_kernel(copies, *refs),
        (
            shaped((4, tiles, width), BF),
            shaped((inner, 4, 32, LANES), BF),
            shaped((devices, 32, LANES), BF),
        ),
        (row_lengths, query_tiles, key_tiles, value_tiles, cotangent),
        scalars=1,
    )
    group_got = swap(group_send, "inner")
    slide_got = swap(slide_send, every)
    near_out, near_lse = run(
        near_fwd_kernel,
        (shaped((tiles, width), F32), shaped((tiles, LANES), F32)),
        (row_lengths, xp),
        scalars=1,
    )
    group_out, slide_out = run(
        owner_fwd_kernel,
        (shaped((inner, 2, 32, LANES), F32), shaped((devices, 2, 8, LANES), F32)),
        (group_got, slide_got),
    )
    group_back = swap(group_out, "inner")
    slide_back = swap(slide_out, every)
    attended, plane_t, group_plane, slide_plane = run(
        lambda *refs: combine_kernel(copies, *refs),
        (
            shaped((tiles, width), BF),
            shaped((LANES, tiles), F32),
            shaped((inner, 32, LANES), F32),
            shaped((devices, 8, LANES), F32),
        ),
        (xp, near_out, near_lse, group_back, slide_back),
        scratch=(pltpu.VMEM((2, tiles, width), F32),),
    )
    group_plane = swap(group_plane, "inner")
    slide_plane = swap(slide_plane, every)
    near_grads = run(
        near_bwd_kernel, shaped((3, tiles, width), F32), (row_lengths, xp, plane_t), scalars=1
    )
    group_grads, slide_grads = run(
        owner_bwd_kernel,
        (shaped((inner, 3, 32, LANES), BF), shaped((devices, 32, LANES), BF)),
        (group_got, slide_got, group_plane, slide_plane),
    )
    group_grads = swap(group_grads, "inner")
    slide_grads = swap(slide_grads, every)
    grads = run(
        final_kernel,
        tuple(shaped((tiles, width), BF) for _ in range(3)),
        (near_grads, group_grads, slide_grads),
        scratch=(pltpu.VMEM((3, tiles, width), F32),),
    )
    return (attended,) + tuple(grads)


def solution(mesh):
    in_specs = (P(("outer", "inner"), None),) * 4 + (P(("outer", "inner")),)
    out_specs = (P(("outer", "inner"), None),) * 4
    inner = mesh.shape["inner"]
    devices = inner * mesh.shape["outer"]

    def step(*args):
        small = 2 * inner == HEADS and devices % HEADS == 0 and devices <= 64
        if small and args[0].shape == (LANES, HEADS * HEAD):
            return fast_local(inner, devices, *args)
        return local(*args)

    return jax.shard_map(step, mesh=mesh, in_specs=in_specs, out_specs=out_specs, check_vma=False)
```

```python
import jax
import jax.numpy as jnp
import numpy as np
from jax import lax
from jax.experimental import pallas as pl
from jax.experimental.pallas import tpu as pltpu
from jax.sharding import PartitionSpec as P

HEADS = 16
HEAD = 48
ROW = 32
STRIDE_GROUP = 4
STRIDE_SLIDE = 16


NEGATIVE_FILL = -1e30
heads_at_once = 4


def as_sent(value):

    def short(part):
        return part.astype(jnp.bfloat16) if part.dtype == jnp.float32 else part

    return jax.tree.map(short, value)


def head_ranges(head_total):
    step_size = min(head_total, heads_at_once)
    return [(first_head, first_head + step_size) for first_head in range(0, head_total, step_size)]


def scores_of(query_block, key_block, score_scale):
    return (
        jnp.einsum("hdq,hdk->hqk", query_block, key_block, preferred_element_type=jnp.float32)
        * score_scale
    )


def branch_stats(query_heads, key_heads, value_heads, key_valid, score_scale):
    peak_list, total_list, sum_list = ([], [], [])
    for first_head, last_head in head_ranges(query_heads.shape[0]):
        raw_scores = scores_of(
            query_heads[first_head:last_head], key_heads[first_head:last_head], score_scale
        )
        key_keep = key_valid[first_head:last_head][:, None, :]
        masked = jnp.where(key_keep, raw_scores, NEGATIVE_FILL)
        row_peak = jnp.max(masked, axis=2)
        weights = jnp.where(key_keep, jnp.exp(masked - row_peak[:, :, None]), 0.0)
        peak_list.append(row_peak)
        total_list.append(jnp.sum(weights, axis=2))
        sum_list.append(
            jnp.einsum(
                "hqk,hdk->hdq",
                weights.astype(jnp.bfloat16),
                value_heads[first_head:last_head],
                preferred_element_type=jnp.float32,
            )
        )
    return (
        jnp.concatenate(peak_list, axis=0),
        jnp.concatenate(total_list, axis=0),
        jnp.concatenate(sum_list, axis=0),
    )


def branch_grads(
    query_heads,
    key_heads,
    value_heads,
    cotan_heads,
    log_norm,
    out_dot,
    key_valid,
    score_scale,
    want_query,
    want_keys,
):
    query_list, key_list, value_list = ([], [], [])
    for first_head, last_head in head_ranges(query_heads.shape[0]):
        query_block = query_heads[first_head:last_head]
        key_block = key_heads[first_head:last_head]
        cotan_block = cotan_heads[first_head:last_head]
        raw_scores = scores_of(query_block, key_block, score_scale)
        key_keep = key_valid[first_head:last_head][:, None, :]
        weights = jnp.where(
            key_keep, jnp.exp(raw_scores - log_norm[first_head:last_head][:, :, None]), 0.0
        )
        weight_grads = jnp.einsum(
            "hdq,hdk->hqk",
            cotan_block,
            value_heads[first_head:last_head],
            preferred_element_type=jnp.float32,
        )
        low_grads = (weights * (weight_grads - out_dot[first_head:last_head][:, :, None])).astype(
            jnp.bfloat16
        )
        if want_query:
            query_list.append(
                score_scale
                * jnp.einsum(
                    "hqk,hdk->hdq", low_grads, key_block, preferred_element_type=jnp.float32
                )
            )
        if want_keys:
            key_list.append(
                score_scale
                * jnp.einsum(
                    "hqk,hdq->hdk", low_grads, query_block, preferred_element_type=jnp.float32
                )
            )
            value_list.append(
                jnp.einsum(
                    "hqk,hdq->hdk",
                    weights.astype(jnp.bfloat16),
                    cotan_block,
                    preferred_element_type=jnp.float32,
                )
            )
    query_part = jnp.concatenate(query_list, axis=0) if want_query else None
    key_part = jnp.concatenate(key_list, axis=0) if want_keys else None
    value_part = jnp.concatenate(value_list, axis=0) if want_keys else None
    return (query_part, key_part, value_part)


def head_offsets(head_total, stride):
    return np.arange(head_total) * stride // head_total


def select_rows(array_in, stride):
    head_total = array_in.shape[0]
    offsets = head_offsets(head_total, stride)
    folded = array_in.reshape(array_in.shape[:-1] + (array_in.shape[-1] // stride, stride))
    return jnp.stack(
        [folded[head_index, ..., int(offsets[head_index])] for head_index in range(head_total)]
    )


def spread_rows(array_in, stride, fill_value):
    head_total = array_in.shape[0]
    chosen = np.arange(stride)[None, :] == head_offsets(head_total, stride)[:, None]
    chosen = chosen.reshape((head_total,) + (1,) * (array_in.ndim - 1) + (stride,))
    full = jnp.where(chosen, array_in[..., None], fill_value)
    return full.reshape(array_in.shape[:-1] + (array_in.shape[-1] * stride,))


def to_heads(flat_in):
    return jnp.transpose(flat_in.reshape(flat_in.shape[0], HEADS, -1), (1, 2, 0))


def to_flat(heads_in):
    return jnp.transpose(heads_in, (2, 0, 1)).reshape(heads_in.shape[2], -1)


def local(query_tiles, key_tiles, value_tiles, cotangent, row_lengths):
    tile_count = query_tiles.shape[0]
    score_scale = HEAD ** (-0.5)
    query_heads = to_heads(query_tiles)
    key_heads = to_heads(key_tiles)
    value_heads = to_heads(value_tiles)
    cotan_heads = to_heads(cotangent)
    tile_slot = jnp.arange(tile_count, dtype=jnp.int32)
    tile_valid = tile_slot % ROW < jnp.repeat(row_lengths, ROW, total_repeat_length=tile_count)
    valid_heads = jnp.broadcast_to(tile_valid[None, :], (HEADS, tile_count))
    group_query = select_rows(query_heads, STRIDE_GROUP)
    group_key = select_rows(key_heads, STRIDE_GROUP)
    group_value = select_rows(value_heads, STRIDE_GROUP)
    group_cotan = select_rows(cotan_heads, STRIDE_GROUP)
    group_valid = select_rows(valid_heads, STRIDE_GROUP)
    group_flag = group_valid.astype(jnp.bfloat16)[:, None, :]
    slide_query = select_rows(query_heads, STRIDE_SLIDE)
    slide_key = select_rows(key_heads, STRIDE_SLIDE)
    slide_value = select_rows(value_heads, STRIDE_SLIDE)
    slide_flag = select_rows(valid_heads, STRIDE_SLIDE).astype(jnp.bfloat16)[:, None, :]
    owned_query, owned_key, owned_value, owned_flag = (
        lax.all_to_all(slide_query, "outer", split_axis=0, concat_axis=2, tiled=True),
        lax.all_to_all(slide_key, "outer", split_axis=0, concat_axis=2, tiled=True),
        lax.all_to_all(slide_value, "outer", split_axis=0, concat_axis=2, tiled=True),
        lax.all_to_all(slide_flag, "outer", split_axis=0, concat_axis=2, tiled=True),
    )
    got_group = (
        lax.all_gather(group_key, "inner", axis=2, tiled=True),
        lax.all_gather(group_value, "inner", axis=2, tiled=True),
        lax.all_gather(group_flag, "inner", axis=2, tiled=True),
    )
    got_slide = (
        lax.all_gather(owned_key, "inner", axis=2, tiled=True),
        lax.all_gather(owned_value, "inner", axis=2, tiled=True),
        lax.all_gather(owned_flag, "inner", axis=2, tiled=True),
    )
    near_peak, near_total, near_sum = branch_stats(
        query_heads, key_heads, value_heads, valid_heads, score_scale
    )
    remote_group_key = got_group[0]
    remote_group_value = got_group[1]
    remote_group_valid = got_group[2][:, 0, :] > 0.5
    group_peak, group_total, group_sum = branch_stats(
        group_query, remote_group_key, remote_group_value, remote_group_valid, score_scale
    )
    slide_all_key = got_slide[0]
    slide_all_value = got_slide[1]
    slide_all_valid = got_slide[2][:, 0, :] > 0.5
    owner_peak, owner_total, owner_sum = branch_stats(
        owned_query, slide_all_key, slide_all_value, slide_all_valid, score_scale
    )
    slide_peak, slide_total, slide_sum = (
        lax.all_to_all(owner_peak[:, None, :], "outer", split_axis=2, concat_axis=0, tiled=True),
        lax.all_to_all(owner_total[:, None, :], "outer", split_axis=2, concat_axis=0, tiled=True),
        lax.all_to_all(owner_sum, "outer", split_axis=2, concat_axis=0, tiled=True),
    )
    slide_peak = slide_peak[:, 0, :]
    slide_total = slide_total[:, 0, :]
    group_peak_full = spread_rows(group_peak, STRIDE_GROUP, NEGATIVE_FILL)
    slide_peak_full = spread_rows(slide_peak, STRIDE_SLIDE, NEGATIVE_FILL)
    best_peak = jnp.maximum(jnp.maximum(near_peak, group_peak_full), slide_peak_full)
    near_weight = jnp.exp(near_peak - best_peak)
    group_weight = jnp.exp(group_peak_full - best_peak)
    slide_weight = jnp.exp(slide_peak_full - best_peak)
    denominator = (
        near_total * near_weight
        + spread_rows(group_total, STRIDE_GROUP, 0.0) * group_weight
        + spread_rows(slide_total, STRIDE_SLIDE, 0.0) * slide_weight
    )
    numerator = (
        near_sum * near_weight[:, None, :]
        + spread_rows(group_sum, STRIDE_GROUP, 0.0) * group_weight[:, None, :]
        + spread_rows(slide_sum, STRIDE_SLIDE, 0.0) * slide_weight[:, None, :]
    )
    attended = (numerator / denominator[:, None, :]).astype(jnp.bfloat16)
    log_norm = best_peak + jnp.log(denominator)
    out_dot = jnp.sum(cotan_heads.astype(jnp.float32) * attended.astype(jnp.float32), axis=1)
    near_query, near_key, near_value = branch_grads(
        query_heads,
        key_heads,
        value_heads,
        cotan_heads,
        log_norm,
        out_dot,
        valid_heads,
        score_scale,
        True,
        True,
    )
    group_lse = select_rows(log_norm, STRIDE_GROUP)
    group_dot = select_rows(out_dot, STRIDE_GROUP)
    group_query_grad = branch_grads(
        group_query,
        remote_group_key,
        remote_group_value,
        group_cotan,
        group_lse,
        group_dot,
        remote_group_valid,
        score_scale,
        True,
        False,
    )[0]
    got_group_rows = (
        lax.all_gather(group_query, "inner", axis=2, tiled=True),
        lax.all_gather(group_cotan, "inner", axis=2, tiled=True),
    )
    got_group_stats = (
        lax.all_gather(group_lse, "inner", axis=1, tiled=True),
        lax.all_gather(group_dot, "inner", axis=1, tiled=True),
    )
    unused_group, group_key_grad, group_value_grad = branch_grads(
        got_group_rows[0],
        group_key,
        group_value,
        got_group_rows[1],
        got_group_stats[0],
        got_group_stats[1],
        group_valid,
        score_scale,
        False,
        True,
    )
    slide_cotan = select_rows(cotan_heads, STRIDE_SLIDE)
    slide_lse = select_rows(log_norm, STRIDE_SLIDE)
    slide_dot = select_rows(out_dot, STRIDE_SLIDE)
    owned_cotan = lax.all_to_all(slide_cotan, "outer", split_axis=0, concat_axis=2, tiled=True)
    owned_lse, owned_dot = (
        lax.all_to_all(slide_lse, "outer", split_axis=0, concat_axis=1, tiled=True),
        lax.all_to_all(slide_dot, "outer", split_axis=0, concat_axis=1, tiled=True),
    )
    owned_query_grad, partial_key, partial_value = branch_grads(
        owned_query,
        slide_all_key,
        slide_all_value,
        owned_cotan,
        owned_lse,
        owned_dot,
        slide_all_valid,
        score_scale,
        True,
        True,
    )
    owned_key_grad, owned_value_grad = (
        lax.psum_scatter(
            partial_key.astype(jnp.bfloat16), "inner", scatter_dimension=2, tiled=True
        ).astype(jnp.float32),
        lax.psum_scatter(
            partial_value.astype(jnp.bfloat16), "inner", scatter_dimension=2, tiled=True
        ).astype(jnp.float32),
    )
    slide_query_grad, slide_key_grad, slide_value_grad = (
        lax.all_to_all(
            as_sent(owned_query_grad), "outer", split_axis=2, concat_axis=0, tiled=True
        ).astype(owned_query_grad.dtype),
        lax.all_to_all(
            owned_key_grad.astype(jnp.bfloat16), "outer", split_axis=2, concat_axis=0, tiled=True
        ).astype(owned_key_grad.dtype),
        lax.all_to_all(
            owned_value_grad.astype(jnp.bfloat16), "outer", split_axis=2, concat_axis=0, tiled=True
        ).astype(owned_value_grad.dtype),
    )
    query_grad = (
        near_query
        + spread_rows(group_query_grad, STRIDE_GROUP, 0.0)
        + spread_rows(slide_query_grad, STRIDE_SLIDE, 0.0)
    )
    key_grad = (
        near_key
        + spread_rows(group_key_grad, STRIDE_GROUP, 0.0)
        + spread_rows(slide_key_grad, STRIDE_SLIDE, 0.0)
    )
    value_grad = (
        near_value
        + spread_rows(group_value_grad, STRIDE_GROUP, 0.0)
        + spread_rows(slide_value_grad, STRIDE_SLIDE, 0.0)
    )
    return (
        to_flat(attended),
        to_flat(query_grad.astype(jnp.bfloat16)),
        to_flat(key_grad.astype(jnp.bfloat16)),
        to_flat(value_grad.astype(jnp.bfloat16)),
    )


BF = jnp.bfloat16
F32 = jnp.float32
LANES = 128
SCALE = HEAD ** (-0.5)
PAIR = 2 * HEAD


def window(first_col, width):
    start = first_col // LANES * LANES
    shift = first_col - start
    return start, (LANES if shift + width <= LANES else 2 * LANES), shift


def iota2(shape, axis):
    return lax.broadcasted_iota(jnp.int32, shape, axis)


def original_tile(j):
    return (j & 7) * 16 + ((j >> 3) & 3) * 4 + (j >> 5)


def permute_matrix(inverse):
    shape = (LANES, LANES)
    j, i = (iota2(shape, 1), iota2(shape, 0)) if inverse else (iota2(shape, 0), iota2(shape, 1))
    return (original_tile(j) == i).astype(F32).astype(BF)


def key_bias(len_ref, axis):
    tile = original_tile(iota2((LANES, LANES), axis))
    row = tile >> 5
    length = jnp.full((LANES, LANES), len_ref[0], jnp.int32)
    for index in range(1, 4):
        length = jnp.where(row == index, len_ref[index], length)
    return jnp.where((tile & 31) < length, 0.0, NEGATIVE_FILL).astype(F32)


def shift_in(width, shift, kept):
    row, col = iota2((width, LANES), 0), iota2((width, LANES), 1)
    return ((row - shift == col) & (col < kept)).astype(F32).astype(BF)


def shift_out(width, shift, kept):
    row, col = iota2((LANES, width), 0), iota2((LANES, width), 1)
    return ((col - shift == row) & (row < kept)).astype(F32).astype(BF)


def lane_mask(width, first, last, extra=-1):
    lane = iota2((1, width), 1)
    keep = (lane >= first) & (lane < last)
    if extra >= 0:
        keep = keep | (lane == extra)
    return keep.astype(F32).astype(BF)


def mm(a, b):
    return jnp.dot(a, b, preferred_element_type=F32)


def mm_t(a, b):
    return lax.dot_general(a, b, (((1,), (1,)), ((), ())), preferred_element_type=F32)


def t_mm(a, b):
    return lax.dot_general(a, b, (((0,), (0,)), ((), ())), preferred_element_type=F32)


def slide_row(r):
    return (r % 4) * 32 + (r // 4) * 8


def split_mm(a, onehot):
    high = a.astype(BF)
    low = (a - high.astype(F32)).astype(BF)
    return mm(high, onehot) + mm(low, onehot)


def prep_kernel(len_ref, q_ref, k_ref, v_ref, c_ref, xp_ref, gs_ref, ss_ref):
    perm = permute_matrix(False)
    xs = []
    for index, ref in enumerate((q_ref, k_ref, v_ref, c_ref)):
        xs.append(mm(perm, ref[...]))
        xp_ref[index] = xs[-1].astype(BF)
    bias = key_bias(len_ref, 0)
    for p in range(HEADS // 2):
        row = p // 2 * 32
        start, width, shift = window(PAIR * p, PAIR)
        stacked = jnp.concatenate(
            [x[row : row + 32, start : start + width].astype(BF) for x in xs], axis=0
        )
        moved = mm(stacked, shift_in(width, shift, PAIR))
        flag = iota2((32, LANES), 1) == PAIR
        gs_ref[p, 0] = jnp.where(flag, 1.0, moved[0:32]).astype(BF)
        gs_ref[p, 1] = jnp.where(flag, bias[row : row + 32], moved[32:64]).astype(BF)
        gs_ref[p, 2] = moved[64:96].astype(BF)
        gs_ref[p, 3] = moved[96:128].astype(BF)
    for r in range(HEADS):
        row = slide_row(r)
        start, width, shift = window(HEAD * r, HEAD)
        stacked = jnp.concatenate(
            [x[row : row + 8, start : start + width] for x in xs], axis=0
        ).astype(BF)
        moved = mm(stacked, shift_in(width, shift, HEAD))
        flag = iota2((8, LANES), 1) == HEAD
        block = jnp.concatenate(
            [
                jnp.where(flag, 1.0, moved[0:8]),
                jnp.where(flag, bias[row : row + 8], moved[8:16]),
                moved[16:32],
            ],
            axis=0,
        ).astype(BF)
        ss_ref[r] = block


def near_fwd_kernel(len_ref, xp_ref, o_ref, lse_ref):
    bias = key_bias(len_ref, 1)
    lane = iota2((LANES, LANES), 1)
    lse = jnp.full((LANES, LANES), NEGATIVE_FILL, F32)
    total = [None] * (HEADS * HEAD // LANES)
    for h in range(HEADS):
        start, width, shift = window(HEAD * h, HEAD)
        mask = lane_mask(width, shift, shift + HEAD)
        s = mm_t(xp_ref[0, :, start : start + width] * mask, xp_ref[1, :, start : start + width])
        s = s * SCALE + bias
        peak = jnp.max(s, axis=1, keepdims=True)
        e = jnp.exp(s - peak)
        norm = jnp.sum(e, axis=1, keepdims=True)
        o = mm(e.astype(BF), xp_ref[2, :, start : start + width] * mask) / norm
        lse = jnp.where(lane == h, peak + jnp.log(norm), lse)
        for part in range(width // LANES):
            t = start // LANES + part
            piece = o[:, part * LANES : (part + 1) * LANES]
            total[t] = piece if total[t] is None else total[t] + piece
    for t, value in enumerate(total):
        o_ref[:, t * LANES : (t + 1) * LANES] = value
    lse_ref[...] = lse


def owner_fwd(q, k, v, heads):
    rows = q.shape[0]
    lane = iota2((rows, LANES), 1)
    lse = jnp.full((rows, LANES), NEGATIVE_FILL, F32)
    out = jnp.zeros((rows, LANES), F32)
    for e in range(heads):
        mask = lane_mask(LANES, HEAD * e, HEAD * (e + 1), HEAD * heads)
        s = mm_t(q * mask, k) * SCALE
        peak = jnp.max(s, axis=1, keepdims=True)
        weights = jnp.exp(s - peak)
        norm = jnp.sum(weights, axis=1, keepdims=True)
        part = mm(weights.astype(BF), v * lane_mask(LANES, HEAD * e, HEAD * (e + 1)))
        out = out + part / norm
        lse = jnp.where(lane == e, peak + jnp.log(norm), lse)
    return out, lse


def slide_members(ss_ref, sources):
    wide = ss_ref[...].astype(F32)
    return [
        wide[:, 8 * a : 8 * a + 8].reshape(sources * 8, LANES).astype(BF) for a in range(4)
    ]


def group_fwd(gr_ref, go_ref):
    groups = gr_ref.shape[0]
    q, k, v = [gr_ref[:, a].reshape(groups * 32, LANES) for a in range(3)]
    out, lse = owner_fwd(q, k, v, 2)
    go_ref[:, 0] = out.reshape(groups, 32, LANES)
    go_ref[:, 1] = lse.reshape(groups, 32, LANES)


def slide_fwd(sr_ref, so_ref):
    sources = sr_ref.shape[0]
    q, k, v, _ = slide_members(sr_ref, sources)
    out, lse = owner_fwd(q, k, v, 1)
    so_ref[:, 0] = out.reshape(sources, 8, LANES)
    so_ref[:, 1] = lse.reshape(sources, 8, LANES)


def head_spread(transposed):
    shape = (HEADS * HEAD, LANES) if transposed else (LANES, HEADS * HEAD)
    head, col = (iota2(shape, 1), iota2(shape, 0)) if transposed else (iota2(shape, 0), iota2(shape, 1))
    return ((col >= head * HEAD) & (col < head * HEAD + HEAD)).astype(F32).astype(BF)


def combine_kernel(
    xp_ref, on_ref, ln_ref, go_ref, so_ref, att_ref, plane_t_ref, g2_ref, s2_ref, acc_ref
):
    lane32 = iota2((32, LANES), 1)
    lane8 = iota2((8, LANES), 1)
    near = ln_ref[...]
    group_rows, slide_rows = [], [None] * HEADS
    for o in range(4):
        pieces = []
        for p in (2 * o, 2 * o + 1):
            moved = pltpu.roll(go_ref[p, 1], 2 * p, 1) if p else go_ref[p, 1]
            keep = (lane32 >= 2 * p) & (lane32 < 2 * p + 2)
            pieces.append(jnp.where(keep, moved, NEGATIVE_FILL))
        group_rows.append(jnp.maximum(pieces[0], pieces[1]))
    for r in range(HEADS):
        moved = pltpu.roll(so_ref[r, 1], r, 1) if r else so_ref[r, 1]
        slide_rows[slide_row(r) // 8] = jnp.where(lane8 == r, moved, NEGATIVE_FILL)
    group = jnp.concatenate(group_rows, axis=0)
    slide = jnp.concatenate(slide_rows, axis=0)
    best = jnp.maximum(jnp.maximum(near, group), slide)
    near_w, group_w, slide_w = jnp.exp(near - best), jnp.exp(group - best), jnp.exp(slide - best)
    den = near_w + group_w + slide_w
    lse = best + jnp.log(den)
    spread = head_spread(False)
    acc_ref[0:2] = jnp.zeros((2,) + acc_ref.shape[1:], F32)
    for p in range(HEADS // 2):
        row = p // 2 * 32
        start, width, shift = window(PAIR * p, PAIR)
        acc_ref[0, row : row + 32, start : start + width] += mm(
            go_ref[p, 0].astype(BF), shift_out(width, shift, PAIR)
        )
    for r in range(HEADS):
        row = slide_row(r)
        start, width, shift = window(HEAD * r, HEAD)
        acc_ref[1, row : row + 8, start : start + width] += mm(
            so_ref[r, 0].astype(BF), shift_out(width, shift, HEAD)
        )
    attended = (
        on_ref[...] * split_mm(near_w / den, spread)
        + acc_ref[0] * split_mm(group_w / den, spread)
        + acc_ref[1] * split_mm(slide_w / den, spread)
    ).astype(BF)
    att_ref[...] = mm(permute_matrix(True), attended).astype(BF)
    product = xp_ref[3].astype(F32) * attended.astype(F32)
    delta = split_mm(product, head_spread(True))
    lane = iota2((LANES, LANES), 1)
    plane = jnp.where(lane < HEADS, lse, pltpu.roll(delta, HEADS, 1))
    plane_t_ref[...] = plane.T
    for p in range(HEADS // 2):
        row = p // 2 * 32
        block = plane[row : row + 32]
        g2_ref[p] = pltpu.roll(block, LANES - 2 * p, 1) if p else block
    for r in range(HEADS):
        row = slide_row(r)
        block = plane[row : row + 8]
        block = pltpu.roll(block, LANES - r, 1) if r else block
        s2_ref[r] = block


def near_bwd_kernel(len_ref, xp_ref, plane_t_ref, grads_ref):
    bias = key_bias(len_ref, 0)
    tiles = HEADS * HEAD // LANES
    totals = [[None] * tiles for _ in range(3)]
    for h in range(HEADS):
        start, width, shift = window(HEAD * h, HEAD)
        mask = lane_mask(width, shift, shift + HEAD)
        qm, km, vm, cm = [xp_ref[a, :, start : start + width] * mask for a in range(4)]
        s = mm_t(km, qm) * SCALE + bias
        weights = jnp.exp(s - plane_t_ref[h : h + 1, :])
        dp = mm_t(vm, cm)
        ds = (weights * (dp - plane_t_ref[HEADS + h : HEADS + h + 1, :])).astype(BF)
        results = (t_mm(ds, km), mm(ds, qm), mm(weights.astype(BF), cm))
        for index, value in enumerate(results):
            for part in range(width // LANES):
                t = start // LANES + part
                piece = value[:, part * LANES : (part + 1) * LANES]
                old = totals[index][t]
                totals[index][t] = piece if old is None else old + piece
    for index in range(3):
        for t in range(tiles):
            value = totals[index][t]
            grads_ref[index, :, t * LANES : (t + 1) * LANES] = value * SCALE if index < 2 else value


def owner_bwd(q, k, v, c, plane, heads):
    plane_t = plane.T
    sums = [None] * 3
    for e in range(heads):
        mask = lane_mask(LANES, HEAD * e, HEAD * (e + 1))
        q_flag = q * lane_mask(LANES, HEAD * e, HEAD * (e + 1), HEAD * heads)
        cm = c * mask
        s = mm_t(k, q_flag) * SCALE
        weights = jnp.exp(s - plane_t[e : e + 1, :])
        dp = mm_t(v, cm)
        ds = (weights * (dp - plane_t[HEADS + e : HEADS + e + 1, :])).astype(BF)
        parts = (t_mm(ds, k * mask), mm(ds, q * mask), mm(weights.astype(BF), cm))
        sums = [part if old is None else old + part for old, part in zip(sums, parts)]
    return sums[0] * SCALE, sums[1] * SCALE, sums[2]


def group_bwd(gr_ref, gp_ref, go_ref):
    groups = gr_ref.shape[0]
    members = [gr_ref[:, a].reshape(groups * 32, LANES) for a in range(4)]
    grads = owner_bwd(*members, gp_ref[...].reshape(groups * 32, LANES), 2)
    for a in range(3):
        go_ref[:, a] = grads[a].reshape(groups, 32, LANES).astype(BF)


def slide_bwd(sr_ref, sp_ref, so_ref):
    sources = sr_ref.shape[0]
    members = slide_members(sr_ref, sources)
    grads = owner_bwd(*members, sp_ref[...].reshape(sources * 8, LANES), 1)
    stacked = [grad.reshape(sources, 8, LANES) for grad in grads]
    stacked.append(jnp.zeros((sources, 8, LANES), F32))
    so_ref[...] = jnp.concatenate(stacked, axis=1).astype(BF)


def final_kernel(near_ref, go_ref, so_ref, dq_ref, dk_ref, dv_ref, acc_ref):
    acc_ref[...] = near_ref[...]
    for p in range(HEADS // 2):
        row = p // 2 * 32
        start, width, shift = window(PAIR * p, PAIR)
        moved = mm(go_ref[p].reshape(96, LANES), shift_out(width, shift, PAIR))
        for a in range(3):
            acc_ref[a, row : row + 32, start : start + width] += moved[32 * a : 32 * a + 32]
    for r in range(HEADS):
        row = slide_row(r)
        start, width, shift = window(HEAD * r, HEAD)
        moved = mm(so_ref[r], shift_out(width, shift, HEAD))
        for a in range(3):
            acc_ref[a, row : row + 8, start : start + width] += moved[8 * a : 8 * a + 8]
    back = permute_matrix(True)
    for a, ref in enumerate((dq_ref, dk_ref, dv_ref)):
        ref[...] = mm(back, acc_ref[a].astype(BF)).astype(BF)


MESH = pl.DeviceIdType.MESH


def remote(src, dst, send_sem, recv_sem, outer, inner):
    return pltpu.make_async_remote_copy(
        src_ref=src,
        dst_ref=dst,
        send_sem=send_sem,
        recv_sem=recv_sem,
        device_id=(outer, inner),
        device_id_type=MESH,
    )


class Group:
    def __init__(self, inner, src, dst, send_sem, recv_sem):
        self.inner, self.src, self.dst = inner, src, dst
        self.send_sem, self.recv_sem = send_sem, recv_sem

    def copy(self, step):
        me = lax.axis_index("inner")
        peer = lax.rem(me + step, self.inner)
        return remote(
            self.src.at[peer],
            self.dst.at[me],
            self.send_sem.at[step],
            self.recv_sem.at[step],
            lax.axis_index("outer"),
            peer,
        )

    def start(self):
        @pl.loop(1, self.inner)
        def _(step):
            self.copy(step).start()

        me = lax.axis_index("inner")
        self.dst[me] = self.src[me]

    def wait_recv(self):
        @pl.loop(1, self.inner)
        def _(step):
            self.copy(step).wait_recv()

    def wait_send(self):
        @pl.loop(1, self.inner)
        def _(step):
            self.copy(step).wait_send()


def owner_of(head, inner):
    return 2 * (head // inner), lax.rem(head, inner)


class ToOwner:
    def __init__(self, inner, devices, src, dst, send_sem, recv_sem):
        self.inner, self.devices, self.src, self.dst = inner, devices, src, dst
        self.send_sem, self.recv_sem = send_sem, recv_sem

    def place(self):
        return lax.axis_index("outer"), lax.axis_index("inner")

    def copy(self, head):
        outer, inner = self.place()
        to_outer, to_inner = owner_of(head, self.inner)
        me = outer * self.inner + inner
        return remote(
            self.src.at[head],
            self.dst.at[me],
            self.send_sem.at[head],
            self.recv_sem.at[me],
            to_outer,
            to_inner,
        )

    def each(self, other, own):
        outer, inner = self.place()
        me = outer * self.inner + inner

        @pl.loop(0, HEADS)
        def _(step):
            head = lax.rem(step + me, HEADS)
            to_outer, to_inner = owner_of(head, self.inner)
            at_home = (to_outer * self.inner + to_inner) == me

            @pl.when(jnp.logical_not(at_home))
            def _():
                other(head)

            if own is not None:

                @pl.when(at_home)
                def _():
                    own(head, me)

    def start(self):
        def keep(head, me):
            self.dst[me] = self.src[head]

        self.each(lambda head: self.copy(head).start(), keep)

    def wait_recv(self):
        outer, inner = self.place()
        me = outer * self.inner + inner

        @pl.loop(0, self.devices)
        def _(source):
            @pl.when(source != me)
            def _():
                remote(
                    self.src.at[0],
                    self.dst.at[source],
                    self.send_sem.at[0],
                    self.recv_sem.at[source],
                    source // self.inner,
                    lax.rem(source, self.inner),
                ).wait_recv()

    def wait_send(self):
        self.each(lambda head: self.copy(head).wait_send(), None)


class FromOwner:
    def __init__(self, inner, devices, src, dst, send_sem, recv_sem):
        self.inner, self.devices, self.src, self.dst = inner, devices, src, dst
        self.send_sem, self.recv_sem = send_sem, recv_sem

    def copy(self, target):
        outer, inner = lax.axis_index("outer"), lax.axis_index("inner")
        head = outer // 2 * self.inner + inner
        return remote(
            self.src.at[target],
            self.dst.at[head],
            self.send_sem.at[target],
            self.recv_sem.at[head],
            target // self.inner,
            lax.rem(target, self.inner),
        )

    def start(self):
        outer, inner = lax.axis_index("outer"), lax.axis_index("inner")
        me = outer * self.inner + inner

        @pl.loop(1, self.devices)
        def _(step):
            self.copy(lax.rem(me + step, self.devices)).start()

        self.dst[outer // 2 * self.inner + inner] = self.src[me]

    def wait_recv(self):
        me = lax.axis_index("outer") * self.inner + lax.axis_index("inner")

        @pl.loop(0, HEADS)
        def _(head):
            from_outer, from_inner = owner_of(head, self.inner)

            @pl.when((from_outer * self.inner + from_inner) != me)
            def _():
                remote(
                    self.src.at[0],
                    self.dst.at[head],
                    self.send_sem.at[0],
                    self.recv_sem.at[head],
                    from_outer,
                    from_inner,
                ).wait_recv()

    def wait_send(self):
        me = lax.axis_index("outer") * self.inner + lax.axis_index("inner")

        @pl.loop(1, self.devices)
        def _(step):
            self.copy(lax.rem(me + step, self.devices)).wait_send()


def whole_kernel(inner, devices, len_ref, q_ref, k_ref, v_ref, c_ref, att_ref, dq_ref, dk_ref, dv_ref, *scratch):
    (xp, near_out, near_lse, plane_t, near_grads, acc) = scratch[:6]
    (g1s, g1r, s1s, s1r, g2s, g2r, s2s, s2r, g3s, g3r, s3s, s3r, g4s, g4r, s4s, s4r) = scratch[6:22]
    group_send, group_recv, slide_send, slide_recv = scratch[22:]
    outer, place = lax.axis_index("outer"), lax.axis_index("inner")
    me = outer * inner + place
    is_owner = lax.rem(outer, 2) == 0

    def group_exchange(phase, src, dst):
        return Group(inner, src, dst, group_send.at[phase], group_recv.at[phase])

    def slide_exchange(kind, phase, src, dst):
        return kind(inner, devices, src, dst, slide_send.at[phase], slide_recv.at[phase])

    group1, slide1 = group_exchange(0, g1s, g1r), slide_exchange(ToOwner, 0, s1s, s1r)
    group2, slide2 = group_exchange(1, g2s, g2r), slide_exchange(FromOwner, 1, s2s, s2r)
    group3, slide3 = group_exchange(2, g3s, g3r), slide_exchange(ToOwner, 2, s3s, s3r)
    group4, slide4 = group_exchange(3, g4s, g4r), slide_exchange(FromOwner, 3, s4s, s4r)

    barrier = pltpu.get_barrier_semaphore()

    @pl.loop(1, devices)
    def _(step):
        other = lax.rem(me + step, devices)
        pl.semaphore_signal(
            barrier,
            inc=1,
            device_id=(other // inner, lax.rem(other, inner)),
            device_id_type=MESH,
        )

    prep_kernel(len_ref, q_ref, k_ref, v_ref, c_ref, xp, g1s, s1s)
    pl.semaphore_wait(barrier, devices - 1)
    slide1.start()
    group1.start()
    near_fwd_kernel(len_ref, xp, near_out, near_lse)

    @pl.when(is_owner)
    def _():
        slide1.wait_recv()
        slide_fwd(s1r, s2s)
        slide2.start()

    group1.wait_recv()
    group_fwd(g1r, g2s)
    group2.start()
    group2.wait_recv()
    slide2.wait_recv()
    combine_kernel(xp, near_out, near_lse, g2r, s2r, att_ref, plane_t, g3s, s3s, acc)
    slide3.start()
    group3.start()
    near_bwd_kernel(len_ref, xp, plane_t, near_grads)

    @pl.when(is_owner)
    def _():
        slide3.wait_recv()
        slide_bwd(s1r, s3r, s4s)
        slide4.start()

    group3.wait_recv()
    group_bwd(g1r, g3r, g4s)
    group4.start()
    group4.wait_recv()
    slide4.wait_recv()
    final_kernel(near_grads, g4r, s4r, dq_ref, dk_ref, dv_ref, acc)
    for sent in (group1, slide1, group2, group3, slide3, group4):
        sent.wait_send()

    @pl.when(is_owner)
    def _():
        slide2.wait_send()
        slide4.wait_send()


def fast_local(inner, devices, *args):
    row_lengths, tiles_in = args[4], args[:4]
    tiles, width = tiles_in[0].shape
    vmem = pl.BlockSpec(memory_space=pltpu.VMEM)

    def both(count, back, shape, dtype):
        return [pltpu.VMEM((count,) + shape, dtype), pltpu.VMEM((back,) + shape, dtype)]

    scratch = [
        pltpu.VMEM((4, tiles, width), BF),
        pltpu.VMEM((tiles, width), F32),
        pltpu.VMEM((tiles, LANES), F32),
        pltpu.VMEM((LANES, tiles), F32),
        pltpu.VMEM((3, tiles, width), F32),
        pltpu.VMEM((3, tiles, width), F32),
    ]
    scratch += both(inner, inner, (4, 32, LANES), BF) + both(HEADS, devices, (32, LANES), BF)
    scratch += both(inner, inner, (2, 32, LANES), F32) + both(devices, HEADS, (2, 8, LANES), F32)
    scratch += both(inner, inner, (32, LANES), F32) + both(HEADS, devices, (8, LANES), F32)
    scratch += both(inner, inner, (3, 32, LANES), BF) + both(devices, HEADS, (32, LANES), BF)
    scratch += [pltpu.SemaphoreType.DMA((4, inner))] * 2 + [pltpu.SemaphoreType.DMA((4, devices))] * 2
    return tuple(
        pl.pallas_call(
            lambda *refs: whole_kernel(inner, devices, *refs),
            out_shape=[jax.ShapeDtypeStruct((tiles, width), BF)] * 4,
            in_specs=[pl.BlockSpec(memory_space=pltpu.SMEM)] + [vmem] * 4,
            out_specs=[vmem] * 4,
            scratch_shapes=scratch,
            compiler_params=pltpu.CompilerParams(
                collective_id=0, has_side_effects=True, vmem_limit_bytes=48 * 1024 * 1024
            ),
        )(row_lengths, *tiles_in)
    )


def solution(mesh):
    in_specs = (P(("outer", "inner"), None),) * 4 + (P(("outer", "inner")),)
    out_specs = (P(("outer", "inner"), None),) * 4
    inner = mesh.shape["inner"]
    devices = inner * mesh.shape["outer"]

    def step(*args):
        owners = 2 * inner == HEADS and devices == 2 * HEADS
        if owners and args[0].shape == (LANES, HEADS * HEAD):
            return fast_local(inner, devices, *args)
        return local(*args)

    return jax.shard_map(step, mesh=mesh, in_specs=in_specs, out_specs=out_specs, check_vma=False)
```

```python
import jax
import jax.numpy as jnp
import numpy as np
from jax import lax
from jax.experimental import pallas as pl
from jax.experimental.pallas import tpu as pltpu
from jax.sharding import PartitionSpec as P

HEADS = 16
HEAD = 48
ROW = 32
STRIDE_GROUP = 4
STRIDE_SLIDE = 16


NEGATIVE_FILL = -1e30
heads_at_once = 4


def as_sent(value):

    def short(part):
        return part.astype(jnp.bfloat16) if part.dtype == jnp.float32 else part

    return jax.tree.map(short, value)


def head_ranges(head_total):
    step_size = min(head_total, heads_at_once)
    return [(first_head, first_head + step_size) for first_head in range(0, head_total, step_size)]


def scores_of(query_block, key_block, score_scale):
    return (
        jnp.einsum("hdq,hdk->hqk", query_block, key_block, preferred_element_type=jnp.float32)
        * score_scale
    )


def branch_stats(query_heads, key_heads, value_heads, key_valid, score_scale):
    peak_list, total_list, sum_list = ([], [], [])
    for first_head, last_head in head_ranges(query_heads.shape[0]):
        raw_scores = scores_of(
            query_heads[first_head:last_head], key_heads[first_head:last_head], score_scale
        )
        key_keep = key_valid[first_head:last_head][:, None, :]
        masked = jnp.where(key_keep, raw_scores, NEGATIVE_FILL)
        row_peak = jnp.max(masked, axis=2)
        weights = jnp.where(key_keep, jnp.exp(masked - row_peak[:, :, None]), 0.0)
        peak_list.append(row_peak)
        total_list.append(jnp.sum(weights, axis=2))
        sum_list.append(
            jnp.einsum(
                "hqk,hdk->hdq",
                weights.astype(jnp.bfloat16),
                value_heads[first_head:last_head],
                preferred_element_type=jnp.float32,
            )
        )
    return (
        jnp.concatenate(peak_list, axis=0),
        jnp.concatenate(total_list, axis=0),
        jnp.concatenate(sum_list, axis=0),
    )


def branch_grads(
    query_heads,
    key_heads,
    value_heads,
    cotan_heads,
    log_norm,
    out_dot,
    key_valid,
    score_scale,
    want_query,
    want_keys,
):
    query_list, key_list, value_list = ([], [], [])
    for first_head, last_head in head_ranges(query_heads.shape[0]):
        query_block = query_heads[first_head:last_head]
        key_block = key_heads[first_head:last_head]
        cotan_block = cotan_heads[first_head:last_head]
        raw_scores = scores_of(query_block, key_block, score_scale)
        key_keep = key_valid[first_head:last_head][:, None, :]
        weights = jnp.where(
            key_keep, jnp.exp(raw_scores - log_norm[first_head:last_head][:, :, None]), 0.0
        )
        weight_grads = jnp.einsum(
            "hdq,hdk->hqk",
            cotan_block,
            value_heads[first_head:last_head],
            preferred_element_type=jnp.float32,
        )
        low_grads = (weights * (weight_grads - out_dot[first_head:last_head][:, :, None])).astype(
            jnp.bfloat16
        )
        if want_query:
            query_list.append(
                score_scale
                * jnp.einsum(
                    "hqk,hdk->hdq", low_grads, key_block, preferred_element_type=jnp.float32
                )
            )
        if want_keys:
            key_list.append(
                score_scale
                * jnp.einsum(
                    "hqk,hdq->hdk", low_grads, query_block, preferred_element_type=jnp.float32
                )
            )
            value_list.append(
                jnp.einsum(
                    "hqk,hdq->hdk",
                    weights.astype(jnp.bfloat16),
                    cotan_block,
                    preferred_element_type=jnp.float32,
                )
            )
    query_part = jnp.concatenate(query_list, axis=0) if want_query else None
    key_part = jnp.concatenate(key_list, axis=0) if want_keys else None
    value_part = jnp.concatenate(value_list, axis=0) if want_keys else None
    return (query_part, key_part, value_part)


def head_offsets(head_total, stride):
    return np.arange(head_total) * stride // head_total


def select_rows(array_in, stride):
    head_total = array_in.shape[0]
    offsets = head_offsets(head_total, stride)
    folded = array_in.reshape(array_in.shape[:-1] + (array_in.shape[-1] // stride, stride))
    return jnp.stack(
        [folded[head_index, ..., int(offsets[head_index])] for head_index in range(head_total)]
    )


def spread_rows(array_in, stride, fill_value):
    head_total = array_in.shape[0]
    chosen = np.arange(stride)[None, :] == head_offsets(head_total, stride)[:, None]
    chosen = chosen.reshape((head_total,) + (1,) * (array_in.ndim - 1) + (stride,))
    full = jnp.where(chosen, array_in[..., None], fill_value)
    return full.reshape(array_in.shape[:-1] + (array_in.shape[-1] * stride,))


def to_heads(flat_in):
    return jnp.transpose(flat_in.reshape(flat_in.shape[0], HEADS, -1), (1, 2, 0))


def to_flat(heads_in):
    return jnp.transpose(heads_in, (2, 0, 1)).reshape(heads_in.shape[2], -1)


def local(query_tiles, key_tiles, value_tiles, cotangent, row_lengths):
    tile_count = query_tiles.shape[0]
    score_scale = HEAD ** (-0.5)
    query_heads = to_heads(query_tiles)
    key_heads = to_heads(key_tiles)
    value_heads = to_heads(value_tiles)
    cotan_heads = to_heads(cotangent)
    tile_slot = jnp.arange(tile_count, dtype=jnp.int32)
    tile_valid = tile_slot % ROW < jnp.repeat(row_lengths, ROW, total_repeat_length=tile_count)
    valid_heads = jnp.broadcast_to(tile_valid[None, :], (HEADS, tile_count))
    group_query = select_rows(query_heads, STRIDE_GROUP)
    group_key = select_rows(key_heads, STRIDE_GROUP)
    group_value = select_rows(value_heads, STRIDE_GROUP)
    group_cotan = select_rows(cotan_heads, STRIDE_GROUP)
    group_valid = select_rows(valid_heads, STRIDE_GROUP)
    group_flag = group_valid.astype(jnp.bfloat16)[:, None, :]
    slide_query = select_rows(query_heads, STRIDE_SLIDE)
    slide_key = select_rows(key_heads, STRIDE_SLIDE)
    slide_value = select_rows(value_heads, STRIDE_SLIDE)
    slide_flag = select_rows(valid_heads, STRIDE_SLIDE).astype(jnp.bfloat16)[:, None, :]
    owned_query, owned_key, owned_value, owned_flag = (
        lax.all_to_all(slide_query, "outer", split_axis=0, concat_axis=2, tiled=True),
        lax.all_to_all(slide_key, "outer", split_axis=0, concat_axis=2, tiled=True),
        lax.all_to_all(slide_value, "outer", split_axis=0, concat_axis=2, tiled=True),
        lax.all_to_all(slide_flag, "outer", split_axis=0, concat_axis=2, tiled=True),
    )
    got_group = (
        lax.all_gather(group_key, "inner", axis=2, tiled=True),
        lax.all_gather(group_value, "inner", axis=2, tiled=True),
        lax.all_gather(group_flag, "inner", axis=2, tiled=True),
    )
    got_slide = (
        lax.all_gather(owned_key, "inner", axis=2, tiled=True),
        lax.all_gather(owned_value, "inner", axis=2, tiled=True),
        lax.all_gather(owned_flag, "inner", axis=2, tiled=True),
    )
    near_peak, near_total, near_sum = branch_stats(
        query_heads, key_heads, value_heads, valid_heads, score_scale
    )
    remote_group_key = got_group[0]
    remote_group_value = got_group[1]
    remote_group_valid = got_group[2][:, 0, :] > 0.5
    group_peak, group_total, group_sum = branch_stats(
        group_query, remote_group_key, remote_group_value, remote_group_valid, score_scale
    )
    slide_all_key = got_slide[0]
    slide_all_value = got_slide[1]
    slide_all_valid = got_slide[2][:, 0, :] > 0.5
    owner_peak, owner_total, owner_sum = branch_stats(
        owned_query, slide_all_key, slide_all_value, slide_all_valid, score_scale
    )
    slide_peak, slide_total, slide_sum = (
        lax.all_to_all(owner_peak[:, None, :], "outer", split_axis=2, concat_axis=0, tiled=True),
        lax.all_to_all(owner_total[:, None, :], "outer", split_axis=2, concat_axis=0, tiled=True),
        lax.all_to_all(owner_sum, "outer", split_axis=2, concat_axis=0, tiled=True),
    )
    slide_peak = slide_peak[:, 0, :]
    slide_total = slide_total[:, 0, :]
    group_peak_full = spread_rows(group_peak, STRIDE_GROUP, NEGATIVE_FILL)
    slide_peak_full = spread_rows(slide_peak, STRIDE_SLIDE, NEGATIVE_FILL)
    best_peak = jnp.maximum(jnp.maximum(near_peak, group_peak_full), slide_peak_full)
    near_weight = jnp.exp(near_peak - best_peak)
    group_weight = jnp.exp(group_peak_full - best_peak)
    slide_weight = jnp.exp(slide_peak_full - best_peak)
    denominator = (
        near_total * near_weight
        + spread_rows(group_total, STRIDE_GROUP, 0.0) * group_weight
        + spread_rows(slide_total, STRIDE_SLIDE, 0.0) * slide_weight
    )
    numerator = (
        near_sum * near_weight[:, None, :]
        + spread_rows(group_sum, STRIDE_GROUP, 0.0) * group_weight[:, None, :]
        + spread_rows(slide_sum, STRIDE_SLIDE, 0.0) * slide_weight[:, None, :]
    )
    attended = (numerator / denominator[:, None, :]).astype(jnp.bfloat16)
    log_norm = best_peak + jnp.log(denominator)
    out_dot = jnp.sum(cotan_heads.astype(jnp.float32) * attended.astype(jnp.float32), axis=1)
    near_query, near_key, near_value = branch_grads(
        query_heads,
        key_heads,
        value_heads,
        cotan_heads,
        log_norm,
        out_dot,
        valid_heads,
        score_scale,
        True,
        True,
    )
    group_lse = select_rows(log_norm, STRIDE_GROUP)
    group_dot = select_rows(out_dot, STRIDE_GROUP)
    group_query_grad = branch_grads(
        group_query,
        remote_group_key,
        remote_group_value,
        group_cotan,
        group_lse,
        group_dot,
        remote_group_valid,
        score_scale,
        True,
        False,
    )[0]
    got_group_rows = (
        lax.all_gather(group_query, "inner", axis=2, tiled=True),
        lax.all_gather(group_cotan, "inner", axis=2, tiled=True),
    )
    got_group_stats = (
        lax.all_gather(group_lse, "inner", axis=1, tiled=True),
        lax.all_gather(group_dot, "inner", axis=1, tiled=True),
    )
    unused_group, group_key_grad, group_value_grad = branch_grads(
        got_group_rows[0],
        group_key,
        group_value,
        got_group_rows[1],
        got_group_stats[0],
        got_group_stats[1],
        group_valid,
        score_scale,
        False,
        True,
    )
    slide_cotan = select_rows(cotan_heads, STRIDE_SLIDE)
    slide_lse = select_rows(log_norm, STRIDE_SLIDE)
    slide_dot = select_rows(out_dot, STRIDE_SLIDE)
    owned_cotan = lax.all_to_all(slide_cotan, "outer", split_axis=0, concat_axis=2, tiled=True)
    owned_lse, owned_dot = (
        lax.all_to_all(slide_lse, "outer", split_axis=0, concat_axis=1, tiled=True),
        lax.all_to_all(slide_dot, "outer", split_axis=0, concat_axis=1, tiled=True),
    )
    owned_query_grad, partial_key, partial_value = branch_grads(
        owned_query,
        slide_all_key,
        slide_all_value,
        owned_cotan,
        owned_lse,
        owned_dot,
        slide_all_valid,
        score_scale,
        True,
        True,
    )
    owned_key_grad, owned_value_grad = (
        lax.psum_scatter(
            partial_key.astype(jnp.bfloat16), "inner", scatter_dimension=2, tiled=True
        ).astype(jnp.float32),
        lax.psum_scatter(
            partial_value.astype(jnp.bfloat16), "inner", scatter_dimension=2, tiled=True
        ).astype(jnp.float32),
    )
    slide_query_grad, slide_key_grad, slide_value_grad = (
        lax.all_to_all(
            as_sent(owned_query_grad), "outer", split_axis=2, concat_axis=0, tiled=True
        ).astype(owned_query_grad.dtype),
        lax.all_to_all(
            owned_key_grad.astype(jnp.bfloat16), "outer", split_axis=2, concat_axis=0, tiled=True
        ).astype(owned_key_grad.dtype),
        lax.all_to_all(
            owned_value_grad.astype(jnp.bfloat16), "outer", split_axis=2, concat_axis=0, tiled=True
        ).astype(owned_value_grad.dtype),
    )
    query_grad = (
        near_query
        + spread_rows(group_query_grad, STRIDE_GROUP, 0.0)
        + spread_rows(slide_query_grad, STRIDE_SLIDE, 0.0)
    )
    key_grad = (
        near_key
        + spread_rows(group_key_grad, STRIDE_GROUP, 0.0)
        + spread_rows(slide_key_grad, STRIDE_SLIDE, 0.0)
    )
    value_grad = (
        near_value
        + spread_rows(group_value_grad, STRIDE_GROUP, 0.0)
        + spread_rows(slide_value_grad, STRIDE_SLIDE, 0.0)
    )
    return (
        to_flat(attended),
        to_flat(query_grad.astype(jnp.bfloat16)),
        to_flat(key_grad.astype(jnp.bfloat16)),
        to_flat(value_grad.astype(jnp.bfloat16)),
    )


BF = jnp.bfloat16
F32 = jnp.float32
LANES = 128
SCALE = HEAD ** (-0.5)
PAIR = 2 * HEAD
UPPER = LANES // 2


def window(first_col, width):
    start = first_col // LANES * LANES
    shift = first_col - start
    return start, (LANES if shift + width <= LANES else 2 * LANES), shift


def iota2(shape, axis):
    return lax.broadcasted_iota(jnp.int32, shape, axis)


def original_tile(j):
    return (j & 7) * 16 + ((j >> 3) & 3) * 4 + (j >> 5)


def permute_matrix(inverse):
    shape = (LANES, LANES)
    j, i = (iota2(shape, 1), iota2(shape, 0)) if inverse else (iota2(shape, 0), iota2(shape, 1))
    return (original_tile(j) == i).astype(F32).astype(BF)


def key_bias(len_ref, axis):
    tile = original_tile(iota2((LANES, LANES), axis))
    row = tile >> 5
    length = jnp.full((LANES, LANES), len_ref[0], jnp.int32)
    for index in range(1, 4):
        length = jnp.where(row == index, len_ref[index], length)
    return jnp.where((tile & 31) < length, 0.0, NEGATIVE_FILL).astype(F32)


def shift_in(width, shift, kept, base=0):
    row, col = iota2((width, LANES), 0), iota2((width, LANES), 1)
    return ((row - shift + base == col) & (col >= base) & (col < base + kept)).astype(F32).astype(BF)


def shift_out(width, shift, kept, base=0):
    row, col = iota2((LANES, width), 0), iota2((LANES, width), 1)
    return ((col - shift + base == row) & (row >= base) & (row < base + kept)).astype(F32).astype(BF)


def lane_mask(width, first, last, extra=-1):
    lane = iota2((1, width), 1)
    keep = (lane >= first) & (lane < last)
    if extra >= 0:
        keep = keep | (lane == extra)
    return keep.astype(F32).astype(BF)


def mm(a, b):
    return jnp.dot(a, b, preferred_element_type=F32)


def mm_t(a, b):
    return lax.dot_general(a, b, (((1,), (1,)), ((), ())), preferred_element_type=F32)


def t_mm(a, b):
    return lax.dot_general(a, b, (((0,), (0,)), ((), ())), preferred_element_type=F32)


def slide_row(r):
    return (r % 4) * 32 + (r // 4) * 8


def split_mm(a, onehot):
    high = a.astype(BF)
    low = (a - high.astype(F32)).astype(BF)
    return mm(high, onehot) + mm(low, onehot)


def prep_kernel(len_ref, q_ref, k_ref, v_ref, c_ref, xp_ref, gs_ref, gc_ref, ss_ref):
    perm = permute_matrix(False)
    xs = []
    for index, ref in enumerate((q_ref, k_ref, v_ref, c_ref)):
        xs.append(mm(perm, ref[...]))
        xp_ref[index] = xs[-1].astype(BF)
    bias = key_bias(len_ref, 0)
    for p in range(HEADS // 2):
        row = p // 2 * 32
        start, width, shift = window(PAIR * p, PAIR)
        stacked = jnp.concatenate(
            [x[row : row + 32, start : start + width].astype(BF) for x in xs], axis=0
        )
        moved = mm(stacked, shift_in(width, shift, PAIR))
        flag = iota2((32, LANES), 1) == PAIR
        gs_ref[p, 0] = jnp.where(flag, 1.0, moved[0:32]).astype(BF)
        gs_ref[p, 1] = jnp.where(flag, bias[row : row + 32], moved[32:64]).astype(BF)
        gs_ref[p, 2] = moved[64:96].astype(BF)
        gc_ref[p] = moved[96:128].astype(BF)
    for r in range(HEADS):
        row = slide_row(r)
        start, width, shift = window(HEAD * r, HEAD)
        low, high = [
            jnp.concatenate(
                [xs[a][row : row + 8, start : start + width] for a in pair], axis=0
            ).astype(BF)
            for pair in ((0, 1), (3, 2))
        ]
        moved = mm(low, shift_in(width, shift, HEAD)) + mm(high, shift_in(width, shift, HEAD, UPPER))
        flags = jnp.concatenate([jnp.ones((8, LANES), F32), bias[row : row + 8]], axis=0)
        ss_ref[r] = jnp.where(iota2((16, LANES), 1) == HEAD, flags, moved).astype(BF)


def near_fwd_kernel(len_ref, xp_ref, o_ref, lse_ref):
    bias = key_bias(len_ref, 1)
    lane = iota2((LANES, LANES), 1)
    lse = jnp.full((LANES, LANES), NEGATIVE_FILL, F32)
    total = [None] * (HEADS * HEAD // LANES)
    for h in range(HEADS):
        start, width, shift = window(HEAD * h, HEAD)
        mask = lane_mask(width, shift, shift + HEAD)
        s = mm_t(xp_ref[0, :, start : start + width] * mask, xp_ref[1, :, start : start + width])
        s = s * SCALE + bias
        peak = jnp.max(s, axis=1, keepdims=True)
        e = jnp.exp(s - peak)
        norm = jnp.sum(e, axis=1, keepdims=True)
        o = mm(e.astype(BF), xp_ref[2, :, start : start + width] * mask) / norm
        lse = jnp.where(lane == h, peak + jnp.log(norm), lse)
        for part in range(width // LANES):
            t = start // LANES + part
            piece = o[:, part * LANES : (part + 1) * LANES]
            total[t] = piece if total[t] is None else total[t] + piece
    for t, value in enumerate(total):
        o_ref[:, t * LANES : (t + 1) * LANES] = value
    lse_ref[...] = lse


def three_parts(value):
    high = value.astype(BF).astype(F32)
    rest = value - high
    middle = rest.astype(BF).astype(F32)
    return high, middle, rest - middle


def attend(q, k, v):
    s = mm_t(q, k) * SCALE
    peak = jnp.max(s, axis=1, keepdims=True)
    weights = jnp.exp(s - peak)
    norm = jnp.sum(weights, axis=1, keepdims=True)
    return mm(weights.astype(BF), v) / norm, three_parts(peak + jnp.log(norm))


def group_fwd(gr_ref, go_ref):
    groups = gr_ref.shape[0]
    q, k, v = [gr_ref[:, a].reshape(groups * 32, LANES) for a in range(3)]
    lane = iota2((groups * 32, LANES), 1)
    total = None
    for e in range(2):
        mask = lane_mask(LANES, HEAD * e, HEAD * (e + 1))
        out, parts = attend(q * lane_mask(LANES, HEAD * e, HEAD * (e + 1), PAIR), k, v * mask)
        for index, part in enumerate(parts):
            out = jnp.where(lane == PAIR + 2 * index + e, part, out)
        total = out if total is None else total + out
    go_ref[...] = total.astype(BF).reshape(groups, 32, LANES)


def slide_members(sr_ref):
    sources = sr_ref.shape[0]
    wide = sr_ref[...].astype(F32)
    return [wide[:, a : a + 8].reshape(sources * 8, LANES).astype(BF) for a in (0, 8)]


def slide_fwd(sr_ref, so_ref):
    sources = sr_ref.shape[0]
    qc, kv = slide_members(sr_ref)
    out, parts = attend(
        qc * lane_mask(LANES, 0, HEAD + 1), kv, kv * lane_mask(LANES, UPPER, UPPER + HEAD)
    )
    lane = iota2((sources * 8, LANES), 1)
    for index, part in enumerate(parts):
        out = jnp.where(lane == index, part, out)
    so_ref[...] = out.reshape(sources, 8, LANES).astype(BF)


def head_spread(transposed):
    shape = (HEADS * HEAD, LANES) if transposed else (LANES, HEADS * HEAD)
    head, col = (iota2(shape, 1), iota2(shape, 0)) if transposed else (iota2(shape, 0), iota2(shape, 1))
    return ((col >= head * HEAD) & (col < head * HEAD + HEAD)).astype(F32).astype(BF)


def combine_kernel(
    xp_ref, on_ref, ln_ref, go_ref, so_ref, att_ref, plane_t_ref, g2_ref, s2_ref, acc_ref
):
    lane32 = iota2((32, LANES), 1)
    lane8 = iota2((8, LANES), 1)
    near = ln_ref[...]
    group_rows, slide_rows = [], [None] * HEADS
    for o in range(4):
        pieces = []
        for p in (2 * o, 2 * o + 1):
            block = go_ref[p].astype(F32)
            block = block + pltpu.roll(block, LANES - 2, 1) + pltpu.roll(block, LANES - 4, 1)
            moved = pltpu.roll(block, LANES - PAIR + 2 * p, 1)
            keep = (lane32 >= 2 * p) & (lane32 < 2 * p + 2)
            pieces.append(jnp.where(keep, moved, NEGATIVE_FILL))
        group_rows.append(jnp.maximum(pieces[0], pieces[1]))
    for r in range(HEADS):
        block = so_ref[r].astype(F32)
        block = block + pltpu.roll(block, LANES - 1, 1) + pltpu.roll(block, LANES - 2, 1)
        moved = pltpu.roll(block, r, 1) if r else block
        slide_rows[slide_row(r) // 8] = jnp.where(lane8 == r, moved, NEGATIVE_FILL)
    group = jnp.concatenate(group_rows, axis=0)
    slide = jnp.concatenate(slide_rows, axis=0)
    best = jnp.maximum(jnp.maximum(near, group), slide)
    near_w, group_w, slide_w = jnp.exp(near - best), jnp.exp(group - best), jnp.exp(slide - best)
    den = near_w + group_w + slide_w
    lse = best + jnp.log(den)
    spread = head_spread(False)
    acc_ref[0:2] = jnp.zeros((2,) + acc_ref.shape[1:], F32)
    for p in range(HEADS // 2):
        row = p // 2 * 32
        start, width, shift = window(PAIR * p, PAIR)
        acc_ref[0, row : row + 32, start : start + width] += mm(
            go_ref[p], shift_out(width, shift, PAIR)
        )
    for r in range(HEADS):
        row = slide_row(r)
        start, width, shift = window(HEAD * r, HEAD)
        acc_ref[1, row : row + 8, start : start + width] += mm(
            so_ref[r], shift_out(width, shift, HEAD, UPPER)
        )
    attended = (
        on_ref[...] * split_mm(near_w / den, spread)
        + acc_ref[0] * split_mm(group_w / den, spread)
        + acc_ref[1] * split_mm(slide_w / den, spread)
    ).astype(BF)
    att_ref[...] = mm(permute_matrix(True), attended).astype(BF)
    product = xp_ref[3].astype(F32) * attended.astype(F32)
    delta = split_mm(product, head_spread(True))
    lane = iota2((LANES, LANES), 1)
    plane = jnp.where(lane < HEADS, lse, pltpu.roll(delta, HEADS, 1))
    turned = plane.T
    plane_t_ref[...] = turned
    turned = turned[: 2 * HEADS]
    g2_ref[...] = jnp.zeros_like(g2_ref)
    s2_ref[...] = jnp.zeros_like(s2_ref)
    for p in range(HEADS // 2):
        moved = pltpu.roll(turned, LANES - p // 2 * 32, 1) if p >= 2 else turned
        g2_ref[p, 0:2] = moved[2 * p : 2 * p + 2]
        g2_ref[p, 2:4] = moved[HEADS + 2 * p : HEADS + 2 * p + 2]
    for r in range(HEADS):
        row = slide_row(r)
        moved = pltpu.roll(turned, LANES - row, 1) if row else turned
        s2_ref[r, 0:1] = moved[r : r + 1]
        s2_ref[r, 1:2] = moved[HEADS + r : HEADS + r + 1]


def near_bwd_kernel(len_ref, xp_ref, plane_t_ref, grads_ref):
    bias = key_bias(len_ref, 0)
    tiles = HEADS * HEAD // LANES
    totals = [[None] * tiles for _ in range(3)]
    for h in range(HEADS):
        start, width, shift = window(HEAD * h, HEAD)
        mask = lane_mask(width, shift, shift + HEAD)
        qm, km, vm, cm = [xp_ref[a, :, start : start + width] * mask for a in range(4)]
        s = mm_t(km, qm) * SCALE + bias
        weights = jnp.exp(s - plane_t_ref[h : h + 1, :])
        dp = mm_t(vm, cm)
        ds = (weights * (dp - plane_t_ref[HEADS + h : HEADS + h + 1, :])).astype(BF)
        results = (t_mm(ds, km), mm(ds, qm), mm(weights.astype(BF), cm))
        for index, value in enumerate(results):
            for part in range(width // LANES):
                t = start // LANES + part
                piece = value[:, part * LANES : (part + 1) * LANES]
                old = totals[index][t]
                totals[index][t] = piece if old is None else old + piece
    for index in range(3):
        for t in range(tiles):
            value = totals[index][t]
            grads_ref[index, :, t * LANES : (t + 1) * LANES] = value * SCALE if index < 2 else value


def join_rows(ref, span):
    sources, per = ref.shape[0], LANES // span
    lane = iota2((8, LANES), 1)
    rows = []
    for first in range(0, sources, per):
        row = ref[first]
        for index in range(1, per):
            moved = pltpu.roll(ref[first + index], index * span, 1)
            row = jnp.where(lane >= index * span, moved, row)
        rows.append(row)
    return jnp.concatenate(rows, axis=1)


def score_grads(q, k, v, c, lse, delta):
    weights = jnp.exp(mm_t(k, q) * SCALE - lse)
    return weights.astype(BF), (weights * (mm_t(v, c) - delta)).astype(BF)


def group_bwd(gr_ref, gc_ref, gp_ref, go_ref):
    groups = gr_ref.shape[0]
    q, k, v = [gr_ref[:, a].reshape(groups * 32, LANES) for a in range(3)]
    c = gc_ref[...].reshape(groups * 32, LANES)
    plane = join_rows(gp_ref, 32)
    sums = [None] * 3
    for e in range(2):
        mask = lane_mask(LANES, HEAD * e, HEAD * (e + 1))
        q_flag = q * lane_mask(LANES, HEAD * e, HEAD * (e + 1), PAIR)
        cm = c * mask
        weights, ds = score_grads(q_flag, k, v, cm, plane[e : e + 1], plane[2 + e : 3 + e])
        parts = (t_mm(ds, k * mask), mm(ds, q * mask), mm(weights, cm))
        sums = [part if old is None else old + part for old, part in zip(sums, parts)]
    for a, grad in enumerate((sums[0] * SCALE, sums[1] * SCALE, sums[2])):
        go_ref[:, a] = grad.reshape(groups, 32, LANES).astype(BF)


def slide_bwd(sr_ref, sp_ref, so_ref):
    sources = sr_ref.shape[0]
    qc, kv = slide_members(sr_ref)
    plane = join_rows(sp_ref, 8)
    low = lane_mask(LANES, 0, HEAD)
    cm = qc * lane_mask(LANES, UPPER, UPPER + HEAD)
    weights, ds = score_grads(
        qc * lane_mask(LANES, 0, HEAD + 1), kv, kv, cm, plane[0:1], plane[1:2]
    )
    query = t_mm(ds, kv * low) * SCALE
    key_value = mm(ds, qc * low) * SCALE + mm(weights, cm)
    stacked = [grad.reshape(sources, 8, LANES) for grad in (query, key_value)]
    so_ref[...] = jnp.concatenate(stacked, axis=1).astype(BF)


def final_kernel(near_ref, go_ref, so_ref, dq_ref, dk_ref, dv_ref, acc_ref):
    acc_ref[...] = near_ref[...]
    for p in range(HEADS // 2):
        row = p // 2 * 32
        start, width, shift = window(PAIR * p, PAIR)
        moved = mm(go_ref[p].reshape(96, LANES), shift_out(width, shift, PAIR))
        for a in range(3):
            acc_ref[a, row : row + 32, start : start + width] += moved[32 * a : 32 * a + 32]
    for r in range(HEADS):
        row = slide_row(r)
        start, width, shift = window(HEAD * r, HEAD)
        moved = mm(so_ref[r], shift_out(width, shift, HEAD))
        upper = mm(so_ref[r], shift_out(width, shift, HEAD, UPPER))
        for a, piece in enumerate((moved[0:8], moved[8:16], upper[8:16])):
            acc_ref[a, row : row + 8, start : start + width] += piece
    back = permute_matrix(True)
    for a, ref in enumerate((dq_ref, dk_ref, dv_ref)):
        ref[...] = mm(back, acc_ref[a].astype(BF)).astype(BF)


MESH = pl.DeviceIdType.MESH


def remote(src, dst, send_sem, recv_sem, outer, inner):
    return pltpu.make_async_remote_copy(
        src_ref=src,
        dst_ref=dst,
        send_sem=send_sem,
        recv_sem=recv_sem,
        device_id=(outer, inner),
        device_id_type=MESH,
    )


class Group:
    def __init__(self, inner, src, dst, send_sem, recv_sem):
        self.inner, self.src, self.dst = inner, src, dst
        self.send_sem, self.recv_sem = send_sem, recv_sem

    def copy(self, step):
        me = lax.axis_index("inner")
        peer = wrapped(me + step, self.inner)
        return remote(
            self.src.at[peer],
            self.dst.at[me],
            self.send_sem.at[step],
            self.recv_sem.at[step],
            lax.axis_index("outer"),
            peer,
        )

    def start(self):
        @pl.loop(1, self.inner)
        def _(step):
            self.copy(step).start()

        me = lax.axis_index("inner")
        self.dst[me] = self.src[me]

    def wait_recv(self):
        @pl.loop(1, self.inner)
        def _(step):
            self.copy(step).wait_recv()

    def wait_send(self):
        @pl.loop(1, self.inner)
        def _(step):
            self.copy(step).wait_send()


def wrapped(value, count):
    return jnp.where(value >= count, value - count, value)


def owner_of(head, inner):
    high = jnp.where(head >= inner, 1, 0)
    return 2 * high, head - inner * high


class ToOwner:
    def __init__(self, inner, devices, src, dst, send_sem, recv_sem):
        self.inner, self.devices, self.src, self.dst = inner, devices, src, dst
        self.send_sem, self.recv_sem = send_sem, recv_sem

    def place(self):
        return lax.axis_index("outer"), lax.axis_index("inner")

    def copy(self, head):
        outer, inner = self.place()
        to_outer, to_inner = owner_of(head, self.inner)
        me = outer * self.inner + inner
        return remote(
            self.src.at[head],
            self.dst.at[me],
            self.send_sem.at[head],
            self.recv_sem.at[me],
            to_outer,
            to_inner,
        )

    def each(self, other, own):
        outer, inner = self.place()
        me = outer * self.inner + inner

        first = wrapped(me, HEADS)

        @pl.loop(0, HEADS)
        def _(step):
            head = wrapped(step + first, HEADS)
            to_outer, to_inner = owner_of(head, self.inner)
            at_home = (to_outer * self.inner + to_inner) == me

            @pl.when(jnp.logical_not(at_home))
            def _():
                other(head)

            if own is not None:

                @pl.when(at_home)
                def _():
                    own(head, me)

    def start(self):
        def keep(head, me):
            self.dst[me] = self.src[head]

        self.each(lambda head: self.copy(head).start(), keep)

    def wait_recv(self):
        outer, inner = self.place()
        me = outer * self.inner + inner

        for source_outer in range(self.devices // self.inner):

            @pl.loop(0, self.inner)
            def _(source_inner):
                source = source_outer * self.inner + source_inner

                @pl.when(source != me)
                def _():
                    remote(
                        self.src.at[0],
                        self.dst.at[source],
                        self.send_sem.at[0],
                        self.recv_sem.at[source],
                        source_outer,
                        source_inner,
                    ).wait_recv()

    def wait_send(self):
        self.each(lambda head: self.copy(head).wait_send(), None)


def others(inner, devices, act):
    mine, me = lax.axis_index("outer"), lax.axis_index("inner")
    count = devices // inner
    for step in range(count):
        to_outer = wrapped(mine + step, count)

        @pl.loop(1 if step == 0 else 0, inner)
        def _(place):
            act(to_outer, wrapped(me + place, inner))


class FromOwner:
    def __init__(self, inner, devices, src, dst, send_sem, recv_sem):
        self.inner, self.devices, self.src, self.dst = inner, devices, src, dst
        self.send_sem, self.recv_sem = send_sem, recv_sem

    def copy(self, to_outer, to_inner):
        target = to_outer * self.inner + to_inner
        outer, inner = lax.axis_index("outer"), lax.axis_index("inner")
        head = outer // 2 * self.inner + inner
        return remote(
            self.src.at[target],
            self.dst.at[head],
            self.send_sem.at[target],
            self.recv_sem.at[head],
            to_outer,
            to_inner,
        )

    def start(self):
        outer, inner = lax.axis_index("outer"), lax.axis_index("inner")
        me = outer * self.inner + inner
        others(self.inner, self.devices, lambda *place: self.copy(*place).start())
        self.dst[outer // 2 * self.inner + inner] = self.src[me]

    def wait_recv(self):
        me = lax.axis_index("outer") * self.inner + lax.axis_index("inner")

        @pl.loop(0, HEADS)
        def _(head):
            from_outer, from_inner = owner_of(head, self.inner)

            @pl.when((from_outer * self.inner + from_inner) != me)
            def _():
                remote(
                    self.src.at[0],
                    self.dst.at[head],
                    self.send_sem.at[0],
                    self.recv_sem.at[head],
                    from_outer,
                    from_inner,
                ).wait_recv()

    def wait_send(self):
        others(self.inner, self.devices, lambda *place: self.copy(*place).wait_send())


def whole_kernel(inner, devices, len_ref, q_ref, k_ref, v_ref, c_ref, att_ref, dq_ref, dk_ref, dv_ref, *scratch):
    (xp, near_out, near_lse, plane_t, near_grads, acc) = scratch[:6]
    staged, gcs, gcr, load_sem = scratch[26:]
    (g1s, g1r, s1s, s1r, g2s, g2r, s2s, s2r, g3s, g3r, s3s, s3r, g4s, g4r, s4s, s4r) = scratch[6:22]
    group_send, group_recv, slide_send, slide_recv = scratch[22:26]
    outer, place = lax.axis_index("outer"), lax.axis_index("inner")
    is_owner = lax.rem(outer, 2) == 0

    def group_exchange(phase, src, dst):
        return Group(inner, src, dst, group_send.at[phase], group_recv.at[phase])

    def slide_exchange(kind, phase, src, dst):
        return kind(inner, devices, src, dst, slide_send.at[phase], slide_recv.at[phase])

    group1, slide1 = group_exchange(0, g1s, g1r), slide_exchange(ToOwner, 0, s1s, s1r)
    group2, slide2 = group_exchange(1, g2s, g2r), slide_exchange(FromOwner, 1, s2s, s2r)
    group3, slide3 = group_exchange(2, g3s, g3r), slide_exchange(ToOwner, 2, s3s, s3r)
    group4, slide4 = group_exchange(3, g4s, g4r), slide_exchange(FromOwner, 3, s4s, s4r)

    group_c = group_exchange(4, gcs, gcr)
    barrier = pltpu.get_barrier_semaphore()

    def greet(*other):
        pl.semaphore_signal(barrier, inc=1, device_id=other, device_id_type=MESH)

    loads = [
        pltpu.make_async_copy(ref, staged.at[a], load_sem.at[a])
        for a, ref in enumerate((q_ref, k_ref, v_ref, c_ref))
    ]
    for load in loads:
        load.start()
    others(inner, devices, greet)
    for load in loads:
        load.wait()
    prep_kernel(len_ref, *[staged.at[a] for a in range(4)], xp, g1s, gcs, s1s)
    pl.semaphore_wait(barrier, devices - 1)
    slide1.start()
    group1.start()
    group_c.start()
    near_fwd_kernel(len_ref, xp, near_out, near_lse)

    @pl.when(is_owner)
    def _():
        slide1.wait_recv()
        slide_fwd(s1r, s2s)
        slide2.start()

    group1.wait_recv()
    group_fwd(g1r, g2s)
    group2.start()
    group2.wait_recv()
    slide2.wait_recv()
    combine_kernel(xp, near_out, near_lse, g2r, s2r, att_ref, plane_t, g3s, s3s, acc)
    slide3.start()
    group3.start()
    near_bwd_kernel(len_ref, xp, plane_t, near_grads)

    @pl.when(is_owner)
    def _():
        slide3.wait_recv()
        slide_bwd(s1r, s3r, s4s)
        slide4.start()

    group_c.wait_recv()
    group3.wait_recv()
    group_bwd(g1r, gcr, g3r, g4s)
    group4.start()
    group4.wait_recv()
    slide4.wait_recv()
    final_kernel(near_grads, g4r, s4r, dq_ref, dk_ref, dv_ref, acc)
    for sent in (group1, slide1, group_c, group2, group3, slide3, group4):
        sent.wait_send()

    @pl.when(is_owner)
    def _():
        slide2.wait_send()
        slide4.wait_send()


def fast_local(inner, devices, *args):
    row_lengths, tiles_in = args[4], args[:4]
    tiles, width = tiles_in[0].shape
    vmem = pl.BlockSpec(memory_space=pltpu.VMEM)

    def both(count, back, shape, dtype):
        return [pltpu.VMEM((count,) + shape, dtype), pltpu.VMEM((back,) + shape, dtype)]

    scratch = [
        pltpu.VMEM((4, tiles, width), BF),
        pltpu.VMEM((tiles, width), F32),
        pltpu.VMEM((tiles, LANES), F32),
        pltpu.VMEM((LANES, tiles), F32),
        pltpu.VMEM((3, tiles, width), F32),
        pltpu.VMEM((3, tiles, width), F32),
    ]
    scratch += both(inner, inner, (3, 32, LANES), BF) + both(HEADS, devices, (16, LANES), BF)
    scratch += both(inner, inner, (32, LANES), BF) + both(devices, HEADS, (8, LANES), BF)
    scratch += both(inner, inner, (8, LANES), F32) + both(HEADS, devices, (8, LANES), F32)
    scratch += both(inner, inner, (3, 32, LANES), BF) + both(devices, HEADS, (16, LANES), BF)
    scratch += [pltpu.SemaphoreType.DMA((5, inner))] * 2 + [pltpu.SemaphoreType.DMA((4, devices))] * 2
    scratch += [pltpu.VMEM((4, tiles, width), BF)] + both(inner, inner, (32, LANES), BF)
    scratch += [pltpu.SemaphoreType.DMA((4,))]
    return tuple(
        pl.pallas_call(
            lambda *refs: whole_kernel(inner, devices, *refs),
            out_shape=[jax.ShapeDtypeStruct((tiles, width), BF)] * 4,
            in_specs=[pl.BlockSpec(memory_space=pltpu.SMEM)] + [pl.BlockSpec(memory_space=pltpu.HBM)] * 4,
            out_specs=[vmem] * 4,
            scratch_shapes=scratch,
            compiler_params=pltpu.CompilerParams(
                collective_id=0, has_side_effects=True, vmem_limit_bytes=48 * 1024 * 1024
            ),
        )(row_lengths, *tiles_in)
    )


def solution(mesh):
    in_specs = (P(("outer", "inner"), None),) * 4 + (P(("outer", "inner")),)
    out_specs = (P(("outer", "inner"), None),) * 4
    inner = mesh.shape["inner"]
    devices = inner * mesh.shape["outer"]

    def step(*args):
        owners = 2 * inner == HEADS and devices == 2 * HEADS
        if owners and args[0].shape == (LANES, HEADS * HEAD):
            return fast_local(inner, devices, *args)
        return local(*args)

    return jax.shard_map(step, mesh=mesh, in_specs=in_specs, out_specs=out_specs, check_vma=False)
```

```python
import jax
import jax.numpy as jnp
import numpy as np
from jax import lax
from jax.experimental import pallas as pl
from jax.experimental.pallas import tpu as pltpu
from jax.sharding import PartitionSpec as P

HEADS = 16
HEAD = 48
ROW = 32
STRIDE_GROUP = 4
STRIDE_SLIDE = 16


NEGATIVE_FILL = -1e30
heads_at_once = 4


def as_sent(value):

    def short(part):
        return part.astype(jnp.bfloat16) if part.dtype == jnp.float32 else part

    return jax.tree.map(short, value)


def head_ranges(head_total):
    step_size = min(head_total, heads_at_once)
    return [(first_head, first_head + step_size) for first_head in range(0, head_total, step_size)]


def scores_of(query_block, key_block, score_scale):
    return (
        jnp.einsum("hdq,hdk->hqk", query_block, key_block, preferred_element_type=jnp.float32)
        * score_scale
    )


def branch_stats(query_heads, key_heads, value_heads, key_valid, score_scale):
    peak_list, total_list, sum_list = ([], [], [])
    for first_head, last_head in head_ranges(query_heads.shape[0]):
        raw_scores = scores_of(
            query_heads[first_head:last_head], key_heads[first_head:last_head], score_scale
        )
        key_keep = key_valid[first_head:last_head][:, None, :]
        masked = jnp.where(key_keep, raw_scores, NEGATIVE_FILL)
        row_peak = jnp.max(masked, axis=2)
        weights = jnp.where(key_keep, jnp.exp(masked - row_peak[:, :, None]), 0.0)
        peak_list.append(row_peak)
        total_list.append(jnp.sum(weights, axis=2))
        sum_list.append(
            jnp.einsum(
                "hqk,hdk->hdq",
                weights.astype(jnp.bfloat16),
                value_heads[first_head:last_head],
                preferred_element_type=jnp.float32,
            )
        )
    return (
        jnp.concatenate(peak_list, axis=0),
        jnp.concatenate(total_list, axis=0),
        jnp.concatenate(sum_list, axis=0),
    )


def branch_grads(
    query_heads,
    key_heads,
    value_heads,
    cotan_heads,
    log_norm,
    out_dot,
    key_valid,
    score_scale,
    want_query,
    want_keys,
):
    query_list, key_list, value_list = ([], [], [])
    for first_head, last_head in head_ranges(query_heads.shape[0]):
        query_block = query_heads[first_head:last_head]
        key_block = key_heads[first_head:last_head]
        cotan_block = cotan_heads[first_head:last_head]
        raw_scores = scores_of(query_block, key_block, score_scale)
        key_keep = key_valid[first_head:last_head][:, None, :]
        weights = jnp.where(
            key_keep, jnp.exp(raw_scores - log_norm[first_head:last_head][:, :, None]), 0.0
        )
        weight_grads = jnp.einsum(
            "hdq,hdk->hqk",
            cotan_block,
            value_heads[first_head:last_head],
            preferred_element_type=jnp.float32,
        )
        low_grads = (weights * (weight_grads - out_dot[first_head:last_head][:, :, None])).astype(
            jnp.bfloat16
        )
        if want_query:
            query_list.append(
                score_scale
                * jnp.einsum(
                    "hqk,hdk->hdq", low_grads, key_block, preferred_element_type=jnp.float32
                )
            )
        if want_keys:
            key_list.append(
                score_scale
                * jnp.einsum(
                    "hqk,hdq->hdk", low_grads, query_block, preferred_element_type=jnp.float32
                )
            )
            value_list.append(
                jnp.einsum(
                    "hqk,hdq->hdk",
                    weights.astype(jnp.bfloat16),
                    cotan_block,
                    preferred_element_type=jnp.float32,
                )
            )
    query_part = jnp.concatenate(query_list, axis=0) if want_query else None
    key_part = jnp.concatenate(key_list, axis=0) if want_keys else None
    value_part = jnp.concatenate(value_list, axis=0) if want_keys else None
    return (query_part, key_part, value_part)


def head_offsets(head_total, stride):
    return np.arange(head_total) * stride // head_total


def select_rows(array_in, stride):
    head_total = array_in.shape[0]
    offsets = head_offsets(head_total, stride)
    folded = array_in.reshape(array_in.shape[:-1] + (array_in.shape[-1] // stride, stride))
    return jnp.stack(
        [folded[head_index, ..., int(offsets[head_index])] for head_index in range(head_total)]
    )


def spread_rows(array_in, stride, fill_value):
    head_total = array_in.shape[0]
    chosen = np.arange(stride)[None, :] == head_offsets(head_total, stride)[:, None]
    chosen = chosen.reshape((head_total,) + (1,) * (array_in.ndim - 1) + (stride,))
    full = jnp.where(chosen, array_in[..., None], fill_value)
    return full.reshape(array_in.shape[:-1] + (array_in.shape[-1] * stride,))


def to_heads(flat_in):
    return jnp.transpose(flat_in.reshape(flat_in.shape[0], HEADS, -1), (1, 2, 0))


def to_flat(heads_in):
    return jnp.transpose(heads_in, (2, 0, 1)).reshape(heads_in.shape[2], -1)


def local(query_tiles, key_tiles, value_tiles, cotangent, row_lengths):
    tile_count = query_tiles.shape[0]
    score_scale = HEAD ** (-0.5)
    query_heads = to_heads(query_tiles)
    key_heads = to_heads(key_tiles)
    value_heads = to_heads(value_tiles)
    cotan_heads = to_heads(cotangent)
    tile_slot = jnp.arange(tile_count, dtype=jnp.int32)
    tile_valid = tile_slot % ROW < jnp.repeat(row_lengths, ROW, total_repeat_length=tile_count)
    valid_heads = jnp.broadcast_to(tile_valid[None, :], (HEADS, tile_count))
    group_query = select_rows(query_heads, STRIDE_GROUP)
    group_key = select_rows(key_heads, STRIDE_GROUP)
    group_value = select_rows(value_heads, STRIDE_GROUP)
    group_cotan = select_rows(cotan_heads, STRIDE_GROUP)
    group_valid = select_rows(valid_heads, STRIDE_GROUP)
    group_flag = group_valid.astype(jnp.bfloat16)[:, None, :]
    slide_query = select_rows(query_heads, STRIDE_SLIDE)
    slide_key = select_rows(key_heads, STRIDE_SLIDE)
    slide_value = select_rows(value_heads, STRIDE_SLIDE)
    slide_flag = select_rows(valid_heads, STRIDE_SLIDE).astype(jnp.bfloat16)[:, None, :]
    owned_query, owned_key, owned_value, owned_flag = (
        lax.all_to_all(slide_query, "outer", split_axis=0, concat_axis=2, tiled=True),
        lax.all_to_all(slide_key, "outer", split_axis=0, concat_axis=2, tiled=True),
        lax.all_to_all(slide_value, "outer", split_axis=0, concat_axis=2, tiled=True),
        lax.all_to_all(slide_flag, "outer", split_axis=0, concat_axis=2, tiled=True),
    )
    got_group = (
        lax.all_gather(group_key, "inner", axis=2, tiled=True),
        lax.all_gather(group_value, "inner", axis=2, tiled=True),
        lax.all_gather(group_flag, "inner", axis=2, tiled=True),
    )
    got_slide = (
        lax.all_gather(owned_key, "inner", axis=2, tiled=True),
        lax.all_gather(owned_value, "inner", axis=2, tiled=True),
        lax.all_gather(owned_flag, "inner", axis=2, tiled=True),
    )
    near_peak, near_total, near_sum = branch_stats(
        query_heads, key_heads, value_heads, valid_heads, score_scale
    )
    remote_group_key = got_group[0]
    remote_group_value = got_group[1]
    remote_group_valid = got_group[2][:, 0, :] > 0.5
    group_peak, group_total, group_sum = branch_stats(
        group_query, remote_group_key, remote_group_value, remote_group_valid, score_scale
    )
    slide_all_key = got_slide[0]
    slide_all_value = got_slide[1]
    slide_all_valid = got_slide[2][:, 0, :] > 0.5
    owner_peak, owner_total, owner_sum = branch_stats(
        owned_query, slide_all_key, slide_all_value, slide_all_valid, score_scale
    )
    slide_peak, slide_total, slide_sum = (
        lax.all_to_all(owner_peak[:, None, :], "outer", split_axis=2, concat_axis=0, tiled=True),
        lax.all_to_all(owner_total[:, None, :], "outer", split_axis=2, concat_axis=0, tiled=True),
        lax.all_to_all(owner_sum, "outer", split_axis=2, concat_axis=0, tiled=True),
    )
    slide_peak = slide_peak[:, 0, :]
    slide_total = slide_total[:, 0, :]
    group_peak_full = spread_rows(group_peak, STRIDE_GROUP, NEGATIVE_FILL)
    slide_peak_full = spread_rows(slide_peak, STRIDE_SLIDE, NEGATIVE_FILL)
    best_peak = jnp.maximum(jnp.maximum(near_peak, group_peak_full), slide_peak_full)
    near_weight = jnp.exp(near_peak - best_peak)
    group_weight = jnp.exp(group_peak_full - best_peak)
    slide_weight = jnp.exp(slide_peak_full - best_peak)
    denominator = (
        near_total * near_weight
        + spread_rows(group_total, STRIDE_GROUP, 0.0) * group_weight
        + spread_rows(slide_total, STRIDE_SLIDE, 0.0) * slide_weight
    )
    numerator = (
        near_sum * near_weight[:, None, :]
        + spread_rows(group_sum, STRIDE_GROUP, 0.0) * group_weight[:, None, :]
        + spread_rows(slide_sum, STRIDE_SLIDE, 0.0) * slide_weight[:, None, :]
    )
    attended = (numerator / denominator[:, None, :]).astype(jnp.bfloat16)
    log_norm = best_peak + jnp.log(denominator)
    out_dot = jnp.sum(cotan_heads.astype(jnp.float32) * attended.astype(jnp.float32), axis=1)
    near_query, near_key, near_value = branch_grads(
        query_heads,
        key_heads,
        value_heads,
        cotan_heads,
        log_norm,
        out_dot,
        valid_heads,
        score_scale,
        True,
        True,
    )
    group_lse = select_rows(log_norm, STRIDE_GROUP)
    group_dot = select_rows(out_dot, STRIDE_GROUP)
    group_query_grad = branch_grads(
        group_query,
        remote_group_key,
        remote_group_value,
        group_cotan,
        group_lse,
        group_dot,
        remote_group_valid,
        score_scale,
        True,
        False,
    )[0]
    got_group_rows = (
        lax.all_gather(group_query, "inner", axis=2, tiled=True),
        lax.all_gather(group_cotan, "inner", axis=2, tiled=True),
    )
    got_group_stats = (
        lax.all_gather(group_lse, "inner", axis=1, tiled=True),
        lax.all_gather(group_dot, "inner", axis=1, tiled=True),
    )
    unused_group, group_key_grad, group_value_grad = branch_grads(
        got_group_rows[0],
        group_key,
        group_value,
        got_group_rows[1],
        got_group_stats[0],
        got_group_stats[1],
        group_valid,
        score_scale,
        False,
        True,
    )
    slide_cotan = select_rows(cotan_heads, STRIDE_SLIDE)
    slide_lse = select_rows(log_norm, STRIDE_SLIDE)
    slide_dot = select_rows(out_dot, STRIDE_SLIDE)
    owned_cotan = lax.all_to_all(slide_cotan, "outer", split_axis=0, concat_axis=2, tiled=True)
    owned_lse, owned_dot = (
        lax.all_to_all(slide_lse, "outer", split_axis=0, concat_axis=1, tiled=True),
        lax.all_to_all(slide_dot, "outer", split_axis=0, concat_axis=1, tiled=True),
    )
    owned_query_grad, partial_key, partial_value = branch_grads(
        owned_query,
        slide_all_key,
        slide_all_value,
        owned_cotan,
        owned_lse,
        owned_dot,
        slide_all_valid,
        score_scale,
        True,
        True,
    )
    owned_key_grad, owned_value_grad = (
        lax.psum_scatter(
            partial_key.astype(jnp.bfloat16), "inner", scatter_dimension=2, tiled=True
        ).astype(jnp.float32),
        lax.psum_scatter(
            partial_value.astype(jnp.bfloat16), "inner", scatter_dimension=2, tiled=True
        ).astype(jnp.float32),
    )
    slide_query_grad, slide_key_grad, slide_value_grad = (
        lax.all_to_all(
            as_sent(owned_query_grad), "outer", split_axis=2, concat_axis=0, tiled=True
        ).astype(owned_query_grad.dtype),
        lax.all_to_all(
            owned_key_grad.astype(jnp.bfloat16), "outer", split_axis=2, concat_axis=0, tiled=True
        ).astype(owned_key_grad.dtype),
        lax.all_to_all(
            owned_value_grad.astype(jnp.bfloat16), "outer", split_axis=2, concat_axis=0, tiled=True
        ).astype(owned_value_grad.dtype),
    )
    query_grad = (
        near_query
        + spread_rows(group_query_grad, STRIDE_GROUP, 0.0)
        + spread_rows(slide_query_grad, STRIDE_SLIDE, 0.0)
    )
    key_grad = (
        near_key
        + spread_rows(group_key_grad, STRIDE_GROUP, 0.0)
        + spread_rows(slide_key_grad, STRIDE_SLIDE, 0.0)
    )
    value_grad = (
        near_value
        + spread_rows(group_value_grad, STRIDE_GROUP, 0.0)
        + spread_rows(slide_value_grad, STRIDE_SLIDE, 0.0)
    )
    return (
        to_flat(attended),
        to_flat(query_grad.astype(jnp.bfloat16)),
        to_flat(key_grad.astype(jnp.bfloat16)),
        to_flat(value_grad.astype(jnp.bfloat16)),
    )


BF = jnp.bfloat16
F32 = jnp.float32
LANES = 128
SCALE = HEAD ** (-0.5)
PAIR = 2 * HEAD
UPPER = LANES // 2


def window(first_col, width):
    start = first_col // LANES * LANES
    shift = first_col - start
    return start, (LANES if shift + width <= LANES else 2 * LANES), shift


def iota2(shape, axis):
    return lax.broadcasted_iota(jnp.int32, shape, axis)


def original_tile(j):
    return (j & 7) * 16 + ((j >> 3) & 3) * 4 + (j >> 5)


def permute_matrix(inverse):
    shape = (LANES, LANES)
    j, i = (iota2(shape, 1), iota2(shape, 0)) if inverse else (iota2(shape, 0), iota2(shape, 1))
    return (original_tile(j) == i).astype(F32).astype(BF)


def key_bias(len_ref, axis):
    tile = original_tile(iota2((LANES, LANES), axis))
    row = tile >> 5
    length = jnp.full((LANES, LANES), len_ref[0], jnp.int32)
    for index in range(1, 4):
        length = jnp.where(row == index, len_ref[index], length)
    return jnp.where((tile & 31) < length, 0.0, NEGATIVE_FILL).astype(F32)


def shift_in(width, shift, kept, base=0):
    row, col = iota2((width, LANES), 0), iota2((width, LANES), 1)
    return ((row - shift + base == col) & (col >= base) & (col < base + kept)).astype(F32).astype(BF)


def shift_out(width, shift, kept, base=0):
    row, col = iota2((LANES, width), 0), iota2((LANES, width), 1)
    return ((col - shift + base == row) & (row >= base) & (row < base + kept)).astype(F32).astype(BF)


def lane_mask(width, first, last, extra=-1):
    lane = iota2((1, width), 1)
    keep = (lane >= first) & (lane < last)
    if extra >= 0:
        keep = keep | (lane == extra)
    return keep.astype(F32).astype(BF)


def mm(a, b):
    return jnp.dot(a, b, preferred_element_type=F32)


def mm_t(a, b):
    return lax.dot_general(a, b, (((1,), (1,)), ((), ())), preferred_element_type=F32)


def t_mm(a, b):
    return lax.dot_general(a, b, (((0,), (0,)), ((), ())), preferred_element_type=F32)


def slide_row(r):
    return (r % 4) * 32 + (r // 4) * 8


def split_mm(a, onehot):
    high = a.astype(BF)
    low = (a - high.astype(F32)).astype(BF)
    return mm(high, onehot) + mm(low, onehot)


def prep_kernel(len_ref, q_ref, k_ref, v_ref, c_ref, xp_ref, gs_ref, gc_ref, ss_ref):
    perm = permute_matrix(False)
    xs = []
    for index, ref in enumerate((q_ref, k_ref, v_ref, c_ref)):
        xs.append(mm(perm, ref[...]))
        xp_ref[index] = xs[-1].astype(BF)
    bias = key_bias(len_ref, 0)
    for p in range(HEADS // 2):
        row = p // 2 * 32
        start, width, shift = window(PAIR * p, PAIR)
        stacked = jnp.concatenate(
            [x[row : row + 32, start : start + width].astype(BF) for x in xs], axis=0
        )
        moved = mm(stacked, shift_in(width, shift, PAIR))
        flag = iota2((32, LANES), 1) == PAIR
        gs_ref[p, 0] = jnp.where(flag, 1.0, moved[0:32]).astype(BF)
        gs_ref[p, 1] = jnp.where(flag, bias[row : row + 32], moved[32:64]).astype(BF)
        gs_ref[p, 2] = moved[64:96].astype(BF)
        gc_ref[p] = moved[96:128].astype(BF)
    for r in range(HEADS):
        row = slide_row(r)
        start, width, shift = window(HEAD * r, HEAD)
        low, high = [
            jnp.concatenate(
                [xs[a][row : row + 8, start : start + width] for a in pair], axis=0
            ).astype(BF)
            for pair in ((0, 1), (3, 2))
        ]
        moved = mm(low, shift_in(width, shift, HEAD)) + mm(high, shift_in(width, shift, HEAD, UPPER))
        flags = jnp.concatenate([jnp.ones((8, LANES), F32), bias[row : row + 8]], axis=0)
        ss_ref[r // 8, r % 8] = jnp.where(iota2((16, LANES), 1) == HEAD, flags, moved).astype(BF)


def near_fwd_kernel(len_ref, xp_ref, o_ref, lse_ref):
    bias = key_bias(len_ref, 1)
    lane = iota2((LANES, LANES), 1)
    lse = jnp.full((LANES, LANES), NEGATIVE_FILL, F32)
    total = [None] * (HEADS * HEAD // LANES)
    for h in range(HEADS):
        start, width, shift = window(HEAD * h, HEAD)
        mask = lane_mask(width, shift, shift + HEAD)
        s = mm_t(xp_ref[0, :, start : start + width] * mask, xp_ref[1, :, start : start + width])
        s = s * SCALE + bias
        peak = jnp.max(s, axis=1, keepdims=True)
        e = jnp.exp(s - peak)
        norm = jnp.sum(e, axis=1, keepdims=True)
        o = mm(e.astype(BF), xp_ref[2, :, start : start + width] * mask) / norm
        lse = jnp.where(lane == h, peak + jnp.log(norm), lse)
        for part in range(width // LANES):
            t = start // LANES + part
            piece = o[:, part * LANES : (part + 1) * LANES]
            total[t] = piece if total[t] is None else total[t] + piece
    for t, value in enumerate(total):
        o_ref[:, t * LANES : (t + 1) * LANES] = value
    lse_ref[...] = lse


def three_parts(value):
    high = value.astype(BF).astype(F32)
    rest = value - high
    middle = rest.astype(BF).astype(F32)
    return high, middle, rest - middle


def attend(q, k, v):
    s = mm_t(q, k) * SCALE
    peak = jnp.max(s, axis=1, keepdims=True)
    weights = jnp.exp(s - peak)
    norm = jnp.sum(weights, axis=1, keepdims=True)
    return mm(weights.astype(BF), v) / norm, three_parts(peak + jnp.log(norm))


def group_fwd(gr_ref, go_ref):
    groups = gr_ref.shape[0]
    q, k, v = [gr_ref[:, a].reshape(groups * 32, LANES) for a in range(3)]
    lane = iota2((groups * 32, LANES), 1)
    total = None
    for e in range(2):
        mask = lane_mask(LANES, HEAD * e, HEAD * (e + 1))
        out, parts = attend(q * lane_mask(LANES, HEAD * e, HEAD * (e + 1), PAIR), k, v * mask)
        for index, part in enumerate(parts):
            out = jnp.where(lane == PAIR + 2 * index + e, part, out)
        total = out if total is None else total + out
    go_ref[...] = total.astype(BF).reshape(groups, 32, LANES)


def slide_members(sr_ref):
    sources = sr_ref.shape[0] * sr_ref.shape[1]
    wide = sr_ref[...].astype(F32).reshape(sources, 16, LANES)
    return [wide[:, a : a + 8].reshape(sources * 8, LANES).astype(BF) for a in (0, 8)]


def slide_fwd(sr_ref, so_ref):
    sources = sr_ref.shape[0] * sr_ref.shape[1]
    qc, kv = slide_members(sr_ref)
    out, parts = attend(
        qc * lane_mask(LANES, 0, HEAD + 1), kv, kv * lane_mask(LANES, UPPER, UPPER + HEAD)
    )
    lane = iota2((sources * 8, LANES), 1)
    for index, part in enumerate(parts):
        out = jnp.where(lane == index, part, out)
    so_ref[...] = out.reshape(so_ref.shape).astype(BF)


def head_spread(transposed):
    shape = (HEADS * HEAD, LANES) if transposed else (LANES, HEADS * HEAD)
    head, col = (iota2(shape, 1), iota2(shape, 0)) if transposed else (iota2(shape, 0), iota2(shape, 1))
    return ((col >= head * HEAD) & (col < head * HEAD + HEAD)).astype(F32).astype(BF)


def combine_kernel(
    xp_ref, on_ref, ln_ref, go_ref, so_ref, att_ref, plane_t_ref, g2_ref, s2_ref, acc_ref
):
    lane32 = iota2((32, LANES), 1)
    lane8 = iota2((8, LANES), 1)
    near = ln_ref[...]
    group_rows, slide_rows = [], [None] * HEADS
    for o in range(4):
        pieces = []
        for p in (2 * o, 2 * o + 1):
            block = go_ref[p].astype(F32)
            block = block + pltpu.roll(block, LANES - 2, 1) + pltpu.roll(block, LANES - 4, 1)
            moved = pltpu.roll(block, LANES - PAIR + 2 * p, 1)
            keep = (lane32 >= 2 * p) & (lane32 < 2 * p + 2)
            pieces.append(jnp.where(keep, moved, NEGATIVE_FILL))
        group_rows.append(jnp.maximum(pieces[0], pieces[1]))
    for r in range(HEADS):
        block = so_ref[r // 8, r % 8].astype(F32)
        block = block + pltpu.roll(block, LANES - 1, 1) + pltpu.roll(block, LANES - 2, 1)
        moved = pltpu.roll(block, r, 1) if r else block
        slide_rows[slide_row(r) // 8] = jnp.where(lane8 == r, moved, NEGATIVE_FILL)
    group = jnp.concatenate(group_rows, axis=0)
    slide = jnp.concatenate(slide_rows, axis=0)
    best = jnp.maximum(jnp.maximum(near, group), slide)
    near_w, group_w, slide_w = jnp.exp(near - best), jnp.exp(group - best), jnp.exp(slide - best)
    den = near_w + group_w + slide_w
    lse = best + jnp.log(den)
    spread = head_spread(False)
    acc_ref[0:2] = jnp.zeros((2,) + acc_ref.shape[1:], F32)
    for p in range(HEADS // 2):
        row = p // 2 * 32
        start, width, shift = window(PAIR * p, PAIR)
        acc_ref[0, row : row + 32, start : start + width] += mm(
            go_ref[p], shift_out(width, shift, PAIR)
        )
    for r in range(HEADS):
        row = slide_row(r)
        start, width, shift = window(HEAD * r, HEAD)
        acc_ref[1, row : row + 8, start : start + width] += mm(
            so_ref[r // 8, r % 8], shift_out(width, shift, HEAD, UPPER)
        )
    attended = (
        on_ref[...] * split_mm(near_w / den, spread)
        + acc_ref[0] * split_mm(group_w / den, spread)
        + acc_ref[1] * split_mm(slide_w / den, spread)
    ).astype(BF)
    att_ref[...] = mm(permute_matrix(True), attended).astype(BF)
    product = xp_ref[3].astype(F32) * attended.astype(F32)
    delta = split_mm(product, head_spread(True))
    lane = iota2((LANES, LANES), 1)
    plane = jnp.where(lane < HEADS, lse, pltpu.roll(delta, HEADS, 1))
    turned = plane.T
    plane_t_ref[...] = turned
    turned = turned[: 2 * HEADS]
    g2_ref[...] = jnp.zeros_like(g2_ref)
    s2_ref[...] = jnp.zeros_like(s2_ref)
    for p in range(HEADS // 2):
        moved = pltpu.roll(turned, LANES - p // 2 * 32, 1) if p >= 2 else turned
        g2_ref[p, 0:2] = moved[2 * p : 2 * p + 2]
        g2_ref[p, 2:4] = moved[HEADS + 2 * p : HEADS + 2 * p + 2]
    for r in range(HEADS):
        row = slide_row(r)
        moved = pltpu.roll(turned, LANES - row, 1) if row else turned
        s2_ref[r // 8, r % 8, 0:1] = moved[r : r + 1]
        s2_ref[r // 8, r % 8, 1:2] = moved[HEADS + r : HEADS + r + 1]


def near_bwd_kernel(len_ref, xp_ref, plane_t_ref, grads_ref):
    bias = key_bias(len_ref, 0)
    tiles = HEADS * HEAD // LANES
    totals = [[None] * tiles for _ in range(3)]
    for h in range(HEADS):
        start, width, shift = window(HEAD * h, HEAD)
        mask = lane_mask(width, shift, shift + HEAD)
        qm, km, vm, cm = [xp_ref[a, :, start : start + width] * mask for a in range(4)]
        s = mm_t(km, qm) * SCALE + bias
        weights = jnp.exp(s - plane_t_ref[h : h + 1, :])
        dp = mm_t(vm, cm)
        ds = (weights * (dp - plane_t_ref[HEADS + h : HEADS + h + 1, :])).astype(BF)
        results = (t_mm(ds, km), mm(ds, qm), mm(weights.astype(BF), cm))
        for index, value in enumerate(results):
            for part in range(width // LANES):
                t = start // LANES + part
                piece = value[:, part * LANES : (part + 1) * LANES]
                old = totals[index][t]
                totals[index][t] = piece if old is None else old + piece
    for index in range(3):
        for t in range(tiles):
            value = totals[index][t]
            grads_ref[index, :, t * LANES : (t + 1) * LANES] = value * SCALE if index < 2 else value


def join_rows(ref, span):
    ref = [ref[i] for i in range(ref.shape[0])] if len(ref.shape) == 3 else [
        ref[i, j] for i in range(ref.shape[0]) for j in range(ref.shape[1])
    ]
    sources, per = len(ref), LANES // span
    lane = iota2((8, LANES), 1)
    rows = []
    for first in range(0, sources, per):
        row = ref[first]
        for index in range(1, per):
            moved = pltpu.roll(ref[first + index], index * span, 1)
            row = jnp.where(lane >= index * span, moved, row)
        rows.append(row)
    return jnp.concatenate(rows, axis=1)


def score_grads(q, k, v, c, lse, delta):
    weights = jnp.exp(mm_t(k, q) * SCALE - lse)
    return weights.astype(BF), (weights * (mm_t(v, c) - delta)).astype(BF)


def group_bwd(gr_ref, gc_ref, gp_ref, go_ref):
    groups = gr_ref.shape[0]
    q, k, v = [gr_ref[:, a].reshape(groups * 32, LANES) for a in range(3)]
    c = gc_ref[...].reshape(groups * 32, LANES)
    plane = join_rows(gp_ref, 32)
    sums = [None] * 3
    for e in range(2):
        mask = lane_mask(LANES, HEAD * e, HEAD * (e + 1))
        q_flag = q * lane_mask(LANES, HEAD * e, HEAD * (e + 1), PAIR)
        cm = c * mask
        weights, ds = score_grads(q_flag, k, v, cm, plane[e : e + 1], plane[2 + e : 3 + e])
        parts = (t_mm(ds, k * mask), mm(ds, q * mask), mm(weights, cm))
        sums = [part if old is None else old + part for old, part in zip(sums, parts)]
    for a, grad in enumerate((sums[0] * SCALE, sums[1] * SCALE, sums[2])):
        go_ref[:, a] = grad.reshape(groups, 32, LANES).astype(BF)


def slide_bwd(sr_ref, sp_ref, so_ref):
    sources = sr_ref.shape[0] * sr_ref.shape[1]
    qc, kv = slide_members(sr_ref)
    plane = join_rows(sp_ref, 8)
    low = lane_mask(LANES, 0, HEAD)
    cm = qc * lane_mask(LANES, UPPER, UPPER + HEAD)
    weights, ds = score_grads(
        qc * lane_mask(LANES, 0, HEAD + 1), kv, kv, cm, plane[0:1], plane[1:2]
    )
    query = t_mm(ds, kv * low) * SCALE
    key_value = mm(ds, qc * low) * SCALE + mm(weights, cm)
    stacked = [grad.reshape(sources, 8, LANES) for grad in (query, key_value)]
    so_ref[...] = jnp.concatenate(stacked, axis=1).reshape(so_ref.shape).astype(BF)


def final_kernel(near_ref, go_ref, so_ref, dq_ref, dk_ref, dv_ref, acc_ref):
    acc_ref[...] = near_ref[...]
    for p in range(HEADS // 2):
        row = p // 2 * 32
        start, width, shift = window(PAIR * p, PAIR)
        moved = mm(go_ref[p].reshape(96, LANES), shift_out(width, shift, PAIR))
        for a in range(3):
            acc_ref[a, row : row + 32, start : start + width] += moved[32 * a : 32 * a + 32]
    for r in range(HEADS):
        row = slide_row(r)
        start, width, shift = window(HEAD * r, HEAD)
        moved = mm(so_ref[r // 8, r % 8], shift_out(width, shift, HEAD))
        upper = mm(so_ref[r // 8, r % 8], shift_out(width, shift, HEAD, UPPER))
        for a, piece in enumerate((moved[0:8], moved[8:16], upper[8:16])):
            acc_ref[a, row : row + 8, start : start + width] += piece
    back = permute_matrix(True)
    for a, ref in enumerate((dq_ref, dk_ref, dv_ref)):
        ref[...] = mm(back, acc_ref[a].astype(BF)).astype(BF)


MESH = pl.DeviceIdType.MESH


def remote(src, dst, send_sem, recv_sem, outer, inner):
    return pltpu.make_async_remote_copy(
        src_ref=src,
        dst_ref=dst,
        send_sem=send_sem,
        recv_sem=recv_sem,
        device_id=(outer, inner),
        device_id_type=MESH,
    )


class Group:
    def __init__(self, inner, src, dst, send_sem, recv_sem, second=False):
        self.second = second
        self.inner, self.src, self.dst = inner, src, dst
        self.send_sem, self.recv_sem = send_sem, recv_sem

    def copy(self, step):
        me = lax.axis_index("inner")
        peer = wrapped(me + step, self.inner)
        return remote(
            self.src.at[:, peer] if self.second else self.src.at[peer],
            self.dst.at[:, me] if self.second else self.dst.at[me],
            self.send_sem.at[step],
            self.recv_sem.at[step],
            lax.axis_index("outer"),
            peer,
        )

    def start(self):
        @pl.loop(1, self.inner)
        def _(step):
            self.copy(step).start()

        me = lax.axis_index("inner")
        if self.second:
            for half in range(2):
                self.dst[half, me] = self.src[half, me]
        else:
            self.dst[me] = self.src[me]

    def wait_recv(self):
        @pl.loop(1, self.inner)
        def _(step):
            self.copy(step).wait_recv()

    def wait_send(self):
        @pl.loop(1, self.inner)
        def _(step):
            self.copy(step).wait_send()


def wrapped(value, count):
    return jnp.where(value >= count, value - count, value)


class ToOwner:
    def __init__(self, count, src, dst, send_sem, recv_sem):
        self.count, self.src, self.dst = count, src, dst
        self.send_sem, self.recv_sem = send_sem, recv_sem
        self.mine, self.place = lax.axis_index("outer"), lax.axis_index("inner")

    def copy(self, half):
        return remote(
            self.src.at[half],
            self.dst.at[self.mine],
            self.send_sem.at[half],
            self.recv_sem.at[self.mine],
            2 * half,
            self.place,
        )

    def start(self):
        for half in range(2):

            @pl.when(self.mine != 2 * half)
            def _():
                self.copy(half).start()

            @pl.when(self.mine == 2 * half)
            def _():
                self.dst[self.mine] = self.src[half]

    def wait_recv(self):
        for source in range(self.count):

            @pl.when(self.mine != source)
            def _():
                remote(
                    self.src.at[0],
                    self.dst.at[source],
                    self.send_sem.at[0],
                    self.recv_sem.at[source],
                    source,
                    self.place,
                ).wait_recv()

    def wait_send(self):
        for half in range(2):

            @pl.when(self.mine != 2 * half)
            def _():
                self.copy(half).wait_send()


class FromOwner:
    def __init__(self, count, src, dst, send_sem, recv_sem):
        self.count, self.src, self.dst = count, src, dst
        self.send_sem, self.recv_sem = send_sem, recv_sem
        self.mine, self.place = lax.axis_index("outer"), lax.axis_index("inner")

    def copy(self, target):
        half = self.mine // 2
        return remote(
            self.src.at[target],
            self.dst.at[half],
            self.send_sem.at[target],
            self.recv_sem.at[half],
            target,
            self.place,
        )

    def each(self, act):
        for target in range(self.count):

            @pl.when(self.mine != target)
            def _():
                act(self.copy(target))

    def start(self):
        self.each(lambda copy: copy.start())
        self.dst[self.mine // 2] = self.src[self.mine]

    def wait_recv(self):
        for half in range(2):

            @pl.when(self.mine != 2 * half)
            def _():
                remote(
                    self.src.at[0],
                    self.dst.at[half],
                    self.send_sem.at[0],
                    self.recv_sem.at[half],
                    2 * half,
                    self.place,
                ).wait_recv()

    def wait_send(self):
        self.each(lambda copy: copy.wait_send())


def neighbours(inner, count, act):
    mine, me = lax.axis_index("outer"), lax.axis_index("inner")
    for step in range(1, count):
        act(wrapped(mine + step, count), me)
    for step in range(1, inner):
        act(mine, wrapped(me + step, inner))


def whole_kernel(inner, devices, len_ref, q_ref, k_ref, v_ref, c_ref, att_ref, dq_ref, dk_ref, dv_ref, *scratch):
    (xp, near_out, near_lse, plane_t, near_grads, acc) = scratch[:6]
    staged, gcs, gcr, load_sem, m1, m2, m3, m4 = scratch[26:]
    count = devices // inner
    (g1s, g1r, s1s, s1r, g2s, g2r, s2s, s2r, g3s, g3r, s3s, s3r, g4s, g4r, s4s, s4r) = scratch[6:22]
    group_send, group_recv, slide_send, slide_recv = scratch[22:26]
    outer, place = lax.axis_index("outer"), lax.axis_index("inner")
    is_owner = lax.rem(outer, 2) == 0

    def group_exchange(phase, src, dst):
        return Group(inner, src, dst, group_send.at[phase], group_recv.at[phase])

    def slide_inner(phase, src, dst):
        return Group(inner, src, dst, group_send.at[phase], group_recv.at[phase], True)

    def slide_exchange(kind, phase, src, dst):
        return kind(count, src, dst, slide_send.at[phase], slide_recv.at[phase])

    group1, near1, slide1 = group_exchange(0, g1s, g1r), slide_inner(5, s1s, m1), slide_exchange(ToOwner, 0, m1, s1r)
    group2, near2, slide2 = group_exchange(1, g2s, g2r), slide_inner(6, m2, s2r), slide_exchange(FromOwner, 1, s2s, m2)
    group3, near3, slide3 = group_exchange(2, g3s, g3r), slide_inner(7, s3s, m3), slide_exchange(ToOwner, 2, m3, s3r)
    group4, near4, slide4 = group_exchange(3, g4s, g4r), slide_inner(8, m4, s4r), slide_exchange(FromOwner, 3, s4s, m4)
    group_c = group_exchange(4, gcs, gcr)
    barrier = pltpu.get_barrier_semaphore()

    def greet(*other):
        pl.semaphore_signal(barrier, inc=1, device_id=other, device_id_type=MESH)

    loads = [
        pltpu.make_async_copy(ref, staged.at[a], load_sem.at[a])
        for a, ref in enumerate((q_ref, k_ref, v_ref, c_ref))
    ]
    for load in loads:
        load.start()
    neighbours(inner, count, greet)
    for load in loads:
        load.wait()
    prep_kernel(len_ref, *[staged.at[a] for a in range(4)], xp, g1s, gcs, s1s)
    pl.semaphore_wait(barrier, inner + count - 2)
    near1.start()
    group1.start()
    near1.wait_recv()
    slide1.start()
    group_c.start()
    near_fwd_kernel(len_ref, xp, near_out, near_lse)

    @pl.when(is_owner)
    def _():
        slide1.wait_recv()
        slide_fwd(s1r, s2s)
        slide2.start()

    group1.wait_recv()
    group_fwd(g1r, g2s)
    group2.start()
    slide2.wait_recv()
    near2.start()
    group2.wait_recv()
    near2.wait_recv()
    combine_kernel(xp, near_out, near_lse, g2r, s2r, att_ref, plane_t, g3s, s3s, acc)
    near3.start()
    group3.start()
    near3.wait_recv()
    slide3.start()
    near_bwd_kernel(len_ref, xp, plane_t, near_grads)

    @pl.when(is_owner)
    def _():
        slide3.wait_recv()
        slide_bwd(s1r, s3r, s4s)
        slide4.start()

    group_c.wait_recv()
    group3.wait_recv()
    group_bwd(g1r, gcr, g3r, g4s)
    group4.start()
    slide4.wait_recv()
    near4.start()
    group4.wait_recv()
    near4.wait_recv()
    final_kernel(near_grads, g4r, s4r, dq_ref, dk_ref, dv_ref, acc)
    for sent in (near1, near2, near3, near4, group1, slide1, group_c, group2, group3, slide3, group4):
        sent.wait_send()

    @pl.when(is_owner)
    def _():
        slide2.wait_send()
        slide4.wait_send()


def fast_local(inner, devices, *args):
    row_lengths, tiles_in = args[4], args[:4]
    tiles, width = tiles_in[0].shape
    vmem = pl.BlockSpec(memory_space=pltpu.VMEM)

    def both(count, back, shape, dtype):
        return [pltpu.VMEM((count,) + shape, dtype), pltpu.VMEM((back,) + shape, dtype)]

    scratch = [
        pltpu.VMEM((4, tiles, width), BF),
        pltpu.VMEM((tiles, width), F32),
        pltpu.VMEM((tiles, LANES), F32),
        pltpu.VMEM((LANES, tiles), F32),
        pltpu.VMEM((3, tiles, width), F32),
        pltpu.VMEM((3, tiles, width), F32),
    ]
    scratch += both(inner, inner, (3, 32, LANES), BF) + both(2, devices // inner, (inner, 16, LANES), BF)
    scratch += both(inner, inner, (32, LANES), BF) + both(devices // inner, 2, (inner, 8, LANES), BF)
    scratch += both(inner, inner, (8, LANES), F32) + both(2, devices // inner, (inner, 8, LANES), F32)
    scratch += both(inner, inner, (3, 32, LANES), BF) + both(devices // inner, 2, (inner, 16, LANES), BF)
    scratch += [pltpu.SemaphoreType.DMA((9, inner))] * 2 + [pltpu.SemaphoreType.DMA((4, devices // inner))] * 2
    scratch += [pltpu.VMEM((4, tiles, width), BF)] + both(inner, inner, (32, LANES), BF)
    scratch += [pltpu.SemaphoreType.DMA((4,))]
    scratch += [
        pltpu.VMEM((2, inner, 16, LANES), BF),
        pltpu.VMEM((2, inner, 8, LANES), BF),
        pltpu.VMEM((2, inner, 8, LANES), F32),
        pltpu.VMEM((2, inner, 16, LANES), BF),
    ]
    return tuple(
        pl.pallas_call(
            lambda *refs: whole_kernel(inner, devices, *refs),
            out_shape=[jax.ShapeDtypeStruct((tiles, width), BF)] * 4,
            in_specs=[pl.BlockSpec(memory_space=pltpu.SMEM)] + [pl.BlockSpec(memory_space=pltpu.HBM)] * 4,
            out_specs=[vmem] * 4,
            scratch_shapes=scratch,
            compiler_params=pltpu.CompilerParams(
                collective_id=0, has_side_effects=True, vmem_limit_bytes=60 * 1024 * 1024
            ),
        )(row_lengths, *tiles_in)
    )


def solution(mesh):
    in_specs = (P(("outer", "inner"), None),) * 4 + (P(("outer", "inner")),)
    out_specs = (P(("outer", "inner"), None),) * 4
    inner = mesh.shape["inner"]
    devices = inner * mesh.shape["outer"]

    def step(*args):
        owners = 2 * inner == HEADS and devices == 2 * HEADS
        if owners and args[0].shape == (LANES, HEADS * HEAD):
            return fast_local(inner, devices, *args)
        return local(*args)

    return jax.shard_map(step, mesh=mesh, in_specs=in_specs, out_specs=out_specs, check_vma=False)
```

```python
import jax
import jax.numpy as jnp
import numpy as np
from jax import lax
from jax.experimental import pallas as pl
from jax.experimental.pallas import tpu as pltpu
from jax.sharding import PartitionSpec as P

HEADS = 16
HEAD = 48
ROW = 32
STRIDE_GROUP = 4
STRIDE_SLIDE = 16


NEGATIVE_FILL = -1e30
heads_at_once = 4


def as_sent(value):

    def short(part):
        return part.astype(jnp.bfloat16) if part.dtype == jnp.float32 else part

    return jax.tree.map(short, value)


def head_ranges(head_total):
    step_size = min(head_total, heads_at_once)
    return [(first_head, first_head + step_size) for first_head in range(0, head_total, step_size)]


def scores_of(query_block, key_block, score_scale):
    return (
        jnp.einsum("hdq,hdk->hqk", query_block, key_block, preferred_element_type=jnp.float32)
        * score_scale
    )


def branch_stats(query_heads, key_heads, value_heads, key_valid, score_scale):
    peak_list, total_list, sum_list = ([], [], [])
    for first_head, last_head in head_ranges(query_heads.shape[0]):
        raw_scores = scores_of(
            query_heads[first_head:last_head], key_heads[first_head:last_head], score_scale
        )
        key_keep = key_valid[first_head:last_head][:, None, :]
        masked = jnp.where(key_keep, raw_scores, NEGATIVE_FILL)
        row_peak = jnp.max(masked, axis=2)
        weights = jnp.where(key_keep, jnp.exp(masked - row_peak[:, :, None]), 0.0)
        peak_list.append(row_peak)
        total_list.append(jnp.sum(weights, axis=2))
        sum_list.append(
            jnp.einsum(
                "hqk,hdk->hdq",
                weights.astype(jnp.bfloat16),
                value_heads[first_head:last_head],
                preferred_element_type=jnp.float32,
            )
        )
    return (
        jnp.concatenate(peak_list, axis=0),
        jnp.concatenate(total_list, axis=0),
        jnp.concatenate(sum_list, axis=0),
    )


def branch_grads(
    query_heads,
    key_heads,
    value_heads,
    cotan_heads,
    log_norm,
    out_dot,
    key_valid,
    score_scale,
    want_query,
    want_keys,
):
    query_list, key_list, value_list = ([], [], [])
    for first_head, last_head in head_ranges(query_heads.shape[0]):
        query_block = query_heads[first_head:last_head]
        key_block = key_heads[first_head:last_head]
        cotan_block = cotan_heads[first_head:last_head]
        raw_scores = scores_of(query_block, key_block, score_scale)
        key_keep = key_valid[first_head:last_head][:, None, :]
        weights = jnp.where(
            key_keep, jnp.exp(raw_scores - log_norm[first_head:last_head][:, :, None]), 0.0
        )
        weight_grads = jnp.einsum(
            "hdq,hdk->hqk",
            cotan_block,
            value_heads[first_head:last_head],
            preferred_element_type=jnp.float32,
        )
        low_grads = (weights * (weight_grads - out_dot[first_head:last_head][:, :, None])).astype(
            jnp.bfloat16
        )
        if want_query:
            query_list.append(
                score_scale
                * jnp.einsum(
                    "hqk,hdk->hdq", low_grads, key_block, preferred_element_type=jnp.float32
                )
            )
        if want_keys:
            key_list.append(
                score_scale
                * jnp.einsum(
                    "hqk,hdq->hdk", low_grads, query_block, preferred_element_type=jnp.float32
                )
            )
            value_list.append(
                jnp.einsum(
                    "hqk,hdq->hdk",
                    weights.astype(jnp.bfloat16),
                    cotan_block,
                    preferred_element_type=jnp.float32,
                )
            )
    query_part = jnp.concatenate(query_list, axis=0) if want_query else None
    key_part = jnp.concatenate(key_list, axis=0) if want_keys else None
    value_part = jnp.concatenate(value_list, axis=0) if want_keys else None
    return (query_part, key_part, value_part)


def head_offsets(head_total, stride):
    return np.arange(head_total) * stride // head_total


def select_rows(array_in, stride):
    head_total = array_in.shape[0]
    offsets = head_offsets(head_total, stride)
    folded = array_in.reshape(array_in.shape[:-1] + (array_in.shape[-1] // stride, stride))
    return jnp.stack(
        [folded[head_index, ..., int(offsets[head_index])] for head_index in range(head_total)]
    )


def spread_rows(array_in, stride, fill_value):
    head_total = array_in.shape[0]
    chosen = np.arange(stride)[None, :] == head_offsets(head_total, stride)[:, None]
    chosen = chosen.reshape((head_total,) + (1,) * (array_in.ndim - 1) + (stride,))
    full = jnp.where(chosen, array_in[..., None], fill_value)
    return full.reshape(array_in.shape[:-1] + (array_in.shape[-1] * stride,))


def to_heads(flat_in):
    return jnp.transpose(flat_in.reshape(flat_in.shape[0], HEADS, -1), (1, 2, 0))


def to_flat(heads_in):
    return jnp.transpose(heads_in, (2, 0, 1)).reshape(heads_in.shape[2], -1)


def local(query_tiles, key_tiles, value_tiles, cotangent, row_lengths):
    tile_count = query_tiles.shape[0]
    score_scale = HEAD ** (-0.5)
    query_heads = to_heads(query_tiles)
    key_heads = to_heads(key_tiles)
    value_heads = to_heads(value_tiles)
    cotan_heads = to_heads(cotangent)
    tile_slot = jnp.arange(tile_count, dtype=jnp.int32)
    tile_valid = tile_slot % ROW < jnp.repeat(row_lengths, ROW, total_repeat_length=tile_count)
    valid_heads = jnp.broadcast_to(tile_valid[None, :], (HEADS, tile_count))
    group_query = select_rows(query_heads, STRIDE_GROUP)
    group_key = select_rows(key_heads, STRIDE_GROUP)
    group_value = select_rows(value_heads, STRIDE_GROUP)
    group_cotan = select_rows(cotan_heads, STRIDE_GROUP)
    group_valid = select_rows(valid_heads, STRIDE_GROUP)
    group_flag = group_valid.astype(jnp.bfloat16)[:, None, :]
    slide_query = select_rows(query_heads, STRIDE_SLIDE)
    slide_key = select_rows(key_heads, STRIDE_SLIDE)
    slide_value = select_rows(value_heads, STRIDE_SLIDE)
    slide_flag = select_rows(valid_heads, STRIDE_SLIDE).astype(jnp.bfloat16)[:, None, :]
    owned_query, owned_key, owned_value, owned_flag = (
        lax.all_to_all(slide_query, "outer", split_axis=0, concat_axis=2, tiled=True),
        lax.all_to_all(slide_key, "outer", split_axis=0, concat_axis=2, tiled=True),
        lax.all_to_all(slide_value, "outer", split_axis=0, concat_axis=2, tiled=True),
        lax.all_to_all(slide_flag, "outer", split_axis=0, concat_axis=2, tiled=True),
    )
    got_group = (
        lax.all_gather(group_key, "inner", axis=2, tiled=True),
        lax.all_gather(group_value, "inner", axis=2, tiled=True),
        lax.all_gather(group_flag, "inner", axis=2, tiled=True),
    )
    got_slide = (
        lax.all_gather(owned_key, "inner", axis=2, tiled=True),
        lax.all_gather(owned_value, "inner", axis=2, tiled=True),
        lax.all_gather(owned_flag, "inner", axis=2, tiled=True),
    )
    near_peak, near_total, near_sum = branch_stats(
        query_heads, key_heads, value_heads, valid_heads, score_scale
    )
    remote_group_key = got_group[0]
    remote_group_value = got_group[1]
    remote_group_valid = got_group[2][:, 0, :] > 0.5
    group_peak, group_total, group_sum = branch_stats(
        group_query, remote_group_key, remote_group_value, remote_group_valid, score_scale
    )
    slide_all_key = got_slide[0]
    slide_all_value = got_slide[1]
    slide_all_valid = got_slide[2][:, 0, :] > 0.5
    owner_peak, owner_total, owner_sum = branch_stats(
        owned_query, slide_all_key, slide_all_value, slide_all_valid, score_scale
    )
    slide_peak, slide_total, slide_sum = (
        lax.all_to_all(owner_peak[:, None, :], "outer", split_axis=2, concat_axis=0, tiled=True),
        lax.all_to_all(owner_total[:, None, :], "outer", split_axis=2, concat_axis=0, tiled=True),
        lax.all_to_all(owner_sum, "outer", split_axis=2, concat_axis=0, tiled=True),
    )
    slide_peak = slide_peak[:, 0, :]
    slide_total = slide_total[:, 0, :]
    group_peak_full = spread_rows(group_peak, STRIDE_GROUP, NEGATIVE_FILL)
    slide_peak_full = spread_rows(slide_peak, STRIDE_SLIDE, NEGATIVE_FILL)
    best_peak = jnp.maximum(jnp.maximum(near_peak, group_peak_full), slide_peak_full)
    near_weight = jnp.exp(near_peak - best_peak)
    group_weight = jnp.exp(group_peak_full - best_peak)
    slide_weight = jnp.exp(slide_peak_full - best_peak)
    denominator = (
        near_total * near_weight
        + spread_rows(group_total, STRIDE_GROUP, 0.0) * group_weight
        + spread_rows(slide_total, STRIDE_SLIDE, 0.0) * slide_weight
    )
    numerator = (
        near_sum * near_weight[:, None, :]
        + spread_rows(group_sum, STRIDE_GROUP, 0.0) * group_weight[:, None, :]
        + spread_rows(slide_sum, STRIDE_SLIDE, 0.0) * slide_weight[:, None, :]
    )
    attended = (numerator / denominator[:, None, :]).astype(jnp.bfloat16)
    log_norm = best_peak + jnp.log(denominator)
    out_dot = jnp.sum(cotan_heads.astype(jnp.float32) * attended.astype(jnp.float32), axis=1)
    near_query, near_key, near_value = branch_grads(
        query_heads,
        key_heads,
        value_heads,
        cotan_heads,
        log_norm,
        out_dot,
        valid_heads,
        score_scale,
        True,
        True,
    )
    group_lse = select_rows(log_norm, STRIDE_GROUP)
    group_dot = select_rows(out_dot, STRIDE_GROUP)
    group_query_grad = branch_grads(
        group_query,
        remote_group_key,
        remote_group_value,
        group_cotan,
        group_lse,
        group_dot,
        remote_group_valid,
        score_scale,
        True,
        False,
    )[0]
    got_group_rows = (
        lax.all_gather(group_query, "inner", axis=2, tiled=True),
        lax.all_gather(group_cotan, "inner", axis=2, tiled=True),
    )
    got_group_stats = (
        lax.all_gather(group_lse, "inner", axis=1, tiled=True),
        lax.all_gather(group_dot, "inner", axis=1, tiled=True),
    )
    unused_group, group_key_grad, group_value_grad = branch_grads(
        got_group_rows[0],
        group_key,
        group_value,
        got_group_rows[1],
        got_group_stats[0],
        got_group_stats[1],
        group_valid,
        score_scale,
        False,
        True,
    )
    slide_cotan = select_rows(cotan_heads, STRIDE_SLIDE)
    slide_lse = select_rows(log_norm, STRIDE_SLIDE)
    slide_dot = select_rows(out_dot, STRIDE_SLIDE)
    owned_cotan = lax.all_to_all(slide_cotan, "outer", split_axis=0, concat_axis=2, tiled=True)
    owned_lse, owned_dot = (
        lax.all_to_all(slide_lse, "outer", split_axis=0, concat_axis=1, tiled=True),
        lax.all_to_all(slide_dot, "outer", split_axis=0, concat_axis=1, tiled=True),
    )
    owned_query_grad, partial_key, partial_value = branch_grads(
        owned_query,
        slide_all_key,
        slide_all_value,
        owned_cotan,
        owned_lse,
        owned_dot,
        slide_all_valid,
        score_scale,
        True,
        True,
    )
    owned_key_grad, owned_value_grad = (
        lax.psum_scatter(
            partial_key.astype(jnp.bfloat16), "inner", scatter_dimension=2, tiled=True
        ).astype(jnp.float32),
        lax.psum_scatter(
            partial_value.astype(jnp.bfloat16), "inner", scatter_dimension=2, tiled=True
        ).astype(jnp.float32),
    )
    slide_query_grad, slide_key_grad, slide_value_grad = (
        lax.all_to_all(
            as_sent(owned_query_grad), "outer", split_axis=2, concat_axis=0, tiled=True
        ).astype(owned_query_grad.dtype),
        lax.all_to_all(
            owned_key_grad.astype(jnp.bfloat16), "outer", split_axis=2, concat_axis=0, tiled=True
        ).astype(owned_key_grad.dtype),
        lax.all_to_all(
            owned_value_grad.astype(jnp.bfloat16), "outer", split_axis=2, concat_axis=0, tiled=True
        ).astype(owned_value_grad.dtype),
    )
    query_grad = (
        near_query
        + spread_rows(group_query_grad, STRIDE_GROUP, 0.0)
        + spread_rows(slide_query_grad, STRIDE_SLIDE, 0.0)
    )
    key_grad = (
        near_key
        + spread_rows(group_key_grad, STRIDE_GROUP, 0.0)
        + spread_rows(slide_key_grad, STRIDE_SLIDE, 0.0)
    )
    value_grad = (
        near_value
        + spread_rows(group_value_grad, STRIDE_GROUP, 0.0)
        + spread_rows(slide_value_grad, STRIDE_SLIDE, 0.0)
    )
    return (
        to_flat(attended),
        to_flat(query_grad.astype(jnp.bfloat16)),
        to_flat(key_grad.astype(jnp.bfloat16)),
        to_flat(value_grad.astype(jnp.bfloat16)),
    )


BF = jnp.bfloat16
F32 = jnp.float32
LANES = 128
SCALE = HEAD ** (-0.5)
PAIR = 2 * HEAD
UPPER = LANES // 2


def window(first_col, width):
    start = first_col // LANES * LANES
    shift = first_col - start
    return start, (LANES if shift + width <= LANES else 2 * LANES), shift


def iota2(shape, axis):
    return lax.broadcasted_iota(jnp.int32, shape, axis)


def original_tile(j):
    return (j & 7) * 16 + ((j >> 3) & 3) * 4 + (j >> 5)


def permute_matrix(inverse):
    shape = (LANES, LANES)
    j, i = (iota2(shape, 1), iota2(shape, 0)) if inverse else (iota2(shape, 0), iota2(shape, 1))
    return (original_tile(j) == i).astype(F32).astype(BF)


def key_bias(len_ref, axis):
    tile = original_tile(iota2((LANES, LANES), axis))
    row = tile >> 5
    length = jnp.full((LANES, LANES), len_ref[0], jnp.int32)
    for index in range(1, 4):
        length = jnp.where(row == index, len_ref[index], length)
    return jnp.where((tile & 31) < length, 0.0, NEGATIVE_FILL).astype(F32)


def shift_in(width, shift, kept, base=0):
    row, col = iota2((width, LANES), 0), iota2((width, LANES), 1)
    return ((row - shift + base == col) & (col >= base) & (col < base + kept)).astype(F32).astype(BF)


def shift_out(width, shift, kept, base=0):
    row, col = iota2((LANES, width), 0), iota2((LANES, width), 1)
    return ((col - shift + base == row) & (row >= base) & (row < base + kept)).astype(F32).astype(BF)


def lane_mask(width, first, last, extra=-1):
    lane = iota2((1, width), 1)
    keep = (lane >= first) & (lane < last)
    if extra >= 0:
        keep = keep | (lane == extra)
    return keep.astype(F32).astype(BF)


def mm(a, b):
    return jnp.dot(a, b, preferred_element_type=F32)


def mm_t(a, b):
    return lax.dot_general(a, b, (((1,), (1,)), ((), ())), preferred_element_type=F32)


def t_mm(a, b):
    return lax.dot_general(a, b, (((0,), (0,)), ((), ())), preferred_element_type=F32)


def slide_row(r):
    return (r % 4) * 32 + (r // 4) * 8


def split_mm(a, onehot):
    high = a.astype(BF)
    low = (a - high.astype(F32)).astype(BF)
    return mm(high, onehot) + mm(low, onehot)


def prep_kernel(len_ref, q_ref, k_ref, v_ref, c_ref, xp_ref, gs_ref, gc_ref, ss_ref):
    perm = permute_matrix(False)
    xs = []
    for index, ref in enumerate((q_ref, k_ref, v_ref, c_ref)):
        xs.append(mm(perm, ref[...]))
        xp_ref[index] = xs[-1].astype(BF)
    bias = key_bias(len_ref, 0)
    for p in range(HEADS // 2):
        row = p // 2 * 32
        start, width, shift = window(PAIR * p, PAIR)
        stacked = jnp.concatenate(
            [x[row : row + 32, start : start + width].astype(BF) for x in xs], axis=0
        )
        moved = mm(stacked, shift_in(width, shift, PAIR))
        flag = iota2((32, LANES), 1) == PAIR
        gs_ref[p, 0] = jnp.where(flag, 1.0, moved[0:32]).astype(BF)
        gs_ref[p, 1] = jnp.where(flag, bias[row : row + 32], moved[32:64]).astype(BF)
        gs_ref[p, 2] = moved[64:96].astype(BF)
        gc_ref[p] = moved[96:128].astype(BF)
    for r in range(HEADS):
        row = slide_row(r)
        start, width, shift = window(HEAD * r, HEAD)
        low, high = [
            jnp.concatenate(
                [xs[a][row : row + 8, start : start + width] for a in pair], axis=0
            ).astype(BF)
            for pair in ((0, 1), (3, 2))
        ]
        moved = mm(low, shift_in(width, shift, HEAD)) + mm(high, shift_in(width, shift, HEAD, UPPER))
        flags = jnp.concatenate([jnp.ones((8, LANES), F32), bias[row : row + 8]], axis=0)
        ss_ref[r // 8, r % 8] = jnp.where(iota2((16, LANES), 1) == HEAD, flags, moved).astype(BF)


def near_fwd_kernel(len_ref, xp_ref, o_ref, lse_ref):
    bias = key_bias(len_ref, 1)
    lane = iota2((LANES, LANES), 1)
    lse = jnp.full((LANES, LANES), NEGATIVE_FILL, F32)
    total = [None] * (HEADS * HEAD // LANES)
    for h in range(HEADS):
        start, width, shift = window(HEAD * h, HEAD)
        mask = lane_mask(width, shift, shift + HEAD)
        s = mm_t(xp_ref[0, :, start : start + width] * mask, xp_ref[1, :, start : start + width])
        s = s * SCALE + bias
        peak = jnp.max(s, axis=1, keepdims=True)
        e = jnp.exp(s - peak)
        norm = jnp.sum(e, axis=1, keepdims=True)
        o = mm(e.astype(BF), xp_ref[2, :, start : start + width] * mask) / norm
        lse = jnp.where(lane == h, peak + jnp.log(norm), lse)
        for part in range(width // LANES):
            t = start // LANES + part
            piece = o[:, part * LANES : (part + 1) * LANES]
            total[t] = piece if total[t] is None else total[t] + piece
    for t, value in enumerate(total):
        o_ref[:, t * LANES : (t + 1) * LANES] = value
    lse_ref[...] = lse


def three_parts(value):
    high = value.astype(BF).astype(F32)
    rest = value - high
    middle = rest.astype(BF).astype(F32)
    return high, middle, rest - middle


def attend(q, k, v):
    s = mm_t(q, k) * SCALE
    peak = jnp.max(s, axis=1, keepdims=True)
    weights = jnp.exp(s - peak)
    norm = jnp.sum(weights, axis=1, keepdims=True)
    return mm(weights.astype(BF), v) / norm, three_parts(peak + jnp.log(norm))


def group_fwd(gr_ref, go_ref):
    groups = gr_ref.shape[0]
    q, k, v = [gr_ref[:, a].reshape(groups * 32, LANES) for a in range(3)]
    lane = iota2((groups * 32, LANES), 1)
    total = None
    for e in range(2):
        mask = lane_mask(LANES, HEAD * e, HEAD * (e + 1))
        out, parts = attend(q * lane_mask(LANES, HEAD * e, HEAD * (e + 1), PAIR), k, v * mask)
        for index, part in enumerate(parts):
            out = jnp.where(lane == PAIR + 2 * index + e, part, out)
        total = out if total is None else total + out
    go_ref[...] = total.astype(BF).reshape(groups, 32, LANES)


def slide_members(sr_ref):
    sources = sr_ref.shape[0] * sr_ref.shape[1]
    wide = sr_ref[...].astype(F32).reshape(sources, 16, LANES)
    return [wide[:, a : a + 8].reshape(sources * 8, LANES).astype(BF) for a in (0, 8)]


def slide_fwd(sr_ref, so_ref):
    sources = sr_ref.shape[0] * sr_ref.shape[1]
    qc, kv = slide_members(sr_ref)
    out, parts = attend(
        qc * lane_mask(LANES, 0, HEAD + 1), kv, kv * lane_mask(LANES, UPPER, UPPER + HEAD)
    )
    lane = iota2((sources * 8, LANES), 1)
    for index, part in enumerate(parts):
        out = jnp.where(lane == index, part, out)
    so_ref[...] = out.reshape(so_ref.shape).astype(BF)


def head_spread(transposed):
    shape = (HEADS * HEAD, LANES) if transposed else (LANES, HEADS * HEAD)
    head, col = (iota2(shape, 1), iota2(shape, 0)) if transposed else (iota2(shape, 0), iota2(shape, 1))
    return ((col >= head * HEAD) & (col < head * HEAD + HEAD)).astype(F32).astype(BF)


def combine_kernel(
    xp_ref, on_ref, ln_ref, go_ref, so_ref, att_ref, plane_t_ref, g2_ref, s2_ref, acc_ref
):
    lane32 = iota2((32, LANES), 1)
    lane8 = iota2((8, LANES), 1)
    near = ln_ref[...]
    group_rows, slide_rows = [], [None] * HEADS
    for o in range(4):
        pieces = []
        for p in (2 * o, 2 * o + 1):
            block = go_ref[p].astype(F32)
            block = block + pltpu.roll(block, LANES - 2, 1) + pltpu.roll(block, LANES - 4, 1)
            moved = pltpu.roll(block, LANES - PAIR + 2 * p, 1)
            keep = (lane32 >= 2 * p) & (lane32 < 2 * p + 2)
            pieces.append(jnp.where(keep, moved, NEGATIVE_FILL))
        group_rows.append(jnp.maximum(pieces[0], pieces[1]))
    for r in range(HEADS):
        block = so_ref[r // 8, r % 8].astype(F32)
        block = block + pltpu.roll(block, LANES - 1, 1) + pltpu.roll(block, LANES - 2, 1)
        moved = pltpu.roll(block, r, 1) if r else block
        slide_rows[slide_row(r) // 8] = jnp.where(lane8 == r, moved, NEGATIVE_FILL)
    group = jnp.concatenate(group_rows, axis=0)
    slide = jnp.concatenate(slide_rows, axis=0)
    best = jnp.maximum(jnp.maximum(near, group), slide)
    near_w, group_w, slide_w = jnp.exp(near - best), jnp.exp(group - best), jnp.exp(slide - best)
    den = near_w + group_w + slide_w
    lse = best + jnp.log(den)
    spread = head_spread(False)
    acc_ref[0:2] = jnp.zeros((2,) + acc_ref.shape[1:], F32)
    for p in range(HEADS // 2):
        row = p // 2 * 32
        start, width, shift = window(PAIR * p, PAIR)
        acc_ref[0, row : row + 32, start : start + width] += mm(
            go_ref[p], shift_out(width, shift, PAIR)
        )
    for r in range(HEADS):
        row = slide_row(r)
        start, width, shift = window(HEAD * r, HEAD)
        acc_ref[1, row : row + 8, start : start + width] += mm(
            so_ref[r // 8, r % 8], shift_out(width, shift, HEAD, UPPER)
        )
    attended = (
        on_ref[...] * split_mm(near_w / den, spread)
        + acc_ref[0] * split_mm(group_w / den, spread)
        + acc_ref[1] * split_mm(slide_w / den, spread)
    ).astype(BF)
    att_ref[...] = mm(permute_matrix(True), attended).astype(BF)
    product = xp_ref[3].astype(F32) * attended.astype(F32)
    delta = split_mm(product, head_spread(True))
    lane = iota2((LANES, LANES), 1)
    plane = jnp.where(lane < HEADS, lse, pltpu.roll(delta, HEADS, 1))
    turned = plane.T
    plane_t_ref[...] = turned
    turned = turned[: 2 * HEADS]
    g2_ref[...] = jnp.zeros_like(g2_ref)
    s2_ref[...] = jnp.zeros_like(s2_ref)
    for p in range(HEADS // 2):
        moved = pltpu.roll(turned, LANES - p // 2 * 32, 1) if p >= 2 else turned
        g2_ref[p, 0:2] = moved[2 * p : 2 * p + 2]
        g2_ref[p, 2:4] = moved[HEADS + 2 * p : HEADS + 2 * p + 2]
    for r in range(HEADS):
        row = slide_row(r)
        moved = pltpu.roll(turned, LANES - row, 1) if row else turned
        s2_ref[r // 8, r % 8, 0:1] = moved[r : r + 1]
        s2_ref[r // 8, r % 8, 1:2] = moved[HEADS + r : HEADS + r + 1]


def near_bwd_kernel(len_ref, xp_ref, plane_t_ref, grads_ref):
    bias = key_bias(len_ref, 0)
    tiles = HEADS * HEAD // LANES
    totals = [[None] * tiles for _ in range(3)]
    for h in range(HEADS):
        start, width, shift = window(HEAD * h, HEAD)
        mask = lane_mask(width, shift, shift + HEAD)
        qm, km, vm, cm = [xp_ref[a, :, start : start + width] * mask for a in range(4)]
        s = mm_t(km, qm) * SCALE + bias
        weights = jnp.exp(s - plane_t_ref[h : h + 1, :])
        dp = mm_t(vm, cm)
        ds = (weights * (dp - plane_t_ref[HEADS + h : HEADS + h + 1, :])).astype(BF)
        results = (t_mm(ds, km), mm(ds, qm), mm(weights.astype(BF), cm))
        for index, value in enumerate(results):
            for part in range(width // LANES):
                t = start // LANES + part
                piece = value[:, part * LANES : (part + 1) * LANES]
                old = totals[index][t]
                totals[index][t] = piece if old is None else old + piece
    for index in range(3):
        for t in range(tiles):
            value = totals[index][t]
            grads_ref[index, :, t * LANES : (t + 1) * LANES] = value * SCALE if index < 2 else value


def join_rows(ref, span):
    ref = [ref[i] for i in range(ref.shape[0])] if len(ref.shape) == 3 else [
        ref[i, j] for i in range(ref.shape[0]) for j in range(ref.shape[1])
    ]
    sources, per = len(ref), LANES // span
    lane = iota2((8, LANES), 1)
    rows = []
    for first in range(0, sources, per):
        row = ref[first]
        for index in range(1, per):
            moved = pltpu.roll(ref[first + index], index * span, 1)
            row = jnp.where(lane >= index * span, moved, row)
        rows.append(row)
    return jnp.concatenate(rows, axis=1)


def score_grads(q, k, v, c, lse, delta):
    weights = jnp.exp(mm_t(k, q) * SCALE - lse)
    return weights.astype(BF), (weights * (mm_t(v, c) - delta)).astype(BF)


def group_bwd(gr_ref, gc_ref, gp_ref, go_ref):
    groups = gr_ref.shape[0]
    q, k, v = [gr_ref[:, a].reshape(groups * 32, LANES) for a in range(3)]
    c = gc_ref[...].reshape(groups * 32, LANES)
    plane = join_rows(gp_ref, 32)
    sums = [None] * 3
    for e in range(2):
        mask = lane_mask(LANES, HEAD * e, HEAD * (e + 1))
        q_flag = q * lane_mask(LANES, HEAD * e, HEAD * (e + 1), PAIR)
        cm = c * mask
        weights, ds = score_grads(q_flag, k, v, cm, plane[e : e + 1], plane[2 + e : 3 + e])
        parts = (t_mm(ds, k * mask), mm(ds, q * mask), mm(weights, cm))
        sums = [part if old is None else old + part for old, part in zip(sums, parts)]
    for a, grad in enumerate((sums[0] * SCALE, sums[1] * SCALE, sums[2])):
        go_ref[:, a] = grad.reshape(groups, 32, LANES).astype(BF)


def slide_bwd(sr_ref, sp_ref, so_ref):
    sources = sr_ref.shape[0] * sr_ref.shape[1]
    qc, kv = slide_members(sr_ref)
    plane = join_rows(sp_ref, 8)
    low = lane_mask(LANES, 0, HEAD)
    cm = qc * lane_mask(LANES, UPPER, UPPER + HEAD)
    weights, ds = score_grads(
        qc * lane_mask(LANES, 0, HEAD + 1), kv, kv, cm, plane[0:1], plane[1:2]
    )
    query = t_mm(ds, kv * low) * SCALE
    key_value = mm(ds, qc * low) * SCALE + mm(weights, cm)
    stacked = [grad.reshape(sources, 8, LANES) for grad in (query, key_value)]
    so_ref[...] = jnp.concatenate(stacked, axis=1).reshape(so_ref.shape).astype(BF)


def final_kernel(near_ref, go_ref, so_ref, dq_ref, dk_ref, dv_ref, acc_ref):
    acc_ref[...] = near_ref[...]
    for p in range(HEADS // 2):
        row = p // 2 * 32
        start, width, shift = window(PAIR * p, PAIR)
        moved = mm(go_ref[p].reshape(96, LANES), shift_out(width, shift, PAIR))
        for a in range(3):
            acc_ref[a, row : row + 32, start : start + width] += moved[32 * a : 32 * a + 32]
    for r in range(HEADS):
        row = slide_row(r)
        start, width, shift = window(HEAD * r, HEAD)
        moved = mm(so_ref[r // 8, r % 8], shift_out(width, shift, HEAD))
        upper = mm(so_ref[r // 8, r % 8], shift_out(width, shift, HEAD, UPPER))
        for a, piece in enumerate((moved[0:8], moved[8:16], upper[8:16])):
            acc_ref[a, row : row + 8, start : start + width] += piece
    back = permute_matrix(True)
    for a, ref in enumerate((dq_ref, dk_ref, dv_ref)):
        ref[...] = mm(back, acc_ref[a].astype(BF)).astype(BF)


MESH = pl.DeviceIdType.MESH


def remote(src, dst, send_sem, recv_sem, outer, inner):
    return pltpu.make_async_remote_copy(
        src_ref=src,
        dst_ref=dst,
        send_sem=send_sem,
        recv_sem=recv_sem,
        device_id=(outer, inner),
        device_id_type=MESH,
    )


class Group:
    def __init__(self, inner, src, dst, send_sem, recv_sem, second=False):
        self.second = second
        self.inner, self.src, self.dst = inner, src, dst
        self.send_sem, self.recv_sem = send_sem, recv_sem

    def copy(self, step):
        me = lax.axis_index("inner")
        peer = wrapped(me + step, self.inner)
        return remote(
            self.src.at[:, peer] if self.second else self.src.at[peer],
            self.dst.at[:, me] if self.second else self.dst.at[me],
            self.send_sem.at[step],
            self.recv_sem.at[step],
            lax.axis_index("outer"),
            peer,
        )

    def start(self):
        @pl.loop(1, self.inner)
        def _(step):
            self.copy(step).start()

        me = lax.axis_index("inner")
        if self.second:
            for half in range(2):
                self.dst[half, me] = self.src[half, me]
        else:
            self.dst[me] = self.src[me]

    def wait_recv(self):
        @pl.loop(1, self.inner)
        def _(step):
            self.copy(step).wait_recv()

    def wait_send(self):
        @pl.loop(1, self.inner)
        def _(step):
            self.copy(step).wait_send()


def wrapped(value, count):
    return jnp.where(value >= count, value - count, value)


class ToOwner:
    def __init__(self, count, src, dst, send_sem, recv_sem):
        self.count, self.src, self.dst = count, src, dst
        self.send_sem, self.recv_sem = send_sem, recv_sem
        self.mine, self.place = lax.axis_index("outer"), lax.axis_index("inner")

    def copy(self, half):
        return remote(
            self.src.at[half],
            self.dst.at[self.mine],
            self.send_sem.at[half],
            self.recv_sem.at[self.mine],
            2 * half,
            self.place,
        )

    def start(self):
        for half in range(2):

            @pl.when(self.mine != 2 * half)
            def _():
                self.copy(half).start()

            @pl.when(self.mine == 2 * half)
            def _():
                self.dst[self.mine] = self.src[half]

    def wait_recv(self):
        for source in range(self.count):

            @pl.when(self.mine != source)
            def _():
                remote(
                    self.src.at[0],
                    self.dst.at[source],
                    self.send_sem.at[0],
                    self.recv_sem.at[source],
                    source,
                    self.place,
                ).wait_recv()

    def wait_send(self):
        for half in range(2):

            @pl.when(self.mine != 2 * half)
            def _():
                self.copy(half).wait_send()


class FromOwner:
    def __init__(self, count, src, dst, send_sem, recv_sem):
        self.count, self.src, self.dst = count, src, dst
        self.send_sem, self.recv_sem = send_sem, recv_sem
        self.mine, self.place = lax.axis_index("outer"), lax.axis_index("inner")

    def copy(self, target):
        half = self.mine // 2
        return remote(
            self.src.at[target],
            self.dst.at[half],
            self.send_sem.at[target],
            self.recv_sem.at[half],
            target,
            self.place,
        )

    def each(self, act):
        for target in range(self.count):

            @pl.when(self.mine != target)
            def _():
                act(self.copy(target))

    def start(self):
        self.each(lambda copy: copy.start())
        self.dst[self.mine // 2] = self.src[self.mine]

    def wait_recv(self):
        for half in range(2):

            @pl.when(self.mine != 2 * half)
            def _():
                remote(
                    self.src.at[0],
                    self.dst.at[half],
                    self.send_sem.at[0],
                    self.recv_sem.at[half],
                    2 * half,
                    self.place,
                ).wait_recv()

    def wait_send(self):
        self.each(lambda copy: copy.wait_send())


def neighbours(inner, count, act):
    mine, me = lax.axis_index("outer"), lax.axis_index("inner")
    for step in range(1, count):
        act(wrapped(mine + step, count), me)
    for step in range(1, inner):
        act(mine, wrapped(me + step, inner))


def whole_kernel(inner, devices, len_ref, q_ref, k_ref, v_ref, c_ref, att_ref, dq_ref, dk_ref, dv_ref, *scratch):
    (xp, near_out, near_lse, plane_t, near_grads, acc) = scratch[:6]
    staged, gcs, gcr, load_sem, m1, m2, m3, m4 = scratch[26:]
    count = devices // inner
    (g1s, g1r, s1s, s1r, g2s, g2r, s2s, s2r, g3s, g3r, s3s, s3r, g4s, g4r, s4s, s4r) = scratch[6:22]
    group_send, group_recv, slide_send, slide_recv = scratch[22:26]
    outer, place = lax.axis_index("outer"), lax.axis_index("inner")
    is_owner = lax.rem(outer, 2) == 0

    def group_exchange(phase, src, dst):
        return Group(inner, src, dst, group_send.at[phase], group_recv.at[phase])

    def slide_inner(phase, src, dst):
        return Group(inner, src, dst, group_send.at[phase], group_recv.at[phase], True)

    def slide_exchange(kind, phase, src, dst):
        return kind(count, src, dst, slide_send.at[phase], slide_recv.at[phase])

    group1, near1, slide1 = group_exchange(0, g1s, g1r), slide_inner(5, s1s, m1), slide_exchange(ToOwner, 0, m1, s1r)
    group2, near2, slide2 = group_exchange(1, g2s, g2r), slide_inner(6, m2, s2r), slide_exchange(FromOwner, 1, s2s, m2)
    group3, near3, slide3 = group_exchange(2, g3s, g3r), slide_inner(7, s3s, m3), slide_exchange(ToOwner, 2, m3, s3r)
    group4, near4, slide4 = group_exchange(3, g4s, g4r), slide_inner(8, m4, s4r), slide_exchange(FromOwner, 3, s4s, m4)
    group_c = group_exchange(4, gcs, gcr)
    barrier = pltpu.get_barrier_semaphore()

    def greet(*other):
        pl.semaphore_signal(barrier, inc=1, device_id=other, device_id_type=MESH)

    loads = [
        pltpu.make_async_copy(ref, staged.at[a], load_sem.at[a])
        for a, ref in enumerate((q_ref, k_ref, v_ref, c_ref))
    ]
    for load in loads:
        load.start()
    neighbours(inner, count, greet)
    for load in loads:
        load.wait()
    prep_kernel(len_ref, *[staged.at[a] for a in range(4)], xp, g1s, gcs, s1s)
    pl.semaphore_wait(barrier, inner + count - 2)
    near1.start()
    group1.start()
    near1.wait_recv()
    slide1.start()
    group_c.start()
    near_fwd_kernel(len_ref, xp, near_out, near_lse)

    @pl.when(is_owner)
    def _():
        slide1.wait_recv()
        slide_fwd(s1r, s2s)
        slide2.start()

    group1.wait_recv()
    group_fwd(g1r, g2s)
    group2.start()
    slide2.wait_recv()
    near2.start()
    group2.wait_recv()
    near2.wait_recv()
    combine_kernel(xp, near_out, near_lse, g2r, s2r, att_ref, plane_t, g3s, s3s, acc)
    near3.start()
    group3.start()
    near3.wait_recv()
    slide3.start()
    near_bwd_kernel(len_ref, xp, plane_t, near_grads)

    @pl.when(is_owner)
    def _():
        slide3.wait_recv()
        slide_bwd(s1r, s3r, s4s)
        slide4.start()

    group_c.wait_recv()
    group3.wait_recv()
    group_bwd(g1r, gcr, g3r, g4s)
    group4.start()
    slide4.wait_recv()
    near4.start()
    group4.wait_recv()
    near4.wait_recv()
    final_kernel(near_grads, g4r, s4r, dq_ref, dk_ref, dv_ref, acc)
    for sent in (near1, near2, near3, near4, group1, slide1, group_c, group2, group3, slide3, group4):
        sent.wait_send()

    @pl.when(is_owner)
    def _():
        slide2.wait_send()
        slide4.wait_send()


def fast_local(inner, devices, *args):
    row_lengths, tiles_in = args[4], args[:4]
    tiles, width = tiles_in[0].shape
    vmem = pl.BlockSpec(memory_space=pltpu.VMEM)

    def both(count, back, shape, dtype):
        return [pltpu.VMEM((count,) + shape, dtype), pltpu.VMEM((back,) + shape, dtype)]

    scratch = [
        pltpu.VMEM((4, tiles, width), BF),
        pltpu.VMEM((tiles, width), F32),
        pltpu.VMEM((tiles, LANES), F32),
        pltpu.VMEM((LANES, tiles), F32),
        pltpu.VMEM((3, tiles, width), F32),
        pltpu.VMEM((3, tiles, width), F32),
    ]
    scratch += both(inner, inner, (3, 32, LANES), BF) + both(2, devices // inner, (inner, 16, LANES), BF)
    scratch += both(inner, inner, (32, LANES), BF) + both(devices // inner, 2, (inner, 8, LANES), BF)
    scratch += both(inner, inner, (8, LANES), F32) + both(2, devices // inner, (inner, 8, LANES), F32)
    scratch += both(inner, inner, (3, 32, LANES), BF) + both(devices // inner, 2, (inner, 16, LANES), BF)
    scratch += [pltpu.SemaphoreType.DMA((9, inner))] * 2 + [pltpu.SemaphoreType.DMA((4, devices // inner))] * 2
    scratch += [pltpu.VMEM((4, tiles, width), BF)] + both(inner, inner, (32, LANES), BF)
    scratch += [pltpu.SemaphoreType.DMA((4,))]
    scratch += [
        pltpu.VMEM((2, inner, 16, LANES), BF),
        pltpu.VMEM((2, inner, 8, LANES), BF),
        pltpu.VMEM((2, inner, 8, LANES), F32),
        pltpu.VMEM((2, inner, 16, LANES), BF),
    ]
    return tuple(
        pl.pallas_call(
            lambda *refs: whole_kernel(inner, devices, *refs),
            out_shape=[jax.ShapeDtypeStruct((tiles, width), BF)] * 4,
            in_specs=[pl.BlockSpec(memory_space=pltpu.SMEM)] + [pl.BlockSpec(memory_space=pltpu.HBM)] * 4,
            out_specs=[vmem] * 4,
            scratch_shapes=scratch,
            compiler_params=pltpu.CompilerParams(
                collective_id=0, has_side_effects=True, vmem_limit_bytes=64 * 1024 * 1024
            ),
        )(row_lengths, *tiles_in)
    )


def solution(mesh):
    in_specs = (P(("outer", "inner"), None),) * 4 + (P(("outer", "inner")),)
    out_specs = (P(("outer", "inner"), None),) * 4
    inner = mesh.shape["inner"]
    devices = inner * mesh.shape["outer"]

    def step(*args):
        owners = 2 * inner == HEADS and devices == 2 * HEADS
        if owners and args[0].shape == (LANES, HEADS * HEAD):
            return fast_local(inner, devices, *args)
        return local(*args)

    return jax.shard_map(step, mesh=mesh, in_specs=in_specs, out_specs=out_specs, check_vma=False)
```
